32 devices in a mesh: ctx: 16 (over z, y, core), fsdp: 2 (over x).
Axes of the slice: x: 2, y: 2, z: 4, core: 2. Of those that a mesh axis runs over, the one named last changes fastest.
Arguments:
- tokens: bfloat16 [2, 4096, 1024], P('fsdp', 'ctx'), may hold values from -6 to 6
- segments: int32 [2, 4096], P('fsdp'), may hold values from 0 to 7, never falling along the last dimension, each value on 1 to 3072 neighbouring positions
- w_query: bfloat16 [1024, 1024], P('fsdp'), may hold values from -0.1875 to 0.1875
- w_key: bfloat16 [1024, 1024], P('fsdp'), may hold values from -0.1875 to 0.1875
- w_value: bfloat16 [1024, 1024], P('fsdp'), may hold values from -0.1875 to 0.1875
- w_out: bfloat16 [1024, 1024], P('fsdp'), may hold values from -0.75 to 0.75
- b_query: bfloat16 [1024], P('fsdp'), may hold values from -3 to 3
- b_value: bfloat16 [1024], P('fsdp'), may hold values from -3 to 3
- b_out: bfloat16 [1024], P('fsdp'), may hold values from -3 to 3
- gain_one: bfloat16 [1024], P('fsdp'), may hold values from 0.099609375 to 1.8984375
- shift_one: bfloat16 [1024], P('fsdp'), may hold values from -3 to 3
- w_up: bfloat16 [1024, 4096], P('fsdp'), may hold values from -0.1875 to 0.1875
- b_up: bfloat16 [4096], P('fsdp'), may hold values from -3 to 3
- w_down: bfloat16 [4096, 1024], P('fsdp'), may hold values from -0.09375 to 0.09375
- b_down: bfloat16 [1024], P('fsdp'), may hold values from -3 to 3
- gain_two: bfloat16 [1024], P('fsdp'), may hold values from 0.099609375 to 1.8984375
- shift_two: bfloat16 [1024], P('fsdp'), may hold values from -3 to 3
- cotangent: bfloat16 [2, 4096, 1024], P('fsdp', 'ctx'), may hold values from -6 to 6
Outputs:
- layer_out: bfloat16 [2, 4096, 1024], P('fsdp', 'ctx')
- token_grad: bfloat16 [2, 4096, 1024], P('fsdp', 'ctx')
- grad_w_query: float32 [1024, 1024], P('fsdp')
- grad_w_key: float32 [1024, 1024], P('fsdp')
- grad_w_value: float32 [1024, 1024], P('fsdp')
- grad_w_out: float32 [1024, 1024], P('fsdp')
- grad_b_query: float32 [1024], P('fsdp')
- grad_b_value: float32 [1024], P('fsdp')
- grad_b_out: float32 [1024], P('fsdp')
- grad_gain_one: float32 [1024], P('fsdp')
- grad_shift_one: float32 [1024], P('fsdp')
- grad_w_up: float32 [1024, 4096], P('fsdp')
- grad_b_up: float32 [4096], P('fsdp')
- grad_w_down: float32 [4096, 1024], P('fsdp')
- grad_b_down: float32 [1024], P('fsdp')
- grad_gain_two: float32 [1024], P('fsdp')
- grad_shift_two: float32 [1024], P('fsdp')
The draws below stay inside these ranges and needn't reach their ends.
Inputs may be any that keep to these rules, and one draw needn't show every extreme that they name: `segments`: within each sequence the document numbers start at 0, never fall and use every number up to 7; no document has more than 3072 tokens, and one in each sequence has exactly 3072.
All inputs are finite; a program needn't handle non-finite values.
Results may differ from the reference program's by a relative error of at most 0.013.
Values may be sent and summed in bfloat16 or wider, within the bound.
No kernel may reach another device: no remote copies, remote signals or barrier semaphores. Data moves between devices by JAX's collectives and lax.ppermute only.
A program may use at most 256 MiB of HBM per device.

```python
import math
import jax
import jax.numpy as jnp
import numpy as np
from jax import lax

D = 1024
HEADS = 16
FF = 4096
LENGTH = 4096
SEQS = 2
DOCS = 8
MOST = 3072


def level_of(key, shape, shards, low, high):
    def one(axis_at, shards_of):
        draws = jax.random.uniform(jax.random.fold_in(jax.random.fold_in(key, 6), axis_at), (shards_of,), jnp.float32, low / len(shards), high / len(shards))
        return jnp.repeat(jnp.exp(draws), shape[axis_at] // shards_of).reshape((-1,) + (1,) * (len(shape) - axis_at - 1))

    loudness = one(*shards[0])
    for cut in shards[1:]:
        loudness = loudness * one(*cut)
    return loudness


def split_up(amount, total, reach, skew):
    weights = [(1 << 20) // math.isqrt(standing ** skew) + 1 for standing in range(2, amount + 1)]
    rest, holding = total - reach - (amount - 1), [1] * (amount - 1)
    while rest > 0:
        movable = [i for i in range(amount - 1) if holding[i] < reach]
        mass, remaining = sum([weights[i] for i in movable]), rest
        for i in movable:
            more = min(reach - holding[i], max(1, remaining * weights[i] // mass), rest)
            holding[i] = holding[i] + more
            rest = rest - more
    return np.array([reach] + holding)


def ragged_sizes(stream_key, number_of, total, limit, slope):
    if number_of == 2:
        one = jax.random.randint(stream_key, (), max(1, total - limit), min(limit, total - 1) + 1)
        return jnp.stack([one, total - one])
    sizes = jnp.asarray(split_up(number_of, total, limit, slope), jnp.int32)
    couples = (number_of - 1) // 2
    donor, receiver = sizes[1:1 + 2 * couples:2], sizes[2:2 + 2 * couples:2]
    margin = jnp.minimum(donor - 1, limit - receiver)
    passed = jax.random.randint(jax.random.fold_in(stream_key, 1), (couples,), 0, 1 << 20) % (margin + 1)
    sizes = sizes.at[1:1 + 2 * couples:2].set(donor - passed).at[2:2 + 2 * couples:2].set(receiver + passed)
    return sizes[jax.random.permutation(jax.random.fold_in(stream_key, 2), number_of)]


def bell_draw(key, dims, width, most, shards=(), kind=jnp.bfloat16):
    loudness = level_of(key, dims, shards, -0.22, 0.18) if shards else 1.0
    entries = jax.random.normal(key, dims, jnp.float32) * width * loudness
    return jnp.minimum(jnp.maximum(entries, -most), most).astype(kind)


def setup_inputs(seed: int = 0) -> dict:
    streams_of = jax.random.split(jax.random.key(seed), 19)
    tokens = bell_draw(streams_of[0], (SEQS, LENGTH, D), 1.0, 6.0, ((0, 2), (1, 16)))
    segments = jax.vmap(lambda own: jnp.searchsorted(jnp.cumsum(ragged_sizes(own, DOCS, LENGTH, MOST, 2)), jnp.arange(LENGTH), side="right"))(jax.random.split(streams_of[1], SEQS)).reshape((SEQS, LENGTH)).astype(jnp.int32)
    w_query = bell_draw(streams_of[2], (D, D), D ** -0.5, 0.1875, ((0, 2),))
    w_key = bell_draw(streams_of[3], (D, D), D ** -0.5, 0.1875, ((0, 2),))
    w_value = bell_draw(streams_of[4], (D, D), D ** -0.5, 0.1875, ((0, 2),))
    w_out = bell_draw(streams_of[5], (D, D), (D // 16) ** -0.5, 0.75, ((0, 2),))
    b_query = bell_draw(streams_of[6], (D,), 0.5, 3.0, ((0, 2),))
    b_value = bell_draw(streams_of[7], (D,), 0.5, 3.0, ((0, 2),))
    b_out = bell_draw(streams_of[8], (D,), 0.5, 3.0, ((0, 2),))
    gain_one = jnp.clip(1.0 + 0.18 * jax.random.normal(streams_of[9], (D,), jnp.float32), 0.099609375, 1.8984375).astype(jnp.bfloat16)
    shift_one = bell_draw(streams_of[10], (D,), 0.5, 3.0, ((0, 2),))
    w_up = bell_draw(streams_of[11], (D, FF), D ** -0.5, 0.1875, ((0, 2),))
    b_up = bell_draw(streams_of[12], (FF,), 0.5, 3.0, ((0, 2),))
    w_down = bell_draw(streams_of[13], (FF, D), FF ** -0.5, 0.09375, ((0, 2),))
    b_down = bell_draw(streams_of[14], (D,), 0.5, 3.0, ((0, 2),))
    gain_two = jnp.clip(1.0 + 0.18 * jax.random.normal(streams_of[15], (D,), jnp.float32), 0.099609375, 1.8984375).astype(jnp.bfloat16)
    shift_two = bell_draw(streams_of[16], (D,), 0.5, 3.0, ((0, 2),))
    cotangent = bell_draw(streams_of[17], (SEQS, LENGTH, D), 1.0, 6.0, ((0, 2), (1, 16)))
    return dict(tokens=tokens, segments=segments, w_query=w_query, w_key=w_key, w_value=w_value, w_out=w_out, b_query=b_query, b_value=b_value, b_out=b_out, gain_one=gain_one, shift_one=shift_one, w_up=w_up, b_up=b_up, w_down=w_down, b_down=b_down, gain_two=gain_two, shift_two=shift_two, cotangent=cotangent)


@jax.custom_vjp
def low(v):
    return lax.optimization_barrier(v.astype(jnp.bfloat16)).astype(jnp.float32)

@jax.custom_vjp
def low_back(v):
    return v

def low_keep(v):
    return (low(v), None)

def low_pass(kept, grad):
    return (grad,)

def back_keep(v):
    return (v, None)

def back_low(kept, grad):
    return (low(grad),)
low.defvjp(low_keep, low_pass)
low_back.defvjp(back_keep, back_low)

def matmul(left, right):
    return jnp.dot(left, right, precision=lax.Precision.HIGHEST)

def layer_norm(hidden, gain, shift):
    mean = lax.optimization_barrier(jnp.mean(hidden, axis=-1, keepdims=True))
    centred = hidden - mean
    variance = lax.optimization_barrier(jnp.mean(centred * centred, axis=-1, keepdims=True))
    return centred * lax.rsqrt(variance + 1e-05) * gain + shift

def sequence_layer(inputs, seg, params):
    w_query, w_key, w_value, w_out, b_query, b_value, b_out, gain_one, shift_one, w_up, b_up, w_down, b_down, gain_two, shift_two = params
    length = inputs.shape[0]
    head = D // HEADS
    scale = 1.0 / math.sqrt(head)
    queries = low(low_back(matmul(inputs, w_query)) + b_query)
    keys = low(low_back(matmul(inputs, w_key)))
    values = low(low_back(matmul(inputs, w_value)) + b_value)
    rows = min(512, length)
    key_heads = keys.reshape(length, HEADS, head)
    value_heads = values.reshape(length, HEADS, head)
    query_blocks = queries.reshape(length // rows, rows, HEADS, head)
    seg_blocks = seg.reshape(length // rows, rows)

    def attend(item):
        block, block_seg = item
        scores = jnp.einsum('qhe,khe->hqk', block, key_heads, precision=lax.Precision.HIGHEST) * scale
        same = (block_seg[:, None] == seg[None, :])[None]
        scores = low_back(jnp.where(same, scores, -1e+30))
        probs = jax.nn.softmax(scores, axis=-1)
        return jnp.einsum('hqk,khe->qhe', low(probs), value_heads, precision=lax.Precision.HIGHEST)
    attended = lax.map(jax.checkpoint(attend), (query_blocks, seg_blocks))
    attended = low_back(low(attended.reshape(length, D)))
    branch = low_back(matmul(attended, w_out)) + b_out
    first = layer_norm(inputs + branch, gain_one, shift_one)
    hidden_pre = low_back(matmul(low(first), w_up)) + b_up
    active = low(jax.nn.gelu(hidden_pre, approximate=False))
    second = low_back(matmul(active, w_down)) + b_down
    return layer_norm(first + second, gain_two, shift_two)

def reference(tokens, segments, w_query, w_key, w_value, w_out, b_query, b_value, b_out, gain_one, shift_one, w_up, b_up, w_down, b_down, gain_two, shift_two, cotangent):
    params = tuple((p.astype(jnp.float32) for p in (w_query, w_key, w_value, w_out, b_query, b_value, b_out, gain_one, shift_one, w_up, b_up, w_down, b_down, gain_two, shift_two)))

    def one_sequence(total, item):
        inputs, seg, grad_out = item

        def apply(values_in, weights):
            return sequence_layer(values_in, seg, weights)
        result, pull = jax.vjp(apply, inputs.astype(jnp.float32), params)
        d_inputs, d_params = pull(grad_out.astype(jnp.float32))
        total = jax.tree.map(jnp.add, total, d_params)
        return (total, (result.astype(jnp.bfloat16), d_inputs.astype(jnp.bfloat16)))
    zeros = tuple((jnp.zeros(p.shape, jnp.float32) for p in params))
    total, (layer_out, token_grad) = lax.scan(one_sequence, zeros, (tokens, segments, cotangent))
    return (layer_out, token_grad, total[0], total[1], total[2], total[3], total[4], total[5], total[6], total[7], total[8], total[9], total[10], total[11], total[12], total[13], total[14])
```

```python
import functools
import math

import jax
import jax.numpy as jnp
from jax import lax
from jax.experimental import pallas as pl
from jax.experimental.pallas import tpu as pltpu
from jax.sharding import PartitionSpec as P

HEADS = 16
LOG2E = 1.4426950408889634
NEG = -1e30
BF = jnp.bfloat16
F32 = jnp.float32


def layer_norm(hidden, gain, shift):
    mean = jnp.mean(hidden, axis=-1, keepdims=True)
    centred = hidden - mean
    variance = jnp.mean(centred * centred, axis=-1, keepdims=True)
    return centred * lax.rsqrt(variance + 1e-05) * gain + shift


def gelu_exact(value):
    return jax.nn.gelu(value, approximate=False)


def dot(left, right, on_left, on_right):
    return lax.dot_general(
        left, right, (((on_left,), (on_right,)), ((), ())), preferred_element_type=F32
    )


def flip(value, axis, bit, size):
    return lax.ppermute(value, axis, [(i, i ^ bit) for i in range(size)])


def forward_kernel(
    lo_ref, hi_ref, in_lo_ref, in_hi_ref, q_ref, k_ref, vt_ref, start_ref, end_ref,
    out_ref, lse_ref, total_ref, *, bk, scale
):
    i = pl.program_id(0)
    bq = q_ref.shape[0]
    q = q_ref[...]
    start, end = start_ref[...], end_ref[...]
    total_ref[...] = jnp.zeros_like(total_ref)

    def step(j, carry, masked):
        peak, norm = carry
        at = pl.multiple_of(j * bk, bk)
        s = dot(k_ref[pl.ds(at, bk), :], q, 1, 1) * (scale * LOG2E)
        if masked:
            at_key = lax.broadcasted_iota(jnp.int32, (bk, bq), 0) + at
            s = jnp.where((at_key >= start) & (at_key < end), s, NEG)
        new_peak = jnp.maximum(peak, jnp.max(s, axis=0, keepdims=True))
        p = jnp.exp2(s - new_peak)
        shrink = jnp.exp2(peak - new_peak)
        norm = norm * shrink + jnp.sum(p, axis=0, keepdims=True)
        total_ref[...] = total_ref[...] * shrink + dot(vt_ref[:, pl.ds(at, bk)], p.astype(BF), 1, 0)
        return new_peak, norm

    lo, hi, in_lo, in_hi = lo_ref[i], hi_ref[i], in_lo_ref[i], in_hi_ref[i]
    carry = (jnp.full((1, bq), NEG, F32), jnp.zeros((1, bq), F32))
    carry = lax.fori_loop(in_lo, in_hi, lambda j, c: step(j, c, False), carry)
    carry = lax.fori_loop(lo, in_lo, lambda j, c: step(j, c, True), carry)
    peak, norm = lax.fori_loop(in_hi, hi, lambda j, c: step(j, c, True), carry)
    out_ref[...] = total_ref[...] / norm
    lse_ref[...] = peak + jnp.log2(norm)


def block_ranges(starts, ends, rows, others):
    first, last = starts.reshape(-1, rows), ends.reshape(-1, rows)
    lo = first[:, 0] // others
    hi = (last[:, -1] + others - 1) // others
    in_lo = jnp.clip((first[:, -1] + others - 1) // others, lo, hi)
    in_hi = jnp.clip(last[:, 0] // others, in_lo, hi)
    return lo, hi, in_lo, in_hi


def attention_forward(q, k, vt, starts, ends, scale, bq=1024, bk=512):
    count, d = q.shape
    length = k.shape[0]
    bq = min(bq, count)
    ranges = block_ranges(starts, ends, bq, bk)
    row = lambda: pl.BlockSpec((1, bq), lambda i, *_: (0, i))
    whole = lambda shape: pl.BlockSpec(shape, lambda i, *_: (0, 0))
    return pl.pallas_call(
        functools.partial(forward_kernel, bk=bk, scale=scale),
        out_shape=(
            jax.ShapeDtypeStruct((d, count), F32),
            jax.ShapeDtypeStruct((1, count), F32),
        ),
        grid_spec=pltpu.PrefetchScalarGridSpec(
            num_scalar_prefetch=4,
            grid=(count // bq,),
            in_specs=[
                pl.BlockSpec((bq, d), lambda i, *_: (i, 0)),
                whole((length, d)),
                whole((d, length)),
                row(),
                row(),
            ],
            out_specs=[pl.BlockSpec((d, bq), lambda i, *_: (0, i)), row()],
            scratch_shapes=[pltpu.VMEM((d, bq), F32)],
        ),
        compiler_params=pltpu.CompilerParams(vmem_limit_bytes=40 << 20),
        cost_estimate=pl.CostEstimate(
            flops=4 * count * length * d, bytes_accessed=length * d * 16, transcendentals=count * length
        ),
        name="attention_forward",
    )(*ranges, q, k, vt, starts[None], ends[None])


def backward_kernel(
    lo_ref, hi_ref, in_lo_ref, in_hi_ref, k_ref, v_ref, kt_ref, q_ref, do_ref, lse_ref, delta_ref, start_ref,
    end_ref, dk_ref, dv_ref, dqt_ref, *, bq, scale
):
    j = pl.program_id(0)
    bk = k_ref.shape[0]

    @pl.when(j == 0)
    def _():
        dqt_ref[...] = jnp.zeros_like(dqt_ref)

    k, v, kt = k_ref[...], v_ref[...], kt_ref[...]
    dk_ref[...] = jnp.zeros_like(dk_ref)
    dv_ref[...] = jnp.zeros_like(dv_ref)

    def step(i, masked):
        at = pl.multiple_of(i * bq, bq)
        row = pl.ds(at, bq)
        q, do = q_ref[row, :], do_ref[row, :]
        s = dot(k, q, 1, 1) * (scale * LOG2E) - lse_ref[:, row]
        if masked:
            at_key = lax.broadcasted_iota(jnp.int32, (bk, bq), 0) + j * bk
            s = jnp.where((at_key >= start_ref[:, row]) & (at_key < end_ref[:, row]), s, NEG)
        p = jnp.exp2(s)
        dp = dot(v, do, 1, 1)
        dv_ref[...] += dot(p.astype(BF), do, 1, 0)
        ds = (p * (dp - delta_ref[:, row])).astype(BF)
        dk_ref[...] += dot(ds, q, 1, 0)
        dqt_ref[:, row] += dot(kt, ds, 1, 0)

    lo, hi, in_lo, in_hi = lo_ref[j], hi_ref[j], in_lo_ref[j], in_hi_ref[j]
    pl.loop(in_lo, in_hi)(lambda i: step(i, False))
    pl.loop(lo, in_lo)(lambda i: step(i, True))
    pl.loop(in_hi, hi)(lambda i: step(i, True))


def attention_backward(q, k, v, kt, do, lse, delta, starts, ends, ranges, scale, bq, bk):
    count, d = q.shape
    length = k.shape[0]
    whole = lambda shape: pl.BlockSpec(shape, lambda j, *_: (0, 0))
    keys = lambda: pl.BlockSpec((bk, d), lambda j, *_: (j, 0))
    return pl.pallas_call(
        functools.partial(backward_kernel, bq=bq, scale=scale),
        out_shape=(
            jax.ShapeDtypeStruct((length, d), F32),
            jax.ShapeDtypeStruct((length, d), F32),
            jax.ShapeDtypeStruct((d, count), F32),
        ),
        grid_spec=pltpu.PrefetchScalarGridSpec(
            num_scalar_prefetch=4,
            grid=(length // bk,),
            in_specs=[
                keys(),
                keys(),
                pl.BlockSpec((d, bk), lambda j, *_: (0, j)),
                whole((count, d)),
                whole((count, d)),
                whole((1, count)),
                whole((1, count)),
                whole((1, count)),
                whole((1, count)),
            ],
            out_specs=[keys(), keys(), whole((d, count))],
        ),
        compiler_params=pltpu.CompilerParams(vmem_limit_bytes=48 << 20),
        cost_estimate=pl.CostEstimate(
            flops=10 * count * length * d, bytes_accessed=length * d * 40, transcendentals=count * length
        ),
        name="attention_backward",
    )(*ranges, k, v, kt, q, do, lse, delta, starts[None], ends[None])


def body(ctx, fsdp, tokens, segments, w_query, w_key, w_value, w_out, b_query, b_value, b_out, gain_one, shift_one,
         w_up, b_up, w_down, b_down, gain_two, shift_two, cotangent):
    _, block, width = tokens.shape
    heads = HEADS
    d = width // heads
    scale = 1.0 / math.sqrt(d)
    parts = ctx // heads
    mine = block // parts
    length = ctx * block
    count = length // parts
    hidden = w_up.shape[1]
    shard = w_query.shape[0]
    me = lax.axis_index("ctx")
    row = lax.axis_index("fsdp")
    head, part = me // parts, me % parts
    core = me % 2
    cut = lambda a, at, size, axis: lax.dynamic_slice_in_dim(a, at, size, axis)

    def gather_small(a):
        if fsdp == 2:
            other = flip(a, "fsdp", 1, 2)
            return jnp.concatenate([jnp.where(row == 0, a, other), jnp.where(row == 0, other, a)], axis=0)
        return lax.all_gather(a, "fsdp", axis=0, tiled=True)

    def gather_weight(w):
        if fsdp != 2:
            return lax.all_gather(w, "fsdp", axis=0, tiled=True)
        rows = w.shape[0]
        half = rows // 2
        near = flip(cut(w, core * half, half, 0), "fsdp", 1, 2)
        far = flip(near, "ctx", 1, ctx)
        whole = jnp.zeros((2 * rows, w.shape[1]), w.dtype)
        whole = lax.dynamic_update_slice_in_dim(whole, w, row * rows, 0)
        whole = lax.dynamic_update_slice_in_dim(whole, near, (1 - row) * rows + core * half, 0)
        return lax.dynamic_update_slice_in_dim(whole, far, (1 - row) * rows + (1 - core) * half, 0)

    everyone = lax.all_gather(tokens[0], "ctx", axis=0, tiled=True)
    slices = jnp.concatenate([cut(w, head * d, d, 1) for w in (w_query, w_key, w_value)], axis=1)
    w_head = gather_small(slices)
    small = jnp.stack([b_query, b_value, b_out, gain_one, shift_one, b_down, gain_two, shift_two])
    small = jnp.concatenate([small.reshape(-1), b_up])[None]
    small = gather_small(small) if fsdp == 2 else lax.all_gather(small, "fsdp", axis=0, tiled=True)
    eight = small[:, : 8 * shard].reshape(-1, 8, shard).transpose(1, 0, 2).reshape(8, width).astype(F32)
    bq_, bv_, bo, gain1, shift1, bd, gain2, shift2 = (eight[i] for i in range(8))
    bu = small[:, 8 * shard :].reshape(hidden).astype(F32)
    wo = gather_weight(w_out)
    wu = gather_weight(w_up)
    wd = gather_weight(w_down)
    wq, wk, wv = gather_weight(w_query), gather_weight(w_key), gather_weight(w_value)

    projected = dot(everyone, w_head, 1, 0)
    my_bias = jnp.concatenate([cut(bq_, head * d, d, 0), jnp.zeros((d,), F32), cut(bv_, head * d, d, 0)])
    projected = (projected + my_bias).astype(BF)
    own_part = lambda a: cut(a.reshape((ctx, block) + a.shape[1:]), part * mine, mine, 1).reshape(
        (count,) + a.shape[1:]
    )
    q = own_part(projected[:, :d])
    k, v = projected[:, d : 2 * d], projected[:, 2 * d :]
    kt, vt = k.T, v.T
    seg = segments[0]
    all_numbers = seg[None, :]
    starts_all = jnp.sum(all_numbers < seg[:, None], axis=1, dtype=jnp.int32)
    ends_all = jnp.sum(all_numbers <= seg[:, None], axis=1, dtype=jnp.int32)
    starts, ends = own_part(starts_all), own_part(ends_all)

    attended_t, lse = attention_forward(q, k, vt, starts, ends, scale)
    outgoing = attended_t.astype(BF).reshape(d, ctx, mine).transpose(1, 0, 2)
    incoming = lax.all_to_all(outgoing, "ctx", 0, 0, tiled=True)
    attended = incoming.reshape(heads, parts, d, mine).transpose(1, 3, 0, 2).reshape(block, width)

    inputs = tokens[0]
    branch = dot(attended, wo, 1, 0) + bo
    first, first_pull = jax.vjp(layer_norm, inputs.astype(F32) + branch, gain1, shift1)
    first_low = first.astype(BF)
    hidden_pre = dot(first_low, wu, 1, 0) + bu
    active, active_pull = jax.vjp(gelu_exact, hidden_pre)
    active_low = active.astype(BF)
    second = dot(active_low, wd, 1, 0) + bd
    output, out_pull = jax.vjp(layer_norm, first + second, gain2, shift2)
    d_second, grad_gain_two, grad_shift_two = out_pull(cotangent[0].astype(F32))
    d_second_low = d_second.astype(BF)
    (d_hidden,) = active_pull(dot(d_second_low, wd, 1, 1))
    d_hidden_low = d_hidden.astype(BF)
    d_first = d_second + dot(d_hidden_low, wu, 1, 1)
    d_branch, grad_gain_one, grad_shift_one = first_pull(d_first)
    d_branch_low = d_branch.astype(BF)
    d_attended_t = dot(wo, d_branch_low, 1, 1).astype(BF)
    outgoing = d_attended_t.reshape(heads, d, parts, mine).transpose(0, 2, 1, 3).reshape(ctx, d, mine)
    do_t = lax.all_to_all(outgoing, "ctx", 0, 0, tiled=True)
    do = do_t.transpose(0, 2, 1).reshape(count, d)
    delta = jnp.sum(
        attended_t.reshape(d, ctx, mine) * do_t.transpose(1, 0, 2).astype(F32), axis=0
    ).reshape(1, count)

    bits = lambda n: [1 << i for i in range(n.bit_length() - 1)]

    def reduce_matrix(left, right, first_bits):
        rows, columns = left.shape[1], right.shape[1]
        order = first_bits + [(a, b) for a, n in (("fsdp", fsdp), ("ctx", ctx)) for b in bits(n) if (a, b) not in first_bits]
        place = [("fsdp", b) for b in reversed(bits(fsdp))] + [("ctx", b) for b in bits(ctx)]
        shape = [2] * len(place)
        chosen = lambda a, b: (lax.axis_index(a) // b) % 2
        size = {"fsdp": fsdp, "ctx": ctx}
        axis, bit = order[0]
        at = place.index((axis, bit))
        halves = left.reshape([left.shape[0]] + shape + [-1])
        pick = lambda which: lax.dynamic_index_in_dim(halves, which, at + 1, keepdims=False).reshape(left.shape[0], -1)
        own = chosen(axis, bit)
        sent = dot(pick(1 - own), right, 0, 0).astype(BF)
        total = (dot(pick(own), right, 0, 0) + flip(sent, axis, bit, size[axis]).astype(F32)).astype(BF)
        place.remove((axis, bit))
        total = total.reshape([2] * len(place) + [-1, columns])
        for axis, bit in order[1:]:
            at = place.index((axis, bit))
            own = chosen(axis, bit)
            keep = lax.dynamic_index_in_dim(total, own, at, keepdims=False)
            send = lax.dynamic_index_in_dim(total, 1 - own, at, keepdims=False)
            total = (keep.astype(F32) + flip(send, axis, bit, size[axis]).astype(F32)).astype(BF)
            place.remove((axis, bit))
        return total

    def spread_matrix(total, rows, columns):
        every = lax.all_gather(total, "ctx", axis=0, tiled=False)
        n = len(bits(ctx))
        every = every.reshape([2] * n + [-1, columns])
        every = every.transpose(list(reversed(range(n))) + [n, n + 1])
        return every.reshape(rows, columns).astype(F32)

    down_bits = [("ctx", 1), ("fsdp", 1), ("ctx", 2)]
    up_bits = [("ctx", 1), ("ctx", 2), ("fsdp", 1)]
    grad_w_down = spread_matrix(reduce_matrix(active_low, d_second_low, down_bits), w_down.shape[0], width)
    grad_w_up = spread_matrix(reduce_matrix(first_low, d_hidden_low, up_bits), shard, hidden)
    grad_w_out = spread_matrix(reduce_matrix(attended, d_branch_low, down_bits), shard, width)

    vectors = [
        jnp.sum(d_branch, axis=0), grad_gain_one, grad_shift_one, jnp.sum(d_second, axis=0), grad_gain_two,
        grad_shift_two,
    ]
    vectors = jnp.concatenate(
        [jnp.stack(vectors).reshape(6, fsdp, shard).transpose(1, 0, 2).reshape(fsdp, -1),
         jnp.sum(d_hidden, axis=0).reshape(fsdp, -1)], axis=1,
    )
    for bit in reversed(bits(fsdp)):
        own = (row // bit) % 2
        pair = vectors.reshape(2, -1, vectors.shape[1])
        keep = lax.dynamic_index_in_dim(pair, own, 0, keepdims=False)
        send = lax.dynamic_index_in_dim(pair, 1 - own, 0, keepdims=False)
        vectors = keep + flip(send, "fsdp", bit, fsdp)
    for bit in bits(ctx):
        vectors = vectors + flip(vectors, "ctx", bit, ctx)
    six = vectors[0, : 6 * shard].reshape(6, shard)
    grad_b_up = vectors[0, 6 * shard :]

    bq, bk = min(512, count), 512
    ranges = block_ranges(starts_all, ends_all, bk, bq * parts)
    dk, dv, dqt = attention_backward(q, k, v, kt, do, lse, delta, starts, ends, ranges, scale, bq, bk)
    dq = (dqt.T * scale).astype(BF)
    dk, dv = (dk * scale).astype(BF), dv.astype(BF)
    share = lambda a: a.reshape(ctx, -1, d)
    if parts == 1:
        outgoing = jnp.concatenate([dq, dk, dv], axis=1).reshape(ctx, block, 3 * d)
        incoming = lax.all_to_all(outgoing, "ctx", 0, 0, tiled=True)
        grads = [incoming[:, :, i * d : (i + 1) * d].transpose(1, 0, 2).reshape(block, width) for i in range(3)]
        everyone_q = everyone
    else:
        back = lambda a: lax.all_to_all(share(a), "ctx", 0, 0, tiled=True).reshape(heads, parts, -1, d)
        dq_in = back(dq).transpose(1, 2, 0, 3).reshape(block, width)
        summed = lambda a: jnp.sum(back(a).astype(F32), axis=1).astype(BF).transpose(1, 0, 2).reshape(block, width)
        grads = [dq_in, summed(dk), summed(dv)]
        everyone_q = own_part(everyone)
    token_grad = d_branch + dot(grads[0], wq, 1, 1) + dot(grads[1], wk, 1, 1) + dot(grads[2], wv, 1, 1)

    sums = jnp.concatenate(
        [jnp.sum(dq.astype(F32), axis=0), jnp.zeros((d,), F32), jnp.sum(dv.astype(F32), axis=0)]
    )
    grad_head = jnp.concatenate([dot(everyone_q, dq, 0, 0), dot(everyone, dk, 0, 0), dot(everyone, dv, 0, 0)], axis=1)
    grad_head = lax.psum_scatter(grad_head.astype(BF), "fsdp", scatter_dimension=0, tiled=True) if fsdp != 2 else (
        cut(grad_head, row * shard, shard, 0)
        + flip(cut(grad_head, (1 - row) * shard, shard, 0).astype(BF), "fsdp", 1, 2).astype(F32)
    ).astype(BF)
    sums = jnp.broadcast_to(lax.psum(sums, "fsdp")[None], (16, 3 * d)).astype(BF)
    every = lax.all_gather(jnp.concatenate([grad_head, sums]), "ctx", axis=0, tiled=False)
    every = every.astype(F32).reshape(heads, parts, shard + 16, 3, d).sum(axis=1)
    every = every.transpose(2, 1, 0, 3).reshape(3, shard + 16, width)
    bias_q = cut(every[0, shard], row * shard, shard, 0)
    bias_v = cut(every[2, shard], row * shard, shard, 0)

    return (
        output[None].astype(BF),
        token_grad[None].astype(BF),
        every[0, :shard],
        every[1, :shard],
        every[2, :shard],
        grad_w_out,
        bias_q,
        bias_v,
        six[0],
        six[1],
        six[2],
        grad_w_up,
        grad_b_up,
        grad_w_down,
        six[3],
        six[4],
        six[5],
    )


def solution(mesh):
    line, matrix, rows = P("fsdp"), P("fsdp", None), P("fsdp", "ctx", None)
    placed = (
        (rows, matrix) + (matrix,) * 4 + (line,) * 5 + (matrix, line, matrix) + (line,) * 3 + (rows,)
    )
    outs = (rows, rows) + (matrix,) * 4 + (line,) * 5 + (matrix, line, matrix) + (line,) * 3
    return jax.shard_map(
        functools.partial(body, mesh.shape["ctx"], mesh.shape["fsdp"]),
        mesh=mesh,
        in_specs=placed,
        out_specs=outs,
        check_vma=False,
    )
```

```python
import functools
import math

import jax
import jax.numpy as jnp
from jax import lax
from jax.experimental import pallas as pl
from jax.experimental.pallas import tpu as pltpu
from jax.sharding import PartitionSpec as P

HEADS = 16
LOG2E = 1.4426950408889634
NEG = -1e30
BF = jnp.bfloat16
F32 = jnp.float32


def layer_norm(hidden, gain, shift):
    mean = jnp.mean(hidden, axis=-1, keepdims=True)
    centred = hidden - mean
    variance = jnp.mean(centred * centred, axis=-1, keepdims=True)
    return centred * lax.rsqrt(variance + 1e-05) * gain + shift


def gelu_exact(value):
    return jax.nn.gelu(value, approximate=False)


def dot(left, right, on_left, on_right):
    return lax.dot_general(
        left, right, (((on_left,), (on_right,)), ((), ())), preferred_element_type=F32
    )


def flip(value, axis, bit, size):
    return lax.ppermute(value, axis, [(i, i ^ bit) for i in range(size)])


def forward_kernel(
    lo_ref, hi_ref, in_lo_ref, in_hi_ref, q_ref, k_ref, vt_ref, start_ref, end_ref,
    out_ref, lse_ref, total_ref, *, bk, scale
):
    i = pl.program_id(0)
    bq = q_ref.shape[0]
    q = q_ref[...]
    start, end = start_ref[...], end_ref[...]
    total_ref[...] = jnp.zeros_like(total_ref)

    def step(j, carry, masked):
        peak, norm = carry
        at = pl.multiple_of(j * bk, bk)
        s = dot(k_ref[pl.ds(at, bk), :], q, 1, 1) * (scale * LOG2E)
        if masked:
            at_key = lax.broadcasted_iota(jnp.int32, (bk, bq), 0) + at
            s = jnp.where((at_key >= start) & (at_key < end), s, NEG)
        new_peak = jnp.maximum(peak, jnp.max(s, axis=0, keepdims=True))
        p = jnp.exp2(s - new_peak)
        shrink = jnp.exp2(peak - new_peak)
        norm = norm * shrink + jnp.sum(p, axis=0, keepdims=True)
        total_ref[...] = total_ref[...] * shrink + dot(vt_ref[:, pl.ds(at, bk)], p.astype(BF), 1, 0)
        return new_peak, norm

    lo, hi, in_lo, in_hi = lo_ref[i], hi_ref[i], in_lo_ref[i], in_hi_ref[i]
    carry = (jnp.full((1, bq), NEG, F32), jnp.zeros((1, bq), F32))
    carry = lax.fori_loop(in_lo, in_hi, lambda j, c: step(j, c, False), carry)
    carry = lax.fori_loop(lo, in_lo, lambda j, c: step(j, c, True), carry)
    peak, norm = lax.fori_loop(in_hi, hi, lambda j, c: step(j, c, True), carry)
    out_ref[...] = total_ref[...] / norm
    lse_ref[...] = peak + jnp.log2(norm)


def block_ranges(starts, ends, rows, others):
    first, last = starts.reshape(-1, rows), ends.reshape(-1, rows)
    lo = first[:, 0] // others
    hi = (last[:, -1] + others - 1) // others
    in_lo = jnp.clip((first[:, -1] + others - 1) // others, lo, hi)
    in_hi = jnp.clip(last[:, 0] // others, in_lo, hi)
    return lo, hi, in_lo, in_hi


def attention_forward(q, k, vt, starts, ends, scale, bq=1024, bk=512):
    count, d = q.shape
    length = k.shape[0]
    bq = min(bq, count)
    ranges = block_ranges(starts, ends, bq, bk)
    row = lambda: pl.BlockSpec((1, bq), lambda i, *_: (0, i))
    whole = lambda shape: pl.BlockSpec(shape, lambda i, *_: (0, 0))
    return pl.pallas_call(
        functools.partial(forward_kernel, bk=bk, scale=scale),
        out_shape=(
            jax.ShapeDtypeStruct((d, count), F32),
            jax.ShapeDtypeStruct((1, count), F32),
        ),
        grid_spec=pltpu.PrefetchScalarGridSpec(
            num_scalar_prefetch=4,
            grid=(count // bq,),
            in_specs=[
                pl.BlockSpec((bq, d), lambda i, *_: (i, 0)),
                whole((length, d)),
                whole((d, length)),
                row(),
                row(),
            ],
            out_specs=[pl.BlockSpec((d, bq), lambda i, *_: (0, i)), row()],
            scratch_shapes=[pltpu.VMEM((d, bq), F32)],
        ),
        compiler_params=pltpu.CompilerParams(vmem_limit_bytes=40 << 20),
        cost_estimate=pl.CostEstimate(
            flops=4 * count * length * d, bytes_accessed=length * d * 16, transcendentals=count * length
        ),
        name="attention_forward",
    )(*ranges, q, k, vt, starts[None], ends[None])


def backward_kernel(
    lo_ref, hi_ref, in_lo_ref, in_hi_ref, k_ref, v_ref, kt_ref, q_ref, do_ref, lse_ref, delta_ref, start_ref,
    end_ref, dqt_in_ref, dk_ref, dv_ref, dqt_ref, dk_sum, dv_sum, *, bq, scale, base
):
    j = pl.program_id(0) + base
    bk = k_ref.shape[0]

    @pl.when(pl.program_id(0) == 0)
    def _():
        dqt_ref[...] = dqt_in_ref[...]

    k, v, kt = k_ref[...], v_ref[...], kt_ref[...]
    dk_sum[...] = jnp.zeros_like(dk_sum)
    dv_sum[...] = jnp.zeros_like(dv_sum)

    def step(i, masked):
        at = pl.multiple_of(i * bq, bq)
        row = pl.ds(at, bq)
        q, do = q_ref[row, :], do_ref[row, :]
        s = dot(k, q, 1, 1) * (scale * LOG2E) - lse_ref[:, row]
        if masked:
            at_key = lax.broadcasted_iota(jnp.int32, (bk, bq), 0) + j * bk
            s = jnp.where((at_key >= start_ref[:, row]) & (at_key < end_ref[:, row]), s, NEG)
        p = jnp.exp2(s)
        dp = dot(v, do, 1, 1)
        dv_sum[...] += dot(p.astype(BF), do, 1, 0)
        ds = (p * (dp - delta_ref[:, row])).astype(BF)
        dk_sum[...] += dot(ds, q, 1, 0)
        dqt_ref[:, row] += dot(kt, ds, 1, 0)

    lo, hi, in_lo, in_hi = lo_ref[j], hi_ref[j], in_lo_ref[j], in_hi_ref[j]
    pl.loop(in_lo, in_hi)(lambda i: step(i, False))
    pl.loop(lo, in_lo)(lambda i: step(i, True))
    pl.loop(in_hi, hi)(lambda i: step(i, True))
    dk_ref[...] = (dk_sum[...] * scale).astype(dk_ref.dtype)
    dv_ref[...] = dv_sum[...].astype(dv_ref.dtype)


def attention_backward(q, k, v, kt, do, lse, delta, starts, ends, ranges, dqt, scale, bq, bk, base, blocks):
    count, d = q.shape
    whole = lambda shape: pl.BlockSpec(shape, lambda j, *_: (0, 0))
    keys = lambda at: pl.BlockSpec((bk, d), lambda j, *_: (j + at, 0))
    return pl.pallas_call(
        functools.partial(backward_kernel, bq=bq, scale=scale, base=base),
        out_shape=(
            jax.ShapeDtypeStruct((blocks * bk, d), BF),
            jax.ShapeDtypeStruct((blocks * bk, d), BF),
            jax.ShapeDtypeStruct((d, count), F32),
        ),
        grid_spec=pltpu.PrefetchScalarGridSpec(
            num_scalar_prefetch=4,
            grid=(blocks,),
            in_specs=[
                keys(base),
                keys(base),
                pl.BlockSpec((d, bk), lambda j, *_: (0, j + base)),
                whole((count, d)),
                whole((count, d)),
                whole((1, count)),
                whole((1, count)),
                whole((1, count)),
                whole((1, count)),
                whole((d, count)),
            ],
            out_specs=[keys(0), keys(0), whole((d, count))],
            scratch_shapes=[pltpu.VMEM((bk, d), F32), pltpu.VMEM((bk, d), F32)],
        ),
        compiler_params=pltpu.CompilerParams(vmem_limit_bytes=32 << 20),
        cost_estimate=pl.CostEstimate(
            flops=40 * count * blocks * bk * d, bytes_accessed=count * d * 24, transcendentals=count * blocks * bk
        ),
        name="attention_backward",
    )(*ranges, k, v, kt, q, do, lse, delta, starts[None], ends[None], dqt)


def body(ctx, fsdp, tokens, segments, w_query, w_key, w_value, w_out, b_query, b_value, b_out, gain_one, shift_one,
         w_up, b_up, w_down, b_down, gain_two, shift_two, cotangent):
    _, block, width = tokens.shape
    heads = HEADS
    d = width // heads
    scale = 1.0 / math.sqrt(d)
    parts = ctx // heads
    mine = block // parts
    length = ctx * block
    count = length // parts
    hidden = w_up.shape[1]
    shard = w_query.shape[0]
    me = lax.axis_index("ctx")
    row = lax.axis_index("fsdp")
    head, part = me // parts, me % parts
    core = me % 2
    cut = lambda a, at, size, axis: lax.dynamic_slice_in_dim(a, at, size, axis)

    bits = lambda n: [1 << i for i in range(n.bit_length() - 1)]
    sizes = {"fsdp": fsdp, "ctx": ctx}
    tie = lambda *arrays: lax.optimization_barrier(arrays)

    def gather_small(a):
        if fsdp == 2:
            other = flip(a, "fsdp", 1, 2)
            return jnp.concatenate([jnp.where(row == 0, a, other), jnp.where(row == 0, other, a)], axis=0)
        return lax.all_gather(a, "fsdp", axis=0, tiled=True)

    def near_half(w):
        if fsdp != 2:
            return lax.all_gather(w, "fsdp", axis=0, tiled=True)
        return flip(cut(w, core * (w.shape[0] // 2), w.shape[0] // 2, 0), "fsdp", 1, 2)

    def far_half(near):
        return flip(near, "ctx", 1, ctx) if fsdp == 2 else near

    def assemble(w, near, far):
        if fsdp != 2:
            return near
        rows, half = w.shape[0], w.shape[0] // 2
        whole = jnp.zeros((2 * rows, w.shape[1]), w.dtype)
        whole = lax.dynamic_update_slice_in_dim(whole, w, row * rows, 0)
        whole = lax.dynamic_update_slice_in_dim(whole, near, (1 - row) * rows + core * half, 0)
        return lax.dynamic_update_slice_in_dim(whole, far, (1 - row) * rows + (1 - core) * half, 0)

    def halves_of(place):
        return [("fsdp", b) for b in reversed(bits(fsdp))] + [("ctx", b) for b in bits(ctx)] if place is None else place

    def begin(left, right, step):
        axis, bit = step
        place = halves_of(None)
        at = place.index(step)
        split = left.reshape([left.shape[0]] + [2] * len(place) + [-1])
        own = (lax.axis_index(axis) // bit) % 2
        pick = lambda which: lax.dynamic_index_in_dim(split, which, at + 1, keepdims=False).reshape(left.shape[0], -1)
        sent = dot(pick(1 - own), right, 0, 0).astype(BF)
        return sent, lambda left_kept, received: (
            dot(left_kept, right, 0, 0) + received.astype(F32)
        ).astype(BF), pick(own)

    def split_step(total, place, step):
        axis, bit = step
        at = place.index(step)
        own = (lax.axis_index(axis) // bit) % 2
        keep = lax.dynamic_index_in_dim(total, own, at, keepdims=False)
        send = lax.dynamic_index_in_dim(total, 1 - own, at, keepdims=False)
        return keep, send, [p for p in place if p != step]

    def move(send, step):
        return flip(send, step[0], step[1], sizes[step[0]])

    def add(keep, received):
        return (keep.astype(F32) + received.astype(F32)).astype(BF)

    def spread(total, rows, columns):
        every = lax.all_gather(total, "ctx", axis=0, tiled=False)
        n = len(bits(ctx))
        every = every.reshape([2] * n + [-1, columns])
        every = every.transpose(list(reversed(range(n))) + [n, n + 1])
        return every.reshape(rows, columns)

    inputs = tokens[0]
    slices = jnp.concatenate([cut(w, head * d, d, 1) for w in (w_query, w_key, w_value)], axis=1)
    small = jnp.stack([b_query, b_value, b_out, gain_one, shift_one, b_down, gain_two, shift_two])
    small = jnp.concatenate([small.reshape(-1), b_up])[None]
    inputs, slices, small = tie(inputs, slices, small)
    everyone = lax.all_gather(inputs, "ctx", axis=0, tiled=True)
    w_head = gather_small(slices)
    small = gather_small(small)
    wo_near = near_half(w_out)
    wu_near = near_half(w_up)
    wo_near, w_down, w_head, small = tie(wo_near, w_down, w_head, small)
    wo = assemble(w_out, wo_near, far_half(wo_near))
    wd_near = near_half(w_down)
    wu_near, w_query, w_key, w_value, wo = tie(wu_near, w_query, w_key, w_value, wo)
    wu = assemble(w_up, wu_near, far_half(wu_near))
    wqkv = jnp.concatenate([w_query, w_key, w_value], axis=1)
    wqkv_near = near_half(wqkv)
    everyone, wu, wo = tie(everyone, wu, wo)

    eight = small[:, : 8 * shard].reshape(-1, 8, shard).transpose(1, 0, 2).reshape(8, width).astype(F32)
    bq_, bv_, bo, gain1, shift1, bd, gain2, shift2 = (eight[i] for i in range(8))
    bu = small[:, 8 * shard :].reshape(hidden).astype(F32)
    projected = dot(everyone, w_head, 1, 0)
    my_bias = jnp.concatenate([cut(bq_, head * d, d, 0), jnp.zeros((d,), F32), cut(bv_, head * d, d, 0)])
    projected = (projected + my_bias).astype(BF)
    own_part = lambda a: cut(a.reshape((ctx, block) + a.shape[1:]), part * mine, mine, 1).reshape(
        (count,) + a.shape[1:]
    )
    q = own_part(projected[:, :d])
    k, v = projected[:, d : 2 * d], projected[:, 2 * d :]
    kt, vt = k.T, v.T
    seg = segments[0]
    starts_all = jnp.sum(seg[None, :] < seg[:, None], axis=1, dtype=jnp.int32)
    ends_all = jnp.sum(seg[None, :] <= seg[:, None], axis=1, dtype=jnp.int32)
    starts, ends = own_part(starts_all), own_part(ends_all)

    attended_t, lse = attention_forward(q, k, vt, starts, ends, scale)
    attended_t, wd_near = tie(attended_t, wd_near)
    outgoing = attended_t.astype(BF).reshape(d, ctx, mine).transpose(1, 0, 2)
    incoming = lax.all_to_all(outgoing, "ctx", 0, 0, tiled=True)
    wd = assemble(w_down, wd_near, far_half(wd_near))
    incoming, wd = tie(incoming, wd)
    attended = incoming.reshape(heads, parts, d, mine).transpose(1, 3, 0, 2).reshape(block, width)
    branch = dot(attended, wo, 1, 0) + bo
    first, first_pull = jax.vjp(layer_norm, inputs.astype(F32) + branch, gain1, shift1)
    first_low = first.astype(BF)
    hidden_pre = dot(first_low, wu, 1, 0) + bu
    active, active_pull = jax.vjp(gelu_exact, hidden_pre)
    active_low = active.astype(BF)
    second = dot(active_low, wd, 1, 0) + bd
    output, out_pull = jax.vjp(layer_norm, first + second, gain2, shift2)

    d_second, grad_gain_two, grad_shift_two = out_pull(cotangent[0].astype(F32))
    d_second_low = d_second.astype(BF)
    core_step = ("ctx", 1)
    down_sent, down_keep, down_left = begin(active_low, d_second_low, core_step)
    down_sent, d_second_low = tie(down_sent, d_second_low)
    down_got = move(down_sent, core_step)
    (d_hidden,) = active_pull(dot(d_second_low, wd, 1, 1))
    d_hidden_low = d_hidden.astype(BF)
    up_sent, up_keep, up_left = begin(first_low, d_hidden_low, core_step)
    up_sent, d_hidden_low = tie(up_sent, d_hidden_low)
    up_got = move(up_sent, core_step)
    d_first = d_second + dot(d_hidden_low, wu, 1, 1)
    d_branch, grad_gain_one, grad_shift_one = first_pull(d_first)
    d_branch_low = d_branch.astype(BF)
    d_attended_t = dot(wo, d_branch_low, 1, 1).astype(BF)
    outgoing = d_attended_t.reshape(heads, d, parts, mine).transpose(0, 2, 1, 3).reshape(ctx, d, mine)
    do_t = lax.all_to_all(outgoing, "ctx", 0, 0, tiled=True)

    outgoing, down_left, up_left, attended = tie(outgoing, down_left, up_left, attended)
    place = [p for p in halves_of(None) if p != core_step]
    down = down_keep(down_left, down_got).reshape([2] * len(place) + [-1, width])
    rest = [("fsdp", b) for b in reversed(bits(fsdp))], [("ctx", b) for b in bits(ctx) if b > 1]
    down_order = rest[0] + rest[1]
    up_order = rest[1][:1] + rest[0] + rest[1][1:]
    down_place = up_place = place
    down_kept, down_send, down_place = split_step(down, down_place, down_order[0])
    down_got = move(down_send, down_order[0])
    out_sent, out_keep, out_left = begin(attended, d_branch_low, core_step)
    out_got = move(out_sent, core_step)
    up = up_keep(up_left, up_got)
    up = jnp.concatenate([up.reshape(-1, hidden), out_keep(out_left, out_got).reshape(-1, width)], axis=1)
    up = up.reshape([2] * len(place) + [-1, hidden + width])
    up_kept, up_send, up_place = split_step(up, up_place, up_order[0])
    up_got = move(up_send, up_order[0])
    do_t, down_send, up_send = tie(do_t, down_send, up_send)

    vectors = [
        jnp.sum(d_branch, axis=0), grad_gain_one, grad_shift_one, jnp.sum(d_second, axis=0), grad_gain_two,
        grad_shift_two,
    ]
    vectors = jnp.concatenate(
        [jnp.stack(vectors).reshape(6, fsdp, shard).transpose(1, 0, 2).reshape(fsdp, -1),
         jnp.sum(d_hidden, axis=0).reshape(fsdp, -1)], axis=1,
    )

    do = do_t.transpose(0, 2, 1).reshape(count, d)
    delta = jnp.sum(
        attended_t.reshape(d, ctx, mine) * do_t.transpose(1, 0, 2).astype(F32), axis=0
    ).reshape(1, count)
    bq, bk = min(512, count), 512
    ranges = block_ranges(starts_all, ends_all, bk, bq * parts)
    calls = 4
    blocks = length // bk // calls
    dqt = jnp.zeros((d, count), F32)
    dk, dv = [], []
    vector_steps = [("fsdp", b) for b in reversed(bits(fsdp))] + [("ctx", b) for b in bits(ctx)]
    todo = list(vector_steps)

    def vector_step(vectors, step):
        axis, bit = step
        if axis == "ctx":
            return vectors + flip(vectors, "ctx", bit, ctx)
        own = (row // bit) % 2
        pair = vectors.reshape(2, -1, vectors.shape[1])
        keep = lax.dynamic_index_in_dim(pair, own, 0, keepdims=False)
        return keep + flip(lax.dynamic_index_in_dim(pair, 1 - own, 0, keepdims=False), "fsdp", bit, fsdp)

    down_at, up_at = 1, 1
    for call in range(calls):
        dk_new, dv_new, dqt = attention_backward(
            q, k, v, kt, do, lse, delta, starts, ends, ranges, dqt, scale, bq, bk, call * blocks, blocks
        )
        dk.append(dk_new)
        dv.append(dv_new)
        if todo:
            vectors = vector_step(vectors, todo.pop(0))
        if call == calls - 2:
            down, up = add(down_kept, down_got), add(up_kept, up_got)
            down_kept, down_send, down_place = split_step(down, down_place, down_order[1])
            down_got = move(down_send, down_order[1])
            up_kept, up_send, up_place = split_step(up, up_place, up_order[1])
            up_got = move(up_send, up_order[1])
            dqt, down_send, up_send, vectors = tie(dqt, down_send, up_send, vectors)
            down_at, up_at = 2, 2
        elif call < calls - 1:
            dqt, vectors = tie(dqt, vectors)
    dk, dv = jnp.concatenate(dk), jnp.concatenate(dv)
    dq = (dqt.T * scale).astype(BF)

    share = lambda a: a.reshape(ctx, -1, d)
    wqkv_all = assemble(wqkv, wqkv_near, far_half(wqkv_near))
    wq, wk, wv = (wqkv_all[:, i * width : (i + 1) * width] for i in range(3))
    if parts == 1:
        outgoing = jnp.concatenate([dq, dk, dv], axis=1).reshape(ctx, block, 3 * d)
        incoming = lax.all_to_all(outgoing, "ctx", 0, 0, tiled=True)
        everyone_q = everyone
    else:
        back = lambda a: lax.all_to_all(share(a), "ctx", 0, 0, tiled=True).reshape(heads, parts, -1, d)
        dq_in = back(dq).transpose(1, 2, 0, 3).reshape(block, width)
        summed = lambda a: jnp.sum(back(a).astype(F32), axis=1).astype(BF).transpose(1, 0, 2).reshape(block, width)
        everyone_q = own_part(everyone)

    grad_head = jnp.concatenate([dot(everyone_q, dq, 0, 0), dot(everyone, dk, 0, 0), dot(everyone, dv, 0, 0)], axis=1)
    sums = jnp.concatenate(
        [jnp.sum(dq.astype(F32), axis=0), jnp.zeros((d,), F32), jnp.sum(dv.astype(F32), axis=0)]
    )
    sums = jnp.broadcast_to(sums[None, None], (fsdp, 16, 3 * d))
    grad_head = jnp.concatenate([grad_head.reshape(fsdp, shard, 3 * d), sums], axis=1)
    if fsdp == 2:
        sent = lax.dynamic_index_in_dim(grad_head, 1 - row, 0, keepdims=False).astype(BF)
        kept = lax.dynamic_index_in_dim(grad_head, row, 0, keepdims=False)
        grad_head = (kept + flip(sent, "fsdp", 1, 2).astype(F32)).astype(BF)
    else:
        grad_head = lax.psum_scatter(
            grad_head.reshape(-1, 3 * d).astype(BF), "fsdp", scatter_dimension=0, tiled=True
        )
    every = lax.all_gather(grad_head, "ctx", axis=0, tiled=False)

    down, up = add(down_kept, down_got), add(up_kept, up_got)
    while down_at < len(down_order):
        kept, send, down_place = split_step(down, down_place, down_order[down_at])
        down_got = move(send, down_order[down_at])
        up_kept, up_send, up_place = split_step(up, up_place, up_order[down_at])
        up_got = move(up_send, up_order[down_at])
        down, up = add(kept, down_got), add(up_kept, up_got)
        down_at += 1
    grad_w_down = spread(down, w_down.shape[0], width).astype(F32)
    grad_up_out = spread(up, shard, hidden + width)
    grad_w_up, grad_w_out = grad_up_out[:, :hidden].astype(F32), grad_up_out[:, hidden:].astype(F32)
    for step in todo:
        vectors = vector_step(vectors, step)
    six = vectors[0, : 6 * shard].reshape(6, shard)
    grad_b_up = vectors[0, 6 * shard :]

    if parts == 1:
        grads = [incoming[:, :, i * d : (i + 1) * d].transpose(1, 0, 2).reshape(block, width) for i in range(3)]
    else:
        grads = [dq_in, summed(dk), summed(dv)]
    token_grad = d_branch + dot(grads[0], wq, 1, 1) + dot(grads[1], wk, 1, 1) + dot(grads[2], wv, 1, 1)

    every = every.astype(F32).reshape(heads, parts, shard + 16, 3, d).sum(axis=1)
    every = every.transpose(2, 1, 0, 3).reshape(3, shard + 16, width)
    bias_q = cut(every[0, shard], row * shard, shard, 0)
    bias_v = cut(every[2, shard], row * shard, shard, 0)

    return (
        output[None].astype(BF),
        token_grad[None].astype(BF),
        every[0, :shard],
        every[1, :shard],
        every[2, :shard],
        grad_w_out,
        bias_q,
        bias_v,
        six[0],
        six[1],
        six[2],
        grad_w_up,
        grad_b_up,
        grad_w_down,
        six[3],
        six[4],
        six[5],
    )


def solution(mesh):
    line, matrix, rows = P("fsdp"), P("fsdp", None), P("fsdp", "ctx", None)
    placed = (
        (rows, matrix) + (matrix,) * 4 + (line,) * 5 + (matrix, line, matrix) + (line,) * 3 + (rows,)
    )
    outs = (rows, rows) + (matrix,) * 4 + (line,) * 5 + (matrix, line, matrix) + (line,) * 3
    return jax.shard_map(
        functools.partial(body, mesh.shape["ctx"], mesh.shape["fsdp"]),
        mesh=mesh,
        in_specs=placed,
        out_specs=outs,
        check_vma=False,
    )
```

```python
import functools
import math

import jax
import jax.numpy as jnp
from jax import lax
from jax.experimental import pallas as pl
from jax.experimental.pallas import tpu as pltpu
from jax.sharding import PartitionSpec as P

HEADS = 16
LOG2E = 1.4426950408889634
NEG = -1e30
BF = jnp.bfloat16
F32 = jnp.float32


def layer_norm(hidden, gain, shift):
    mean = jnp.mean(hidden, axis=-1, keepdims=True)
    centred = hidden - mean
    variance = jnp.mean(centred * centred, axis=-1, keepdims=True)
    return centred * lax.rsqrt(variance + 1e-05) * gain + shift


def gelu_exact(value):
    return jax.nn.gelu(value, approximate=False)


def dot(left, right, on_left, on_right):
    return lax.dot_general(
        left, right, (((on_left,), (on_right,)), ((), ())), preferred_element_type=F32
    )


def flip(value, axis, bit, size):
    return lax.ppermute(value, axis, [(i, i ^ bit) for i in range(size)])


def forward_kernel(
    lo_ref, hi_ref, in_lo_ref, in_hi_ref, q_ref, k_ref, v_ref, start_ref, end_ref,
    out_ref, low_ref, lse_ref, total_ref, vt_ref, *, bk, scale
):
    i = pl.program_id(0)
    bq = q_ref.shape[0]

    @pl.when(i == 0)
    def _():
        @pl.loop(0, v_ref.shape[0] // bk)
        def _(j):
            at = pl.multiple_of(j * bk, bk)
            vt_ref[:, pl.ds(at, bk)] = v_ref[pl.ds(at, bk), :].T

    q = q_ref[...]
    start, end = start_ref[...], end_ref[...]
    total_ref[...] = jnp.zeros_like(total_ref)

    def step(j, carry, masked):
        peak, norm = carry
        at = pl.multiple_of(j * bk, bk)
        s = dot(k_ref[pl.ds(at, bk), :], q, 1, 1) * (scale * LOG2E)
        if masked:
            at_key = lax.broadcasted_iota(jnp.int32, (bk, bq), 0) + at
            s = jnp.where((at_key >= start) & (at_key < end), s, NEG)
        new_peak = jnp.maximum(peak, jnp.max(s, axis=0, keepdims=True))
        p = jnp.exp2(s - new_peak)
        shrink = jnp.exp2(peak - new_peak)
        norm = norm * shrink + jnp.sum(p, axis=0, keepdims=True)
        total_ref[...] = total_ref[...] * shrink + dot(vt_ref[:, pl.ds(at, bk)], p.astype(BF), 1, 0)
        return new_peak, norm

    lo, hi, in_lo, in_hi = lo_ref[i], hi_ref[i], in_lo_ref[i], in_hi_ref[i]
    carry = (jnp.full((1, bq), NEG, F32), jnp.zeros((1, bq), F32))
    carry = lax.fori_loop(in_lo, in_hi, lambda j, c: step(j, c, False), carry)
    carry = lax.fori_loop(lo, in_lo, lambda j, c: step(j, c, True), carry)
    peak, norm = lax.fori_loop(in_hi, hi, lambda j, c: step(j, c, True), carry)
    out = total_ref[...] / norm
    out_ref[...] = out
    n = low_ref.shape[2]
    for piece in range(bq // n):
        low_ref[piece] = out[:, piece * n : (piece + 1) * n].astype(low_ref.dtype)
    lse_ref[...] = peak + jnp.log2(norm)


def block_ranges(starts, ends, rows, others):
    first, last = starts.reshape(-1, rows), ends.reshape(-1, rows)
    lo = first[:, 0] // others
    hi = (last[:, -1] + others - 1) // others
    in_lo = jnp.clip((first[:, -1] + others - 1) // others, lo, hi)
    in_hi = jnp.clip(last[:, 0] // others, in_lo, hi)
    return lo, hi, in_lo, in_hi


def attention_forward(q, k, v, starts, ends, scale, n, bq=1024, bk=512):
    count, d = q.shape
    length = k.shape[0]
    bq = min(bq, count)
    ranges = block_ranges(starts, ends, bq, bk)
    row = lambda: pl.BlockSpec((1, bq), lambda i, *_: (0, i))
    whole = lambda shape: pl.BlockSpec(shape, lambda i, *_: (0, 0))
    return pl.pallas_call(
        functools.partial(forward_kernel, bk=bk, scale=scale),
        out_shape=(
            jax.ShapeDtypeStruct((d, count), F32),
            jax.ShapeDtypeStruct((count // n, d, n), BF),
            jax.ShapeDtypeStruct((1, count), F32),
        ),
        grid_spec=pltpu.PrefetchScalarGridSpec(
            num_scalar_prefetch=4,
            grid=(count // bq,),
            in_specs=[
                pl.BlockSpec((bq, d), lambda i, *_: (i, 0)),
                whole((length, d)),
                whole((length, d)),
                row(),
                row(),
            ],
            out_specs=[
                pl.BlockSpec((d, bq), lambda i, *_: (0, i)),
                pl.BlockSpec((bq // n, d, n), lambda i, *_: (i, 0, 0)),
                row(),
            ],
            scratch_shapes=[pltpu.VMEM((d, bq), F32), pltpu.VMEM((d, length), BF)],
        ),
        compiler_params=pltpu.CompilerParams(vmem_limit_bytes=40 << 20),
        cost_estimate=pl.CostEstimate(
            flops=16 * count * length * d, bytes_accessed=length * d * 16, transcendentals=count * length
        ),
        name="attention_forward",
    )(*ranges, q, k, v, starts[None], ends[None])


def backward_kernel(
    lo_ref, hi_ref, in_lo_ref, in_hi_ref, k_ref, v_ref, q_ref, do_ref, lse_ref, delta_ref, start_ref,
    end_ref, dqt_in_ref, dkt_ref, dvt_ref, dqt_ref, dk_sum, dv_sum, *, bq, scale, base
):
    j = pl.program_id(0) + base
    bk = k_ref.shape[0]
    pieces = bq // do_ref.shape[2]

    @pl.when(pl.program_id(0) == 0)
    def _():
        dqt_ref[...] = dqt_in_ref[...]

    k, v = k_ref[...], v_ref[...]
    kt = k.T
    dk_sum[...] = jnp.zeros_like(dk_sum)
    dv_sum[...] = jnp.zeros_like(dv_sum)

    def step(i, masked):
        at = pl.multiple_of(i * bq, bq)
        row = pl.ds(at, bq)
        q = q_ref[row, :]
        do_t = jnp.concatenate([do_ref[i * pieces + n] for n in range(pieces)], axis=1)
        s = dot(k, q, 1, 1) * (scale * LOG2E) - lse_ref[:, row]
        if masked:
            at_key = lax.broadcasted_iota(jnp.int32, (bk, bq), 0) + j * bk
            s = jnp.where((at_key >= start_ref[:, row]) & (at_key < end_ref[:, row]), s, NEG)
        p = jnp.exp2(s)
        dp = dot(v, do_t, 1, 0)
        dv_sum[...] += dot(p.astype(BF), do_t, 1, 1)
        ds = (p * (dp - delta_ref[:, row])).astype(BF)
        dk_sum[...] += dot(ds, q, 1, 0)
        dqt_ref[:, row] += dot(kt, ds, 1, 0)

    lo, hi, in_lo, in_hi = lo_ref[j], hi_ref[j], in_lo_ref[j], in_hi_ref[j]
    pl.loop(in_lo, in_hi)(lambda i: step(i, False))
    pl.loop(lo, in_lo)(lambda i: step(i, True))
    pl.loop(in_hi, hi)(lambda i: step(i, True))
    dkt_ref[...] = (dk_sum[...] * scale).T.astype(dkt_ref.dtype)
    dvt_ref[...] = dv_sum[...].T.astype(dvt_ref.dtype)


def attention_backward(q, k, v, do_t, lse, delta, starts, ends, ranges, dqt, scale, bq, bk, base, blocks):
    count, d = q.shape
    whole = lambda shape: pl.BlockSpec(shape, lambda j, *_: (0,) * len(shape))
    keys = lambda: pl.BlockSpec((bk, d), lambda j, *_: (j + base, 0))
    columns = lambda: pl.BlockSpec((d, bk), lambda j, *_: (0, j))
    return pl.pallas_call(
        functools.partial(backward_kernel, bq=bq, scale=scale, base=base),
        out_shape=(
            jax.ShapeDtypeStruct((d, blocks * bk), BF),
            jax.ShapeDtypeStruct((d, blocks * bk), BF),
            jax.ShapeDtypeStruct((d, count), F32),
        ),
        grid_spec=pltpu.PrefetchScalarGridSpec(
            num_scalar_prefetch=4,
            grid=(blocks,),
            in_specs=[
                keys(),
                keys(),
                whole((count, d)),
                whole(do_t.shape),
                whole((1, count)),
                whole((1, count)),
                whole((1, count)),
                whole((1, count)),
                whole((d, count)),
            ],
            out_specs=[columns(), columns(), whole((d, count))],
            scratch_shapes=[pltpu.VMEM((bk, d), F32), pltpu.VMEM((bk, d), F32)],
        ),
        compiler_params=pltpu.CompilerParams(vmem_limit_bytes=32 << 20),
        cost_estimate=pl.CostEstimate(
            flops=40 * count * blocks * bk * d, bytes_accessed=count * d * 24, transcendentals=count * blocks * bk
        ),
        name="attention_backward",
    )(*ranges, k, v, q, do_t, lse, delta, starts[None], ends[None], dqt)


class Halving:
    def __init__(self, place, sizes):
        self.place, self.sizes, self.terms = list(place), sizes, []

    def own(self, step):
        return (lax.axis_index(step[0]) // step[1]) % 2

    def share(self, step, which):
        at = self.place.index(step)
        return [lax.dynamic_index_in_dim(t, which, at, keepdims=False) for t in self.terms]

    def total(self, terms):
        return sum((t.astype(F32) for t in terms[1:]), terms[0].astype(F32)).astype(BF)

    def send(self, step):
        sent = self.total(self.share(step, 1 - self.own(step)))
        self.terms = self.share(step, self.own(step))
        self.place.remove(step)
        return sent

    def receive(self, got):
        self.terms.append(got)


def body(ctx, fsdp, tokens, segments, w_query, w_key, w_value, w_out, b_query, b_value, b_out, gain_one, shift_one,
         w_up, b_up, w_down, b_down, gain_two, shift_two, cotangent):
    _, block, width = tokens.shape
    heads = HEADS
    d = width // heads
    scale = 1.0 / math.sqrt(d)
    parts = ctx // heads
    mine = block // parts
    length = ctx * block
    count = length // parts
    hidden = w_up.shape[1]
    shard = w_query.shape[0]
    me = lax.axis_index("ctx")
    row = lax.axis_index("fsdp")
    head, part = me // parts, me % parts
    core = me % 2
    cut = lambda a, at, size, axis: lax.dynamic_slice_in_dim(a, at, size, axis)

    bits = lambda n: [1 << i for i in range(n.bit_length() - 1)]
    sizes = {"fsdp": fsdp, "ctx": ctx}
    tie = lambda *arrays: lax.optimization_barrier(arrays)

    def gather_small(a):
        if fsdp == 2:
            other = flip(a, "fsdp", 1, 2)
            return jnp.concatenate([jnp.where(row == 0, a, other), jnp.where(row == 0, other, a)], axis=0)
        return lax.all_gather(a, "fsdp", axis=0, tiled=True)

    def near_half(w):
        if fsdp != 2:
            return lax.all_gather(w, "fsdp", axis=0, tiled=True)
        return flip(cut(w, core * (w.shape[0] // 2), w.shape[0] // 2, 0), "fsdp", 1, 2)

    def far_half(near):
        return flip(near, "ctx", 1, ctx) if fsdp == 2 else near

    def assemble(w, near, far):
        if fsdp != 2:
            return near
        rows, half = w.shape[0], w.shape[0] // 2
        whole = jnp.zeros((2 * rows, w.shape[1]), w.dtype)
        whole = lax.dynamic_update_slice_in_dim(whole, w, row * rows, 0)
        whole = lax.dynamic_update_slice_in_dim(whole, near, (1 - row) * rows + core * half, 0)
        return lax.dynamic_update_slice_in_dim(whole, far, (1 - row) * rows + (1 - core) * half, 0)

    def move(send, step):
        return flip(send, step[0], step[1], sizes[step[0]])

    core_step = ("ctx", 1)
    every_place = [("fsdp", b) for b in reversed(bits(fsdp))] + [("ctx", b) for b in bits(ctx)]
    own_bit = lambda step: (lax.axis_index(step[0]) // step[1]) % 2

    def columns_of(left, chosen):
        depth = max(every_place.index(step) for step in chosen) + 1
        size = left.shape[1] >> depth
        offsets = [0]
        for level, step in enumerate(every_place[:depth]):
            stride = left.shape[1] >> (level + 1)
            options = [chosen[step]] if step in chosen else [0, 1]
            offsets = [at + which * stride for at in offsets for which in options]
        return jnp.concatenate([cut(left, at, size, 1) for at in offsets], axis=1)

    def blocks(rows_data, place):
        return rows_data.reshape([2] * len(place) + [-1, rows_data.shape[1]])

    def first_share(left, right):
        return dot(columns_of(left, {core_step: 1 - own_bit(core_step)}), right, 0, 0).astype(BF)

    def second_share(left, right, got, step):
        place = [p for p in every_place if p != core_step]
        got = blocks(got, place)
        inner = [p for p in place if p != step]
        parts_of = []
        for which in (1 - own_bit(step), own_bit(step)):
            rows_data = dot(columns_of(left, {core_step: own_bit(core_step), step: which}), right, 0, 0)
            added = lax.dynamic_index_in_dim(got, which, place.index(step), keepdims=False)
            parts_of.append((blocks(rows_data, inner) + added.astype(F32)).astype(BF))
        rest = Halving(inner, sizes)
        rest.terms = [parts_of[1]]
        return parts_of[0], rest

    def in_order(every):
        n = len(bits(ctx))
        shape = every.shape
        every = every.reshape((2,) * n + shape[1:]).transpose(list(reversed(range(n))) + [n, n + 1])
        return every.reshape(-1, shape[2])

    inputs = tokens[0]
    everyone = lax.all_gather(inputs, "ctx", axis=0, tiled=True)
    by_head = lambda w: w.reshape(shard, heads, 1, d)
    wqkv = jnp.concatenate([by_head(w) for w in (w_query, w_key, w_value)], axis=2).reshape(shard, 3 * width)
    small = jnp.stack([b_query, b_value, b_out, gain_one, shift_one, b_down, gain_two, shift_two])
    small = jnp.concatenate([small.reshape(-1), b_up])[None]
    w_head = gather_small(jnp.concatenate([cut(w, head * d, d, 1) for w in (w_query, w_key, w_value)], axis=1))
    small = gather_small(small)
    wo_near = near_half(w_out)
    wu_near = near_half(w_up)
    wo_near, w_down, w_head, small = tie(wo_near, w_down, w_head, small)
    wo = assemble(w_out, wo_near, far_half(wo_near))
    wd_near = near_half(w_down)
    wu_near, wqkv, wo = tie(wu_near, wqkv, wo)
    wu = assemble(w_up, wu_near, far_half(wu_near))
    wqkv_near = near_half(wqkv)
    everyone, wu, wo = tie(everyone, wu, wo)

    eight = small[:, : 8 * shard].reshape(-1, 8, shard).transpose(1, 0, 2).reshape(8, width).astype(F32)
    bq_, bv_, bo, gain1, shift1, bd, gain2, shift2 = (eight[i] for i in range(8))
    bu = small[:, 8 * shard :].reshape(hidden).astype(F32)
    projected = dot(everyone, w_head, 1, 0)
    my_bias = jnp.concatenate([cut(bq_, head * d, d, 0), jnp.zeros((d,), F32), cut(bv_, head * d, d, 0)])
    projected = (projected + my_bias).astype(BF)
    own_part = lambda a: cut(a.reshape((ctx, block) + a.shape[1:]), part * mine, mine, 1).reshape(
        (count,) + a.shape[1:]
    )
    q = own_part(projected[:, :d])
    k, v = projected[:, d : 2 * d], projected[:, 2 * d :]
    seg = segments[0]
    starts_all = jnp.sum(seg[None, :] < seg[:, None], axis=1, dtype=jnp.int32)
    ends_all = jnp.sum(seg[None, :] <= seg[:, None], axis=1, dtype=jnp.int32)
    starts, ends = own_part(starts_all), own_part(ends_all)

    attended_t, outgoing, lse = attention_forward(q, k, v, starts, ends, scale, mine)
    outgoing, wd_near = tie(outgoing, wd_near)
    incoming = lax.all_to_all(outgoing, "ctx", 0, 0, tiled=True)
    wd = assemble(w_down, wd_near, far_half(wd_near))
    wqkv_all = assemble(wqkv, wqkv_near, far_half(wqkv_near))
    incoming, wd, wqkv_all = tie(incoming, wd, wqkv_all)
    attended = incoming.reshape(heads, parts, d, mine).transpose(1, 3, 0, 2).reshape(block, width)
    branch = dot(attended, wo, 1, 0) + bo
    first, first_pull = jax.vjp(layer_norm, inputs.astype(F32) + branch, gain1, shift1)
    first_low = first.astype(BF)
    hidden_pre = dot(first_low, wu, 1, 0) + bu
    active, active_pull = jax.vjp(gelu_exact, hidden_pre)
    active_low = active.astype(BF)
    second = dot(active_low, wd, 1, 0) + bd
    output, out_pull = jax.vjp(layer_norm, first + second, gain2, shift2)

    fsdp_steps = [("fsdp", b) for b in reversed(bits(fsdp))]
    ctx_steps = [("ctx", b) for b in bits(ctx) if b > 1]
    down_order = fsdp_steps + ctx_steps
    up_order = ctx_steps[1:2] + fsdp_steps + ctx_steps[:1] + ctx_steps[2:]
    d_second, grad_gain_two, grad_shift_two = out_pull(cotangent[0].astype(F32))
    d_second_low = d_second.astype(BF)
    down_sent = first_share(active_low, d_second_low)
    down_sent, d_second_low = tie(down_sent, d_second_low)
    down_got = move(down_sent, core_step)
    (d_hidden,) = active_pull(dot(d_second_low, wd, 1, 1))
    d_hidden_low = d_hidden.astype(BF)
    up_sent = first_share(first_low, d_hidden_low)
    up_sent, d_hidden_low, down_got = tie(up_sent, d_hidden_low, down_got)
    up_got = move(up_sent, core_step)
    down_sent, down = second_share(active_low, d_second_low, down_got, down_order[0])
    down_sent, d_hidden_low = tie(down_sent, d_hidden_low)
    down_got = move(down_sent, down_order[0])
    d_first = d_second + dot(d_hidden_low, wu, 1, 1)
    d_branch, grad_gain_one, grad_shift_one = first_pull(d_first)
    d_branch_low = d_branch.astype(BF)
    out_sent = first_share(attended, d_branch_low)
    d_attended_t = dot(wo, d_branch_low, 1, 1).astype(BF)
    outgoing = d_attended_t.reshape(heads, d, parts, mine).transpose(0, 2, 1, 3).reshape(ctx, d, mine)
    do_t = lax.all_to_all(outgoing, "ctx", 0, 0, tiled=True)

    outgoing, up_got, out_sent = tie(outgoing, up_got, out_sent)
    out_got = move(out_sent, core_step)
    up_sent, up = second_share(first_low, d_hidden_low, up_got, up_order[0])
    up_got = move(up_sent, up_order[0])
    up_sent, out_got = tie(up_sent, out_got)
    out_sent, out = second_share(attended, d_branch_low, out_got, up_order[0])
    out_got = move(out_sent, up_order[0])
    vectors = [
        jnp.sum(d_branch, axis=0), grad_gain_one, grad_shift_one, jnp.sum(d_second, axis=0), grad_gain_two,
        grad_shift_two,
    ]
    vectors = jnp.concatenate(
        [jnp.stack(vectors).reshape(6, fsdp, shard).transpose(1, 0, 2).reshape(fsdp, -1),
         jnp.sum(d_hidden, axis=0).reshape(fsdp, -1)], axis=1,
    )
    do_t, out_sent, down.terms[0], up.terms[0], out.terms[0], vectors = tie(
        do_t, out_sent, down.terms[0], up.terms[0], out.terms[0], vectors
    )

    delta = jnp.sum(
        attended_t.reshape(d, ctx, mine) * do_t.transpose(1, 0, 2).astype(F32), axis=0
    ).reshape(1, count)
    bq, bk = min(512, count), 512
    ranges = block_ranges(starts_all, ends_all, bk, bq * parts)
    calls = 8
    per_call = length // bk // calls
    dqt = jnp.zeros((d, count), F32)
    dkt, dvt = [], []
    todo = fsdp_steps + [("ctx", b) for b in bits(ctx)]

    def vector_step(vectors, step):
        axis, bit = step
        if axis == "ctx":
            return vectors + flip(vectors, "ctx", bit, ctx)
        pair = vectors.reshape(2, -1, vectors.shape[1])
        keep = lax.dynamic_index_in_dim(pair, own_bit(step), 0, keepdims=False)
        return keep + flip(lax.dynamic_index_in_dim(pair, 1 - own_bit(step), 0, keepdims=False), "fsdp", bit, fsdp)

    down_left, up_left = down_order[1:], up_order[1:]

    def down_step(got):
        down.receive(got)
        sent = down.send(down_left[0])
        return sent, move(sent, down_left.pop(0))

    def up_step(got):
        up.receive(got[..., :hidden])
        out.receive(got[..., hidden:])
        step = up_left.pop(0)
        sent = jnp.concatenate([up.send(step), out.send(step)], axis=-1)
        return sent, move(sent, step)

    for call in range(calls):
        dk_new, dv_new, dqt = attention_backward(
            q, k, v, do_t, lse, delta, starts, ends, ranges, dqt, scale, bq, bk, call * per_call, per_call
        )
        dkt.append(dk_new)
        dvt.append(dv_new)
        if call == 2:
            dqt, down_got = tie(dqt, down_got)
            down_sent, down_got = down_step(down_got)
            dqt, down_sent = tie(dqt, down_sent)
        if call == 6:
            dqt, up_got, out_got = tie(dqt, up_got, out_got)
            up_sent, up_got = up_step(jnp.concatenate([up_got, out_got], axis=-1))
            dqt, up_sent = tie(dqt, up_sent)
        if todo and call in (1, 3, 4, 5, 6):
            vectors = vector_step(vectors, todo.pop(0))
            dqt, vectors = tie(dqt, vectors)

    down_got, dqt = tie(down_got, dqt)
    down_sent, down_got = down_step(down_got)
    dqt, down_sent = tie(dqt, down_sent)
    dkt, dvt = jnp.concatenate(dkt, axis=1), jnp.concatenate(dvt, axis=1)
    dqt = (dqt * scale).astype(BF)
    if parts == 1:
        dqkv_t = jnp.concatenate([dqt, dkt, dvt], axis=0)
        outgoing = dqkv_t.reshape(3 * d, ctx, block).transpose(1, 0, 2)
        incoming = lax.all_to_all(outgoing, "ctx", 0, 0, tiled=True)
        outgoing, dqkv_t = tie(outgoing, dqkv_t)
        grad_head = dot(dqkv_t, everyone, 1, 0)
        sums = jnp.sum(dqkv_t.astype(F32), axis=1)
    else:
        back = lambda a: lax.all_to_all(
            a.reshape(d, ctx, -1).transpose(1, 0, 2), "ctx", 0, 0, tiled=True
        ).reshape(heads, parts, d, -1)
        summed = lambda a: jnp.sum(back(a).astype(F32), axis=1).astype(BF)
        incoming = jnp.stack([back(dqt).transpose(0, 2, 1, 3).reshape(heads, d, block), summed(dkt), summed(dvt)], axis=1)
        grad_head = jnp.concatenate([dot(dqt, own_part(everyone), 1, 0), dot(dkt, everyone, 1, 0), dot(dvt, everyone, 1, 0)])
        sums = jnp.concatenate([jnp.sum(a.astype(F32), axis=1) for a in (dqt, dkt, dvt)])
    grad_head = grad_head.reshape(3 * d, fsdp, shard).transpose(1, 0, 2)
    extra = jnp.pad(sums[None, None], ((0, 0), (0, 15), (0, shard - 3 * d))) if shard >= 3 * d else jnp.pad(
        sums.reshape(1, -1, shard // 2), ((0, 0), (0, 16 - 6 * d // shard), (0, shard // 2))
    )
    grad_head = jnp.concatenate([grad_head, jnp.broadcast_to(extra, (fsdp, 16, shard))], axis=1)
    for step in fsdp_steps:
        pair = grad_head.reshape(2, -1, 3 * d + 16, shard)
        sent = lax.dynamic_index_in_dim(pair, 1 - own_bit(step), 0, keepdims=False).astype(BF)
        kept = lax.dynamic_index_in_dim(pair, own_bit(step), 0, keepdims=False)
        grad_head = kept + move(sent, step).astype(F32)
    grad_head = grad_head[0].astype(BF)

    down_got, grad_head = tie(down_got, grad_head)
    down_sent, down_got = down_step(down_got)
    up_got, down_sent = tie(up_got, down_sent)
    up_sent, up_got = up_step(up_got)
    incoming, up_sent = tie(incoming, up_sent)
    while down_left:
        down_sent, down_got = down_step(down_got)
    token_grad = d_branch + dot(incoming.reshape(3 * width, block), wqkv_all, 0, 1)
    token_grad, down_got, up_got = tie(token_grad, down_got, up_got)
    down.receive(down_got)
    down_block = down.total(down.terms)
    while up_left:
        up_sent, up_got = up_step(up_got)
    up.receive(up_got[..., :hidden])
    out.receive(up_got[..., hidden:])
    for step in todo:
        vectors = vector_step(vectors, step)
    six = vectors[0, : 6 * shard].reshape(6, shard)
    grad_b_up = vectors[0, 6 * shard :]

    up_block = up.total(up.terms)
    rows_up, rows_down = up_block.shape[0], down_block.shape[0]
    wide = hidden // width
    rows_head = (3 * d + 16) * shard // width
    per_row = width // shard
    pieces = [down_block] + [up_block[:, i * width : (i + 1) * width] for i in range(wide)] + [out.total(out.terms)]
    split = grad_head.reshape(per_row, -1, shard)
    pieces.append(jnp.concatenate([split[i] for i in range(per_row)], axis=1))
    every = lax.all_gather(jnp.concatenate(pieces, axis=0), "ctx", axis=0, tiled=False)
    grad_w_down = in_order(every[:, :rows_down]).astype(F32)
    take = lambda i: in_order(every[:, rows_down + i * rows_up : rows_down + (i + 1) * rows_up]).astype(F32)
    grad_w_up = jnp.concatenate([take(i) for i in range(wide)], axis=1)
    grad_w_out = take(wide)
    every_head = every[:, rows_down + (wide + 1) * rows_up :]
    every_head = jnp.concatenate([every_head[:, :, i * shard : (i + 1) * shard] for i in range(per_row)], axis=1)
    every_head = every_head.astype(F32).reshape(heads, parts, 3 * d + 16, shard).sum(axis=1)
    grad_qkv = every_head[:, : 3 * d].reshape(heads, 3, d, shard).transpose(1, 3, 0, 2).reshape(3, shard, width)
    sums = every_head[:, 3 * d :]
    if shard >= 3 * d:
        sums = sums[:, 0, : 3 * d]
    else:
        sums = sums[:, : 6 * d // shard, : shard // 2]
    sums = sums.reshape(heads, 3, d).transpose(1, 0, 2).reshape(3, width)
    bias_q = cut(sums[0], row * shard, shard, 0)
    bias_v = cut(sums[2], row * shard, shard, 0)

    return (
        output[None].astype(BF),
        token_grad[None].astype(BF),
        grad_qkv[0],
        grad_qkv[1],
        grad_qkv[2],
        grad_w_out,
        bias_q,
        bias_v,
        six[0],
        six[1],
        six[2],
        grad_w_up,
        grad_b_up,
        grad_w_down,
        six[3],
        six[4],
        six[5],
    )


def solution(mesh):
    line, matrix, rows = P("fsdp"), P("fsdp", None), P("fsdp", "ctx", None)
    placed = (
        (rows, matrix) + (matrix,) * 4 + (line,) * 5 + (matrix, line, matrix) + (line,) * 3 + (rows,)
    )
    outs = (rows, rows) + (matrix,) * 4 + (line,) * 5 + (matrix, line, matrix) + (line,) * 3
    return jax.shard_map(
        functools.partial(body, mesh.shape["ctx"], mesh.shape["fsdp"]),
        mesh=mesh,
        in_specs=placed,
        out_specs=outs,
        check_vma=False,
    )
```

```python
import functools
import math

import jax
import jax.numpy as jnp
from jax import lax
from jax.experimental import pallas as pl
from jax.experimental.pallas import tpu as pltpu
from jax.sharding import PartitionSpec as P

HEADS = 16
LOG2E = 1.4426950408889634
NEG = -1e30
BF = jnp.bfloat16
F32 = jnp.float32


def layer_norm(hidden, gain, shift):
    mean = jnp.mean(hidden, axis=-1, keepdims=True)
    centred = hidden - mean
    variance = jnp.mean(centred * centred, axis=-1, keepdims=True)
    return centred * lax.rsqrt(variance + 1e-05) * gain + shift


def gelu_exact(value):
    return jax.nn.gelu(value, approximate=False)


def dot(left, right, on_left, on_right):
    return lax.dot_general(
        left, right, (((on_left,), (on_right,)), ((), ())), preferred_element_type=F32
    )


def flip(value, axis, bit, size):
    return lax.ppermute(value, axis, [(i, i ^ bit) for i in range(size)])


def forward_kernel(
    lo_ref, hi_ref, in_lo_ref, in_hi_ref, q_ref, k_ref, v_ref, start_ref, end_ref,
    out_ref, low_ref, lse_ref, total_ref, vt_ref, *, bk, scale
):
    i = pl.program_id(0)
    bq = q_ref.shape[0]

    @pl.when(i == 0)
    def _():
        @pl.loop(0, v_ref.shape[0] // bk)
        def _(j):
            at = pl.multiple_of(j * bk, bk)
            vt_ref[:, pl.ds(at, bk)] = v_ref[pl.ds(at, bk), :].T

    q = q_ref[...]
    start, end = start_ref[...], end_ref[...]
    total_ref[...] = jnp.zeros_like(total_ref)

    def step(j, carry, masked):
        peak, norm = carry
        at = pl.multiple_of(j * bk, bk)
        s = dot(k_ref[pl.ds(at, bk), :], q, 1, 1) * (scale * LOG2E)
        if masked:
            at_key = lax.broadcasted_iota(jnp.int32, (bk, bq), 0) + at
            s = jnp.where((at_key >= start) & (at_key < end), s, NEG)
        new_peak = jnp.maximum(peak, jnp.max(s, axis=0, keepdims=True))
        p = jnp.exp2(s - new_peak)
        shrink = jnp.exp2(peak - new_peak)
        norm = norm * shrink + jnp.sum(p, axis=0, keepdims=True)
        total_ref[...] = total_ref[...] * shrink + dot(vt_ref[:, pl.ds(at, bk)], p.astype(BF), 1, 0)
        return new_peak, norm

    lo, hi, in_lo, in_hi = lo_ref[i], hi_ref[i], in_lo_ref[i], in_hi_ref[i]
    carry = (jnp.full((1, bq), NEG, F32), jnp.zeros((1, bq), F32))
    carry = lax.fori_loop(in_lo, in_hi, lambda j, c: step(j, c, False), carry)
    carry = lax.fori_loop(lo, in_lo, lambda j, c: step(j, c, True), carry)
    peak, norm = lax.fori_loop(in_hi, hi, lambda j, c: step(j, c, True), carry)
    out = total_ref[...] / norm
    out_ref[...] = out
    n = low_ref.shape[2]
    for piece in range(bq // n):
        low_ref[piece] = out[:, piece * n : (piece + 1) * n].astype(low_ref.dtype)
    lse_ref[...] = peak + jnp.log2(norm)


def block_ranges(starts, ends, rows, others):
    first, last = starts.reshape(-1, rows), ends.reshape(-1, rows)
    lo = first[:, 0] // others
    hi = (last[:, -1] + others - 1) // others
    in_lo = jnp.clip((first[:, -1] + others - 1) // others, lo, hi)
    in_hi = jnp.clip(last[:, 0] // others, in_lo, hi)
    return lo, hi, in_lo, in_hi


def attention_forward(q, k, v, starts, ends, scale, n, bq=1024, bk=512):
    count, d = q.shape
    length = k.shape[0]
    bq = min(bq, count)
    ranges = block_ranges(starts, ends, bq, bk)
    row = lambda: pl.BlockSpec((1, bq), lambda i, *_: (0, i))
    whole = lambda shape: pl.BlockSpec(shape, lambda i, *_: (0, 0))
    return pl.pallas_call(
        functools.partial(forward_kernel, bk=bk, scale=scale),
        out_shape=(
            jax.ShapeDtypeStruct((d, count), F32),
            jax.ShapeDtypeStruct((count // n, d, n), BF),
            jax.ShapeDtypeStruct((1, count), F32),
        ),
        grid_spec=pltpu.PrefetchScalarGridSpec(
            num_scalar_prefetch=4,
            grid=(count // bq,),
            in_specs=[
                pl.BlockSpec((bq, d), lambda i, *_: (i, 0)),
                whole((length, d)),
                whole((length, d)),
                row(),
                row(),
            ],
            out_specs=[
                pl.BlockSpec((d, bq), lambda i, *_: (0, i)),
                pl.BlockSpec((bq // n, d, n), lambda i, *_: (i, 0, 0)),
                row(),
            ],
            scratch_shapes=[pltpu.VMEM((d, bq), F32), pltpu.VMEM((d, length), BF)],
        ),
        compiler_params=pltpu.CompilerParams(vmem_limit_bytes=40 << 20),
        cost_estimate=pl.CostEstimate(
            flops=16 * count * length * d, bytes_accessed=length * d * 16, transcendentals=count * length
        ),
        name="attention_forward",
    )(*ranges, q, k, v, starts[None], ends[None])


def backward_kernel(
    lo_ref, hi_ref, in_lo_ref, in_hi_ref, k_ref, v_ref, q_ref, do_ref, lse_ref, delta_ref, start_ref,
    end_ref, dqt_in_ref, dkt_ref, dvt_ref, dqt_ref, dk_sum, dv_sum, *, bq, scale, base
):
    j = pl.program_id(0) + base
    bk = k_ref.shape[0]
    pieces = bq // do_ref.shape[2]

    @pl.when(pl.program_id(0) == 0)
    def _():
        dqt_ref[...] = dqt_in_ref[...]

    k, v = k_ref[...], v_ref[...]
    kt = k.T
    dk_sum[...] = jnp.zeros_like(dk_sum)
    dv_sum[...] = jnp.zeros_like(dv_sum)

    def step(i, masked):
        at = pl.multiple_of(i * bq, bq)
        row = pl.ds(at, bq)
        q = q_ref[row, :]
        do_t = jnp.concatenate([do_ref[i * pieces + n] for n in range(pieces)], axis=1)
        s = dot(k, q, 1, 1) * (scale * LOG2E) - lse_ref[:, row]
        if masked:
            at_key = lax.broadcasted_iota(jnp.int32, (bk, bq), 0) + j * bk
            s = jnp.where((at_key >= start_ref[:, row]) & (at_key < end_ref[:, row]), s, NEG)
        p = jnp.exp2(s)
        dp = dot(v, do_t, 1, 0)
        dv_sum[...] += dot(p.astype(BF), do_t, 1, 1)
        ds = (p * (dp - delta_ref[:, row])).astype(BF)
        dk_sum[...] += dot(ds, q, 1, 0)
        dqt_ref[:, row] += dot(kt, ds, 1, 0)

    lo, hi, in_lo, in_hi = lo_ref[j], hi_ref[j], in_lo_ref[j], in_hi_ref[j]
    pl.loop(in_lo, in_hi)(lambda i: step(i, False))
    pl.loop(lo, in_lo)(lambda i: step(i, True))
    pl.loop(in_hi, hi)(lambda i: step(i, True))
    dkt_ref[...] = (dk_sum[...] * scale).T.astype(dkt_ref.dtype)
    dvt_ref[...] = dv_sum[...].T.astype(dvt_ref.dtype)


def attention_backward(q, k, v, do_t, lse, delta, starts, ends, ranges, dqt, scale, bq, bk, base, blocks):
    count, d = q.shape
    whole = lambda shape: pl.BlockSpec(shape, lambda j, *_: (0,) * len(shape))
    keys = lambda: pl.BlockSpec((bk, d), lambda j, *_: (j + base, 0))
    columns = lambda: pl.BlockSpec((d, bk), lambda j, *_: (0, j))
    return pl.pallas_call(
        functools.partial(backward_kernel, bq=bq, scale=scale, base=base),
        out_shape=(
            jax.ShapeDtypeStruct((d, blocks * bk), BF),
            jax.ShapeDtypeStruct((d, blocks * bk), BF),
            jax.ShapeDtypeStruct((d, count), F32),
        ),
        grid_spec=pltpu.PrefetchScalarGridSpec(
            num_scalar_prefetch=4,
            grid=(blocks,),
            in_specs=[
                keys(),
                keys(),
                whole((count, d)),
                whole(do_t.shape),
                whole((1, count)),
                whole((1, count)),
                whole((1, count)),
                whole((1, count)),
                whole((d, count)),
            ],
            out_specs=[columns(), columns(), whole((d, count))],
            scratch_shapes=[pltpu.VMEM((bk, d), F32), pltpu.VMEM((bk, d), F32)],
        ),
        compiler_params=pltpu.CompilerParams(vmem_limit_bytes=32 << 20),
        cost_estimate=pl.CostEstimate(
            flops=40 * count * blocks * bk * d, bytes_accessed=count * d * 24, transcendentals=count * blocks * bk
        ),
        name="attention_backward",
    )(*ranges, k, v, q, do_t, lse, delta, starts[None], ends[None], dqt)


class Halving:
    def __init__(self, place, sizes):
        self.place, self.sizes, self.terms = list(place), sizes, []

    def own(self, step):
        return (lax.axis_index(step[0]) // step[1]) % 2

    def share(self, step, which):
        at = self.place.index(step)
        return [lax.dynamic_index_in_dim(t, which, at, keepdims=False) for t in self.terms]

    def total(self, terms):
        return sum((t.astype(F32) for t in terms[1:]), terms[0].astype(F32)).astype(BF)

    def send(self, step):
        sent = self.total(self.share(step, 1 - self.own(step)))
        self.terms = self.share(step, self.own(step))
        self.place.remove(step)
        return sent

    def receive(self, got):
        self.terms.append(got)


def reversed_bits(i, count):
    n = count.bit_length() - 1
    return sum(((i // (1 << b)) % 2) * (1 << (n - 1 - b)) for b in range(n))


def down_kernel(every_ref, out_ref):
    for half in range(2):
        out_ref[half, 0] = every_ref[half].astype(F32)


def down_in_order(every):
    n, rows, columns = every.shape
    out = pl.pallas_call(
        down_kernel,
        out_shape=jax.ShapeDtypeStruct((2, n // 2, rows, columns), F32),
        grid=(n // 2,),
        in_specs=[pl.BlockSpec((2, rows, columns), lambda i: (i, 0, 0))],
        out_specs=pl.BlockSpec((2, 1, rows, columns), lambda i: (0, reversed_bits(i, n // 2), 0, 0)),
        compiler_params=pltpu.CompilerParams(vmem_limit_bytes=32 << 20),
        cost_estimate=pl.CostEstimate(flops=0, bytes_accessed=6 * every.size, transcendentals=0),
        name="down_in_order",
    )(every)
    return out.reshape(n * rows, columns)


def rest_kernel(every_ref, up_ref, out_ref, qkv_ref, *, rows, wide, d, shard):
    width = out_ref.shape[3]
    at = (wide + 1) * rows
    halves = []
    for half in range(2):
        for i in range(wide):
            up_ref[half, 0, :, i * width : (i + 1) * width] = every_ref[half, i * rows : (i + 1) * rows, :].astype(F32)
        out_ref[half, 0] = every_ref[half, wide * rows : at, :].astype(F32)
        both = every_ref[half, at:, :].astype(F32)
        halves.append(jnp.concatenate([both[:, :shard], both[:, shard:]], axis=0))
    for t in range(3):
        pair = jnp.concatenate([h[t * d : (t + 1) * d] for h in halves], axis=0)
        qkv_ref[t] = pair.T


def rest_in_order(every, rows, wide, d, shard):
    n, whole, width = every.shape
    place = lambda i: (0, reversed_bits(i, n // 2), 0, 0)
    up, out, qkv = pl.pallas_call(
        functools.partial(rest_kernel, rows=rows, wide=wide, d=d, shard=shard),
        out_shape=(
            jax.ShapeDtypeStruct((2, n // 2, rows, wide * width), F32),
            jax.ShapeDtypeStruct((2, n // 2, rows, width), F32),
            jax.ShapeDtypeStruct((3, shard, n * d), F32),
        ),
        grid=(n // 2,),
        in_specs=[pl.BlockSpec((2, whole, width), lambda i: (i, 0, 0))],
        out_specs=[
            pl.BlockSpec((2, 1, rows, wide * width), place),
            pl.BlockSpec((2, 1, rows, width), place),
            pl.BlockSpec((3, shard, 2 * d), lambda i: (0, 0, i)),
        ],
        compiler_params=pltpu.CompilerParams(vmem_limit_bytes=32 << 20),
        cost_estimate=pl.CostEstimate(flops=0, bytes_accessed=6 * every.size, transcendentals=0),
        name="rest_in_order",
    )(every)
    return up.reshape(n * rows, wide * width), out.reshape(n * rows, width), qkv


def body(ctx, fsdp, tokens, segments, w_query, w_key, w_value, w_out, b_query, b_value, b_out, gain_one, shift_one,
         w_up, b_up, w_down, b_down, gain_two, shift_two, cotangent):
    _, block, width = tokens.shape
    heads = HEADS
    d = width // heads
    scale = 1.0 / math.sqrt(d)
    parts = ctx // heads
    mine = block // parts
    length = ctx * block
    count = length // parts
    hidden = w_up.shape[1]
    shard = w_query.shape[0]
    me = lax.axis_index("ctx")
    row = lax.axis_index("fsdp")
    head, part = me // parts, me % parts
    core = me % 2
    cut = lambda a, at, size, axis: lax.dynamic_slice_in_dim(a, at, size, axis)

    bits = lambda n: [1 << i for i in range(n.bit_length() - 1)]
    sizes = {"fsdp": fsdp, "ctx": ctx}
    tie = lambda *arrays: lax.optimization_barrier(arrays)

    def gather_small(a):
        if fsdp == 2:
            other = flip(a, "fsdp", 1, 2)
            return jnp.concatenate([jnp.where(row == 0, a, other), jnp.where(row == 0, other, a)], axis=0)
        return lax.all_gather(a, "fsdp", axis=0, tiled=True)

    def near_half(w):
        if fsdp != 2:
            return lax.all_gather(w, "fsdp", axis=0, tiled=True)
        return flip(cut(w, core * (w.shape[0] // 2), w.shape[0] // 2, 0), "fsdp", 1, 2)

    def far_half(near):
        return flip(near, "ctx", 1, ctx) if fsdp == 2 else near

    def assemble(w, near, far):
        if fsdp != 2:
            return near
        rows, half = w.shape[0], w.shape[0] // 2
        whole = jnp.zeros((2 * rows, w.shape[1]), w.dtype)
        whole = lax.dynamic_update_slice_in_dim(whole, w, row * rows, 0)
        whole = lax.dynamic_update_slice_in_dim(whole, near, (1 - row) * rows + core * half, 0)
        return lax.dynamic_update_slice_in_dim(whole, far, (1 - row) * rows + (1 - core) * half, 0)

    def move(send, step):
        return flip(send, step[0], step[1], sizes[step[0]])

    core_step = ("ctx", 1)
    every_place = [("fsdp", b) for b in reversed(bits(fsdp))] + [("ctx", b) for b in bits(ctx)]
    own_bit = lambda step: (lax.axis_index(step[0]) // step[1]) % 2

    def columns_of(left, chosen):
        depth = max(every_place.index(step) for step in chosen) + 1
        size = left.shape[1] >> depth
        offsets = [0]
        for level, step in enumerate(every_place[:depth]):
            stride = left.shape[1] >> (level + 1)
            options = [chosen[step]] if step in chosen else [0, 1]
            offsets = [at + which * stride for at in offsets for which in options]
        return jnp.concatenate([cut(left, at, size, 1) for at in offsets], axis=1)

    def blocks(rows_data, place):
        return rows_data.reshape([2] * len(place) + [-1, rows_data.shape[1]])

    def first_share(left, right):
        return dot(columns_of(left, {core_step: 1 - own_bit(core_step)}), right, 0, 0).astype(BF)

    def second_share(left, right, got, step):
        place = [p for p in every_place if p != core_step]
        got = blocks(got, place)
        inner = [p for p in place if p != step]
        parts_of = []
        for which in (1 - own_bit(step), own_bit(step)):
            rows_data = dot(columns_of(left, {core_step: own_bit(core_step), step: which}), right, 0, 0)
            added = lax.dynamic_index_in_dim(got, which, place.index(step), keepdims=False)
            parts_of.append((blocks(rows_data, inner) + added.astype(F32)).astype(BF))
        rest = Halving(inner, sizes)
        rest.terms = [parts_of[1]]
        return parts_of[0], rest

    def in_order(every):
        n = len(bits(ctx))
        shape = every.shape
        every = every.reshape((2,) * n + shape[1:]).transpose(list(reversed(range(n))) + [n, n + 1])
        return every.reshape(-1, shape[2])

    inputs = tokens[0]
    everyone = lax.all_gather(inputs, "ctx", axis=0, tiled=True)
    by_head = lambda w: w.reshape(shard, heads, 1, d)
    wqkv = jnp.concatenate([by_head(w) for w in (w_query, w_key, w_value)], axis=2).reshape(shard, 3 * width)
    small = jnp.stack([b_query, b_value, b_out, gain_one, shift_one, b_down, gain_two, shift_two])
    small = jnp.concatenate([small.reshape(-1), b_up])[None]
    w_head = gather_small(jnp.concatenate([cut(w, head * d, d, 1) for w in (w_query, w_key, w_value)], axis=1))
    small = gather_small(small)
    wo_near = near_half(w_out)
    wu_near = near_half(w_up)
    wo_near, w_head, small = tie(wo_near, w_head, small)
    wo = assemble(w_out, wo_near, far_half(wo_near))
    wu_near, w_down, wo = tie(wu_near, w_down, wo)
    wd_near = near_half(w_down)
    wu_far = far_half(wu_near)
    everyone, wu_near = tie(everyone, wu_near)

    eight = small[:, : 8 * shard].reshape(-1, 8, shard).transpose(1, 0, 2).reshape(8, width).astype(F32)
    bq_, bv_, bo, gain1, shift1, bd, gain2, shift2 = (eight[i] for i in range(8))
    bu = small[:, 8 * shard :].reshape(hidden).astype(F32)
    projected = dot(everyone, w_head, 1, 0)
    my_bias = jnp.concatenate([cut(bq_, head * d, d, 0), jnp.zeros((d,), F32), cut(bv_, head * d, d, 0)])
    projected = (projected + my_bias).astype(BF)
    own_part = lambda a: cut(a.reshape((ctx, block) + a.shape[1:]), part * mine, mine, 1).reshape(
        (count,) + a.shape[1:]
    )
    q = own_part(projected[:, :d])
    k, v = projected[:, d : 2 * d], projected[:, 2 * d :]
    seg = segments[0]
    starts_all = jnp.sum(seg[None, :] < seg[:, None], axis=1, dtype=jnp.int32)
    ends_all = jnp.sum(seg[None, :] <= seg[:, None], axis=1, dtype=jnp.int32)
    starts, ends = own_part(starts_all), own_part(ends_all)

    attended_t, outgoing, lse = attention_forward(q, k, v, starts, ends, scale, mine)
    incoming = lax.all_to_all(outgoing, "ctx", 0, 0, tiled=True)
    wu_far, outgoing, wu_near = tie(wu_far, outgoing, wu_near)
    wu = assemble(w_up, wu_near, wu_far)
    incoming, wu = tie(incoming, wu)
    attended = incoming.reshape(heads, parts, d, mine).transpose(1, 3, 0, 2).reshape(block, width)
    branch = dot(attended, wo, 1, 0) + bo
    first, first_pull = jax.vjp(layer_norm, inputs.astype(F32) + branch, gain1, shift1)
    first_low, wd_near = tie(first.astype(BF), wd_near)
    wd = assemble(w_down, wd_near, far_half(wd_near))
    hidden_pre = dot(first_low, wu, 1, 0) + bu
    active, active_pull = jax.vjp(gelu_exact, hidden_pre)
    active_low = active.astype(BF)
    second = dot(active_low, wd, 1, 0) + bd
    output, out_pull = jax.vjp(layer_norm, first + second, gain2, shift2)

    fsdp_steps = [("fsdp", b) for b in reversed(bits(fsdp))]
    ctx_steps = [("ctx", b) for b in bits(ctx) if b > 1]
    down_order = fsdp_steps + ctx_steps
    up_order = ctx_steps[1:2] + fsdp_steps + ctx_steps[:1] + ctx_steps[2:]
    d_second, grad_gain_two, grad_shift_two = out_pull(cotangent[0].astype(F32))
    d_second_low = d_second.astype(BF)
    down_sent = first_share(active_low, d_second_low)
    down_sent, d_second_low = tie(down_sent, d_second_low)
    down_got = move(down_sent, core_step)
    (d_hidden,) = active_pull(dot(d_second_low, wd, 1, 1))
    d_hidden_low = d_hidden.astype(BF)
    up_sent = first_share(first_low, d_hidden_low)
    up_sent, d_hidden_low, down_got = tie(up_sent, d_hidden_low, down_got)
    up_got = move(up_sent, core_step)
    down_sent, down = second_share(active_low, d_second_low, down_got, down_order[0])
    down_sent, d_hidden_low = tie(down_sent, d_hidden_low)
    down_got = move(down_sent, down_order[0])
    d_first = d_second + dot(d_hidden_low, wu, 1, 1)
    d_branch, grad_gain_one, grad_shift_one = first_pull(d_first)
    d_branch_low = d_branch.astype(BF)
    out_sent = first_share(attended, d_branch_low)
    d_attended_t = dot(wo, d_branch_low, 1, 1).astype(BF)
    outgoing = d_attended_t.reshape(heads, d, parts, mine).transpose(0, 2, 1, 3).reshape(ctx, d, mine)
    do_t = lax.all_to_all(outgoing, "ctx", 0, 0, tiled=True)

    outgoing, up_got, out_sent = tie(outgoing, up_got, out_sent)
    out_got = move(out_sent, core_step)
    up_sent, up = second_share(first_low, d_hidden_low, up_got, up_order[0])
    up_got = move(up_sent, up_order[0])
    up_sent, out_got = tie(up_sent, out_got)
    out_sent, out = second_share(attended, d_branch_low, out_got, up_order[0])
    out_got = move(out_sent, up_order[0])
    vectors = [
        jnp.sum(d_branch, axis=0), grad_gain_one, grad_shift_one, jnp.sum(d_second, axis=0), grad_gain_two,
        grad_shift_two,
    ]
    vectors = jnp.concatenate(
        [jnp.stack(vectors).reshape(6, fsdp, shard).transpose(1, 0, 2).reshape(fsdp, -1),
         jnp.sum(d_hidden, axis=0).reshape(fsdp, -1)], axis=1,
    )
    vectors = lax.all_gather(vectors, ("ctx", "fsdp"), axis=0, tiled=False)
    do_t, out_sent, down.terms[0], up.terms[0], out.terms[0] = tie(
        do_t, out_sent, down.terms[0], up.terms[0], out.terms[0]
    )

    delta = jnp.sum(
        attended_t.reshape(d, ctx, mine) * do_t.transpose(1, 0, 2).astype(F32), axis=0
    ).reshape(1, count)
    bq, bk = min(512, count), 512
    ranges = block_ranges(starts_all, ends_all, bk, bq * parts)
    calls = 4
    per_call = length // bk // calls
    dqt = jnp.zeros((d, count), F32)
    dkt, dvt = [], []
    down_left, up_left = down_order[1:], up_order[1:]

    def down_step(got):
        down.receive(got)
        sent = down.send(down_left[0])
        return sent, move(sent, down_left.pop(0))

    def up_step(got):
        up.receive(got[..., :hidden])
        out.receive(got[..., hidden:])
        step = up_left.pop(0)
        sent = jnp.concatenate([up.send(step), out.send(step)], axis=-1)
        return sent, move(sent, step)

    for call in range(calls):
        dk_new, dv_new, dqt = attention_backward(
            q, k, v, do_t, lse, delta, starts, ends, ranges, dqt, scale, bq, bk, call * per_call, per_call
        )
        dkt.append(dk_new)
        dvt.append(dv_new)
        if call == 2:
            dqt, down_got, vectors = tie(dqt, down_got, vectors)
            down_sent, down_got = down_step(down_got)
            dqt, down_sent = tie(dqt, down_sent)

    dkt, dvt = jnp.concatenate(dkt, axis=1), jnp.concatenate(dvt, axis=1)
    dqt = (dqt * scale).astype(BF)
    if parts == 1:
        dqkv_t = jnp.concatenate([dqt, dkt, dvt], axis=0)
        outgoing = dqkv_t.reshape(3 * d, ctx, block).transpose(1, 0, 2)
        incoming = lax.all_to_all(outgoing, "ctx", 0, 0, tiled=True)
        outgoing, dqkv_t, up_got, out_got = tie(outgoing, dqkv_t, up_got, out_got)
        up_sent, up_got = up_step(jnp.concatenate([up_got, out_got], axis=-1))
        down_got, up_sent = tie(down_got, up_sent)
        down_sent, down_got = down_step(down_got)
        dqkv_t, down_sent = tie(dqkv_t, down_sent)
        grad_head = dot(dqkv_t, everyone, 1, 0)
        sums = jnp.sum(dqkv_t.astype(F32), axis=1)
    else:
        dqt, up_got, out_got = tie(dqt, up_got, out_got)
        up_sent, up_got = up_step(jnp.concatenate([up_got, out_got], axis=-1))
        down_got, up_sent = tie(down_got, up_sent)
        down_sent, down_got = down_step(down_got)
        dqt, down_sent = tie(dqt, down_sent)
        back = lambda a: lax.all_to_all(
            a.reshape(d, ctx, -1).transpose(1, 0, 2), "ctx", 0, 0, tiled=True
        ).reshape(heads, parts, d, -1)
        summed = lambda a: jnp.sum(back(a).astype(F32), axis=1).astype(BF)
        incoming = jnp.stack([back(dqt).transpose(0, 2, 1, 3).reshape(heads, d, block), summed(dkt), summed(dvt)], axis=1)
        grad_head = jnp.concatenate([dot(dqt, own_part(everyone), 1, 0), dot(dkt, everyone, 1, 0), dot(dvt, everyone, 1, 0)])
        sums = jnp.concatenate([jnp.sum(a.astype(F32), axis=1) for a in (dqt, dkt, dvt)])
    grad_head = grad_head.reshape(3 * d, fsdp, shard).transpose(1, 0, 2)
    extra = jnp.pad(sums[None, None], ((0, 0), (0, 15), (0, shard - 3 * d))) if shard >= 3 * d else jnp.pad(
        sums.reshape(1, -1, shard // 2), ((0, 0), (0, 16 - 6 * d // shard), (0, shard // 2))
    )
    grad_head = jnp.concatenate([grad_head, jnp.broadcast_to(extra, (fsdp, 16, shard))], axis=1)
    first_sent = None
    for step in fsdp_steps:
        pair = grad_head.reshape(2, -1, 3 * d + 16, shard)
        sent = lax.dynamic_index_in_dim(pair, 1 - own_bit(step), 0, keepdims=False).astype(BF)
        kept = lax.dynamic_index_in_dim(pair, own_bit(step), 0, keepdims=False)
        if first_sent is None:
            down_got, sent = tie(down_got, sent)
            first_sent = sent
        grad_head = kept + move(sent, step).astype(F32)
    grad_head = grad_head[0].astype(BF)

    down_sent, down_got = down_step(down_got)
    up_got, down_sent = tie(up_got, down_sent)
    up_sent, up_got = up_step(up_got)
    down_got, up_sent, wqkv = tie(down_got, up_sent, wqkv)
    wqkv_near = near_half(wqkv)
    while down_left:
        down_sent, down_got = down_step(down_got)
    down.receive(down_got)
    down_block = down.total(down.terms)
    every_down = lax.all_gather(down_block, "ctx", axis=0, tiled=False)
    up_got, down_block, grad_head = tie(up_got, down_block, grad_head)
    while up_left:
        up_sent, up_got = up_step(up_got)
    up.receive(up_got[..., :hidden])
    out.receive(up_got[..., hidden:])
    vectors = jnp.sum(lax.dynamic_index_in_dim(vectors, row, 1, keepdims=False), axis=0)
    six = vectors[: 6 * shard].reshape(6, shard)
    grad_b_up = vectors[6 * shard :]

    up_block = up.total(up.terms)
    rows_up = up_block.shape[0]
    wide = hidden // width
    per_row = width // shard
    rows_head = (3 * d + 16) // per_row
    at_head = (wide + 1) * rows_up
    pieces = [up_block[:, i * width : (i + 1) * width] for i in range(wide)] + [out.total(out.terms)]
    split = grad_head.reshape(per_row, -1, shard)
    pieces.append(jnp.concatenate([split[i] for i in range(per_row)], axis=1))
    pieces = jnp.concatenate(pieces, axis=0)
    every = lax.all_gather(pieces, "ctx", axis=0, tiled=False)
    incoming, pieces, wqkv_near = tie(incoming, pieces, wqkv_near)
    wqkv_all = assemble(wqkv, wqkv_near, far_half(wqkv_near))
    token_grad = d_branch + dot(incoming.reshape(3 * width, block), wqkv_all, 0, 1)
    grad_w_down = down_in_order(every_down)
    if parts == 1 and per_row == 2 and shard >= 3 * d:
        grad_w_up, grad_w_out, grad_qkv = rest_in_order(every, rows_up, wide, d, shard)
        at = (3 * d) % rows_head
        sums = every[:, at_head + at, shard : shard + 3 * d].astype(F32)
    else:
        take = lambda i: in_order(every[:, i * rows_up : (i + 1) * rows_up]).astype(F32)
        grad_w_up = jnp.concatenate([take(i) for i in range(wide)], axis=1)
        grad_w_out = take(wide)
        every_head = every[:, at_head:]
        every_head = jnp.concatenate([every_head[:, :, i * shard : (i + 1) * shard] for i in range(per_row)], axis=1)
        every_head = every_head.astype(F32).reshape(heads, parts, 3 * d + 16, shard).sum(axis=1)
        grad_qkv = every_head[:, : 3 * d].reshape(heads, 3, d, shard).transpose(1, 3, 0, 2).reshape(3, shard, width)
        sums = every_head[:, 3 * d :]
        if shard >= 3 * d:
            sums = sums[:, 0, : 3 * d]
        else:
            sums = sums[:, : 6 * d // shard, : shard // 2]
    sums = sums.reshape(heads, 3, d).transpose(1, 0, 2).reshape(3, width)
    bias_q = cut(sums[0], row * shard, shard, 0)
    bias_v = cut(sums[2], row * shard, shard, 0)

    return (
        output[None].astype(BF),
        token_grad[None].astype(BF),
        grad_qkv[0],
        grad_qkv[1],
        grad_qkv[2],
        grad_w_out,
        bias_q,
        bias_v,
        six[0],
        six[1],
        six[2],
        grad_w_up,
        grad_b_up,
        grad_w_down,
        six[3],
        six[4],
        six[5],
    )


def solution(mesh):
    line, matrix, rows = P("fsdp"), P("fsdp", None), P("fsdp", "ctx", None)
    placed = (
        (rows, matrix) + (matrix,) * 4 + (line,) * 5 + (matrix, line, matrix) + (line,) * 3 + (rows,)
    )
    outs = (rows, rows) + (matrix,) * 4 + (line,) * 5 + (matrix, line, matrix) + (line,) * 3
    return jax.shard_map(
        functools.partial(body, mesh.shape["ctx"], mesh.shape["fsdp"]),
        mesh=mesh,
        in_specs=placed,
        out_specs=outs,
        check_vma=False,
    )
```

```python
import functools
import math

import jax
import jax.numpy as jnp
from jax import lax
from jax.experimental import pallas as pl
from jax.experimental.pallas import tpu as pltpu
from jax.sharding import PartitionSpec as P

HEADS = 16
LOG2E = 1.4426950408889634
NEG = -1e30
BF = jnp.bfloat16
F32 = jnp.float32


def layer_norm(hidden, gain, shift):
    mean = jnp.mean(hidden, axis=-1, keepdims=True)
    centred = hidden - mean
    variance = jnp.mean(centred * centred, axis=-1, keepdims=True)
    return centred * lax.rsqrt(variance + 1e-05) * gain + shift


def gelu_exact(value):
    return jax.nn.gelu(value, approximate=False)


def dot(left, right, on_left, on_right):
    return lax.dot_general(
        left, right, (((on_left,), (on_right,)), ((), ())), preferred_element_type=F32
    )


def flip(value, axis, bit, size):
    return lax.ppermute(value, axis, [(i, i ^ bit) for i in range(size)])


def forward_kernel(
    lo_ref, hi_ref, in_lo_ref, in_hi_ref, q_ref, k_ref, v_ref, start_ref, end_ref,
    out_ref, low_ref, lse_ref, total_ref, vt_ref, *, bk, scale
):
    i = pl.program_id(0)
    bq = q_ref.shape[0]

    @pl.when(i == 0)
    def _():
        @pl.loop(0, v_ref.shape[0] // bk)
        def _(j):
            at = pl.multiple_of(j * bk, bk)
            vt_ref[:, pl.ds(at, bk)] = v_ref[pl.ds(at, bk), :].T

    q = q_ref[...]
    start, end = start_ref[...], end_ref[...]
    total_ref[...] = jnp.zeros_like(total_ref)

    def step(j, carry, masked):
        peak, norm = carry
        at = pl.multiple_of(j * bk, bk)
        s = dot(k_ref[pl.ds(at, bk), :], q, 1, 1) * (scale * LOG2E)
        if masked:
            at_key = lax.broadcasted_iota(jnp.int32, (bk, bq), 0) + at
            s = jnp.where((at_key >= start) & (at_key < end), s, NEG)
        new_peak = jnp.maximum(peak, jnp.max(s, axis=0, keepdims=True))
        p = jnp.exp2(s - new_peak)
        shrink = jnp.exp2(peak - new_peak)
        norm = norm * shrink + jnp.sum(p, axis=0, keepdims=True)
        total_ref[...] = total_ref[...] * shrink + dot(vt_ref[:, pl.ds(at, bk)], p.astype(BF), 1, 0)
        return new_peak, norm

    lo, hi, in_lo, in_hi = lo_ref[i], hi_ref[i], in_lo_ref[i], in_hi_ref[i]
    carry = (jnp.full((1, bq), NEG, F32), jnp.zeros((1, bq), F32))
    carry = lax.fori_loop(in_lo, in_hi, lambda j, c: step(j, c, False), carry)
    carry = lax.fori_loop(lo, in_lo, lambda j, c: step(j, c, True), carry)
    peak, norm = lax.fori_loop(in_hi, hi, lambda j, c: step(j, c, True), carry)
    out = total_ref[...] / norm
    out_ref[...] = out
    n = low_ref.shape[2]
    for piece in range(bq // n):
        low_ref[piece] = out[:, piece * n : (piece + 1) * n].astype(low_ref.dtype)
    lse_ref[...] = peak + jnp.log2(norm)


def block_ranges(starts, ends, rows, others):
    first, last = starts.reshape(-1, rows), ends.reshape(-1, rows)
    lo = first[:, 0] // others
    hi = (last[:, -1] + others - 1) // others
    in_lo = jnp.clip((first[:, -1] + others - 1) // others, lo, hi)
    in_hi = jnp.clip(last[:, 0] // others, in_lo, hi)
    return lo, hi, in_lo, in_hi


def attention_forward(q, k, v, starts, ends, scale, n, bq=1024, bk=512):
    count, d = q.shape
    length = k.shape[0]
    bq = min(bq, count)
    ranges = block_ranges(starts, ends, bq, bk)
    row = lambda: pl.BlockSpec((1, bq), lambda i, *_: (0, i))
    whole = lambda shape: pl.BlockSpec(shape, lambda i, *_: (0, 0))
    return pl.pallas_call(
        functools.partial(forward_kernel, bk=bk, scale=scale),
        out_shape=(
            jax.ShapeDtypeStruct((d, count), F32),
            jax.ShapeDtypeStruct((count // n, d, n), BF),
            jax.ShapeDtypeStruct((1, count), F32),
        ),
        grid_spec=pltpu.PrefetchScalarGridSpec(
            num_scalar_prefetch=4,
            grid=(count // bq,),
            in_specs=[
                pl.BlockSpec((bq, d), lambda i, *_: (i, 0)),
                whole((length, d)),
                whole((length, d)),
                row(),
                row(),
            ],
            out_specs=[
                pl.BlockSpec((d, bq), lambda i, *_: (0, i)),
                pl.BlockSpec((bq // n, d, n), lambda i, *_: (i, 0, 0)),
                row(),
            ],
            scratch_shapes=[pltpu.VMEM((d, bq), F32), pltpu.VMEM((d, length), BF)],
        ),
        compiler_params=pltpu.CompilerParams(vmem_limit_bytes=40 << 20),
        cost_estimate=pl.CostEstimate(
            flops=16 * count * length * d, bytes_accessed=length * d * 16, transcendentals=count * length
        ),
        name="attention_forward",
    )(*ranges, q, k, v, starts[None], ends[None])


def backward_kernel(
    lo_ref, hi_ref, in_lo_ref, in_hi_ref, k_ref, v_ref, q_ref, do_ref, lse_ref, delta_ref, start_ref,
    end_ref, dqt_in_ref, dkt_ref, dvt_ref, dqt_ref, dk_sum, dv_sum, *, bq, scale, base
):
    j = pl.program_id(0) + base
    bk = k_ref.shape[0]
    pieces = bq // do_ref.shape[2]

    @pl.when(pl.program_id(0) == 0)
    def _():
        dqt_ref[...] = dqt_in_ref[...]

    k, v = k_ref[...], v_ref[...]
    kt = k.T
    dk_sum[...] = jnp.zeros_like(dk_sum)
    dv_sum[...] = jnp.zeros_like(dv_sum)

    def step(i, masked):
        at = pl.multiple_of(i * bq, bq)
        row = pl.ds(at, bq)
        q = q_ref[row, :]
        do_t = jnp.concatenate([do_ref[i * pieces + n] for n in range(pieces)], axis=1)
        s = dot(k, q, 1, 1) * (scale * LOG2E) - lse_ref[:, row]
        if masked:
            at_key = lax.broadcasted_iota(jnp.int32, (bk, bq), 0) + j * bk
            s = jnp.where((at_key >= start_ref[:, row]) & (at_key < end_ref[:, row]), s, NEG)
        p = jnp.exp2(s)
        dp = dot(v, do_t, 1, 0)
        dv_sum[...] += dot(p.astype(BF), do_t, 1, 1)
        ds = (p * (dp - delta_ref[:, row])).astype(BF)
        dk_sum[...] += dot(ds, q, 1, 0)
        dqt_ref[:, row] += dot(kt, ds, 1, 0)

    lo, hi, in_lo, in_hi = lo_ref[j], hi_ref[j], in_lo_ref[j], in_hi_ref[j]
    pl.loop(in_lo, in_hi)(lambda i: step(i, False))
    pl.loop(lo, in_lo)(lambda i: step(i, True))
    pl.loop(in_hi, hi)(lambda i: step(i, True))
    dkt_ref[...] = (dk_sum[...] * scale).T.astype(dkt_ref.dtype)
    dvt_ref[...] = dv_sum[...].T.astype(dvt_ref.dtype)


def attention_backward(q, k, v, do_t, lse, delta, starts, ends, ranges, dqt, scale, bq, bk, base, blocks):
    count, d = q.shape
    whole = lambda shape: pl.BlockSpec(shape, lambda j, *_: (0,) * len(shape))
    keys = lambda: pl.BlockSpec((bk, d), lambda j, *_: (j + base, 0))
    columns = lambda: pl.BlockSpec((d, bk), lambda j, *_: (0, j))
    return pl.pallas_call(
        functools.partial(backward_kernel, bq=bq, scale=scale, base=base),
        out_shape=(
            jax.ShapeDtypeStruct((d, blocks * bk), BF),
            jax.ShapeDtypeStruct((d, blocks * bk), BF),
            jax.ShapeDtypeStruct((d, count), F32),
        ),
        grid_spec=pltpu.PrefetchScalarGridSpec(
            num_scalar_prefetch=4,
            grid=(blocks,),
            in_specs=[
                keys(),
                keys(),
                whole((count, d)),
                whole(do_t.shape),
                whole((1, count)),
                whole((1, count)),
                whole((1, count)),
                whole((1, count)),
                whole((d, count)),
            ],
            out_specs=[columns(), columns(), whole((d, count))],
            scratch_shapes=[pltpu.VMEM((bk, d), F32), pltpu.VMEM((bk, d), F32)],
        ),
        compiler_params=pltpu.CompilerParams(vmem_limit_bytes=32 << 20),
        cost_estimate=pl.CostEstimate(
            flops=count * d, bytes_accessed=count * d, transcendentals=0
        ),
        name="attention_backward",
    )(*ranges, k, v, q, do_t, lse, delta, starts[None], ends[None], dqt)


class Halving:
    def __init__(self, place, sizes):
        self.place, self.sizes, self.terms = list(place), sizes, []

    def own(self, step):
        return (lax.axis_index(step[0]) // step[1]) % 2

    def share(self, step, which):
        at = self.place.index(step)
        return [lax.dynamic_index_in_dim(t, which, at, keepdims=False) for t in self.terms]

    def total(self, terms):
        return sum((t.astype(F32) for t in terms[1:]), terms[0].astype(F32)).astype(BF)

    def send(self, step):
        sent = self.total(self.share(step, 1 - self.own(step)))
        self.terms = self.share(step, self.own(step))
        self.place.remove(step)
        return sent

    def receive(self, got):
        self.terms.append(got)


def reversed_bits(i, count):
    n = count.bit_length() - 1
    return sum(((i // (1 << b)) % 2) * (1 << (n - 1 - b)) for b in range(n))


def order_kernel(every_ref, down_ref, up_ref, out_ref, qkv_ref, *, rows, wide, d, shard):
    rows_down, width = down_ref.shape[2:]
    starts = [rows_down + i * rows for i in range(wide + 2)]
    halves = []
    for half in range(2):
        down_ref[half, 0] = every_ref[half, :rows_down, :].astype(F32)
        for i in range(wide):
            slab = every_ref[half, starts[i] : starts[i + 1], :]
            up_ref[half, 0, :, i * width : (i + 1) * width] = slab.astype(F32)
        out_ref[half, 0] = every_ref[half, starts[wide] : starts[wide + 1], :].astype(F32)
        both = every_ref[half, starts[wide + 1] :, :].astype(F32)
        halves.append(jnp.concatenate([both[:, :shard], both[:, shard:]], axis=0))
    for t in range(3):
        pair = jnp.concatenate([h[t * d : (t + 1) * d] for h in halves], axis=0)
        qkv_ref[t] = pair.T


def in_order(every, rows_down, rows, wide, d, shard):
    n, whole, width = every.shape
    place = lambda i: (0, reversed_bits(i, n // 2), 0, 0)
    down, up, out, qkv = pl.pallas_call(
        functools.partial(order_kernel, rows=rows, wide=wide, d=d, shard=shard),
        out_shape=(
            jax.ShapeDtypeStruct((2, n // 2, rows_down, width), F32),
            jax.ShapeDtypeStruct((2, n // 2, rows, wide * width), F32),
            jax.ShapeDtypeStruct((2, n // 2, rows, width), F32),
            jax.ShapeDtypeStruct((3, shard, n * d), F32),
        ),
        grid=(n // 2,),
        in_specs=[pl.BlockSpec((2, whole, width), lambda i: (i, 0, 0))],
        out_specs=[
            pl.BlockSpec((2, 1, rows_down, width), place),
            pl.BlockSpec((2, 1, rows, wide * width), place),
            pl.BlockSpec((2, 1, rows, width), place),
            pl.BlockSpec((3, shard, 2 * d), lambda i: (0, 0, i)),
        ],
        compiler_params=pltpu.CompilerParams(vmem_limit_bytes=32 << 20),
        cost_estimate=pl.CostEstimate(flops=0, bytes_accessed=6 * every.size, transcendentals=0),
        name="in_order",
    )(every)
    return down.reshape(n * rows_down, width), up.reshape(n * rows, wide * width), out.reshape(n * rows, width), qkv


def body(ctx, fsdp, tokens, segments, w_query, w_key, w_value, w_out, b_query, b_value, b_out, gain_one, shift_one,
         w_up, b_up, w_down, b_down, gain_two, shift_two, cotangent):
    _, block, width = tokens.shape
    heads = HEADS
    d = width // heads
    scale = 1.0 / math.sqrt(d)
    parts = ctx // heads
    mine = block // parts
    length = ctx * block
    count = length // parts
    hidden = w_up.shape[1]
    shard = w_query.shape[0]
    me = lax.axis_index("ctx")
    row = lax.axis_index("fsdp")
    head, part = me // parts, me % parts
    core = me % 2
    cut = lambda a, at, size, axis: lax.dynamic_slice_in_dim(a, at, size, axis)

    bits = lambda n: [1 << i for i in range(n.bit_length() - 1)]
    sizes = {"fsdp": fsdp, "ctx": ctx}
    tie = lambda *arrays: lax.optimization_barrier(arrays)

    def gather_small(a):
        if fsdp == 2:
            other = flip(a, "fsdp", 1, 2)
            return jnp.concatenate([jnp.where(row == 0, a, other), jnp.where(row == 0, other, a)], axis=0)
        return lax.all_gather(a, "fsdp", axis=0, tiled=True)

    def near_half(w):
        if fsdp != 2:
            return lax.all_gather(w, "fsdp", axis=0, tiled=True)
        return flip(cut(w, core * (w.shape[0] // 2), w.shape[0] // 2, 0), "fsdp", 1, 2)

    def far_half(near):
        return flip(near, "ctx", 1, ctx) if fsdp == 2 else near

    def assemble(w, near, far):
        if fsdp != 2:
            return near
        rows, half = w.shape[0], w.shape[0] // 2
        whole = jnp.zeros((2 * rows, w.shape[1]), w.dtype)
        whole = lax.dynamic_update_slice_in_dim(whole, w, row * rows, 0)
        whole = lax.dynamic_update_slice_in_dim(whole, near, (1 - row) * rows + core * half, 0)
        return lax.dynamic_update_slice_in_dim(whole, far, (1 - row) * rows + (1 - core) * half, 0)

    def move(send, step):
        return flip(send, step[0], step[1], sizes[step[0]])

    core_step = ("ctx", 1)
    every_place = [("fsdp", b) for b in reversed(bits(fsdp))] + [("ctx", b) for b in bits(ctx)]
    own_bit = lambda step: (lax.axis_index(step[0]) // step[1]) % 2

    def columns_of(left, chosen):
        depth = max(every_place.index(step) for step in chosen) + 1
        size = left.shape[1] >> depth
        offsets = [0]
        for level, step in enumerate(every_place[:depth]):
            stride = left.shape[1] >> (level + 1)
            options = [chosen[step]] if step in chosen else [0, 1]
            offsets = [at + which * stride for at in offsets for which in options]
        return jnp.concatenate([cut(left, at, size, 1) for at in offsets], axis=1)

    def blocks(rows_data, place):
        return rows_data.reshape([2] * len(place) + [-1, rows_data.shape[1]])

    def first_share(left, right):
        return dot(columns_of(left, {core_step: 1 - own_bit(core_step)}), right, 0, 0).astype(BF)

    def second_share(left, right, got, step):
        place = [p for p in every_place if p != core_step]
        got = blocks(got, place)
        inner = [p for p in place if p != step]
        parts_of = []
        for which in (1 - own_bit(step), own_bit(step)):
            rows_data = dot(columns_of(left, {core_step: own_bit(core_step), step: which}), right, 0, 0)
            added = lax.dynamic_index_in_dim(got, which, place.index(step), keepdims=False)
            parts_of.append((blocks(rows_data, inner) + added.astype(F32)).astype(BF))
        rest = Halving(inner, sizes)
        rest.terms = [parts_of[1]]
        return parts_of[0], rest

    def sorted_rows(every):
        n = len(bits(ctx))
        shape = every.shape
        every = every.reshape((2,) * n + shape[1:]).transpose(list(reversed(range(n))) + [n, n + 1])
        return every.reshape(-1, shape[2])

    inputs = tokens[0]
    everyone = lax.all_gather(inputs, "ctx", axis=0, tiled=True)
    by_head = lambda w: w.reshape(shard, heads, 1, d)
    wqkv = jnp.concatenate([by_head(w) for w in (w_query, w_key, w_value)], axis=2).reshape(shard, 3 * width)
    small = jnp.stack([b_query, b_value, b_out, gain_one, shift_one, b_down, gain_two, shift_two])
    small = jnp.concatenate([small.reshape(-1), b_up])[None]
    w_head = gather_small(jnp.concatenate([cut(w, head * d, d, 1) for w in (w_query, w_key, w_value)], axis=1))
    small = gather_small(small)
    wo_near = near_half(w_out)
    wu_near = near_half(w_up)
    wo_near, w_head, small = tie(wo_near, w_head, small)
    wo = assemble(w_out, wo_near, far_half(wo_near))
    wu_near, w_down, wo = tie(wu_near, w_down, wo)
    wd_near = near_half(w_down)
    wu_far = far_half(wu_near)
    everyone, wu_near = tie(everyone, wu_near)

    eight = small[:, : 8 * shard].reshape(-1, 8, shard).transpose(1, 0, 2).reshape(8, width).astype(F32)
    bq_, bv_, bo, gain1, shift1, bd, gain2, shift2 = (eight[i] for i in range(8))
    bu = small[:, 8 * shard :].reshape(hidden).astype(F32)
    projected = dot(everyone, w_head, 1, 0)
    my_bias = jnp.concatenate([cut(bq_, head * d, d, 0), jnp.zeros((d,), F32), cut(bv_, head * d, d, 0)])
    projected = (projected + my_bias).astype(BF)
    own_part = lambda a: cut(a.reshape((ctx, block) + a.shape[1:]), part * mine, mine, 1).reshape(
        (count,) + a.shape[1:]
    )
    q = own_part(projected[:, :d])
    k, v = projected[:, d : 2 * d], projected[:, 2 * d :]
    seg = segments[0]
    starts_all = jnp.sum(seg[None, :] < seg[:, None], axis=1, dtype=jnp.int32)
    ends_all = jnp.sum(seg[None, :] <= seg[:, None], axis=1, dtype=jnp.int32)
    starts, ends = own_part(starts_all), own_part(ends_all)

    attended_t, outgoing, lse = attention_forward(q, k, v, starts, ends, scale, mine)
    incoming = lax.all_to_all(outgoing, "ctx", 0, 0, tiled=True)
    wu_far, outgoing, wu_near = tie(wu_far, outgoing, wu_near)
    wu = assemble(w_up, wu_near, wu_far)
    incoming, wu = tie(incoming, wu)
    attended = incoming.reshape(heads, parts, d, mine).transpose(1, 3, 0, 2).reshape(block, width)
    branch = dot(attended, wo, 1, 0) + bo
    first, first_pull = jax.vjp(layer_norm, inputs.astype(F32) + branch, gain1, shift1)
    first_low, wd_near = tie(first.astype(BF), wd_near)
    wd = assemble(w_down, wd_near, far_half(wd_near))
    hidden_pre = dot(first_low, wu, 1, 0) + bu
    active, active_pull = jax.vjp(gelu_exact, hidden_pre)
    (slope,) = active_pull(jnp.ones_like(active))
    active_low, slope = tie(active.astype(BF), slope)
    second = dot(active_low, wd, 1, 0) + bd
    output, out_pull = jax.vjp(layer_norm, first + second, gain2, shift2)

    fsdp_steps = [("fsdp", b) for b in reversed(bits(fsdp))]
    ctx_steps = [("ctx", b) for b in bits(ctx) if b > 1]
    down_order = fsdp_steps + ctx_steps
    up_order = ctx_steps[1:2] + fsdp_steps + ctx_steps[:1] + ctx_steps[2:]
    out_order = ctx_steps[:1] + fsdp_steps + ctx_steps[1:]
    d_second, grad_gain_two, grad_shift_two = out_pull(cotangent[0].astype(F32))
    d_second_low = d_second.astype(BF)
    down_sent = first_share(active_low, d_second_low)
    down_sent, d_second_low = tie(down_sent, d_second_low)
    down_got = move(down_sent, core_step)
    d_hidden = dot(d_second_low, wd, 1, 1) * slope
    d_hidden_low = d_hidden.astype(BF)
    up_sent = first_share(first_low, d_hidden_low)
    up_sent, d_hidden_low, down_got = tie(up_sent, d_hidden_low, down_got)
    up_got = move(up_sent, core_step)
    down_sent, down = second_share(active_low, d_second_low, down_got, down_order[0])
    down_sent, d_hidden_low = tie(down_sent, d_hidden_low)
    down_got = move(down_sent, down_order[0])
    d_first = d_second + dot(d_hidden_low, wu, 1, 1)
    d_branch, grad_gain_one, grad_shift_one = first_pull(d_first)
    d_branch_low, up_got = tie(d_branch.astype(BF), up_got)
    up_sent, up = second_share(first_low, d_hidden_low, up_got, up_order[0])
    up_sent, d_branch_low = tie(up_sent, d_branch_low)
    up_got = move(up_sent, up_order[0])
    out_sent = first_share(attended, d_branch_low)
    d_attended_t = dot(wo, d_branch_low, 1, 1).astype(BF)
    outgoing = d_attended_t.reshape(heads, d, parts, mine).transpose(0, 2, 1, 3).reshape(ctx, d, mine)
    do_t = lax.all_to_all(outgoing, "ctx", 0, 0, tiled=True)

    outgoing, out_sent = tie(outgoing, out_sent)
    out_got = move(out_sent, core_step)
    out_sent, out = second_share(attended, d_branch_low, out_got, out_order[0])
    out_got = move(out_sent, out_order[0])
    vectors = [
        jnp.sum(d_branch, axis=0), grad_gain_one, grad_shift_one, jnp.sum(d_second, axis=0), grad_gain_two,
        grad_shift_two,
    ]
    vectors = jnp.concatenate(
        [jnp.stack(vectors).reshape(6, fsdp, shard).transpose(1, 0, 2).reshape(fsdp, -1),
         jnp.sum(d_hidden, axis=0).reshape(fsdp, -1)], axis=1,
    )
    vectors = lax.all_gather(vectors, ("ctx", "fsdp"), axis=0, tiled=False)
    do_t, out_sent, down.terms[0], up.terms[0], out.terms[0] = tie(
        do_t, out_sent, down.terms[0], up.terms[0], out.terms[0]
    )

    delta = jnp.sum(
        attended_t.reshape(d, ctx, mine) * do_t.transpose(1, 0, 2).astype(F32), axis=0
    ).reshape(1, count)
    bq, bk = min(512, count), 512
    ranges = block_ranges(starts_all, ends_all, bk, bq * parts)
    calls = 4
    per_call = length // bk // calls
    dqt = jnp.zeros((d, count), F32)
    dkt, dvt = [], []
    down_left, up_left, out_left = down_order[1:], up_order[1:], out_order[1:]

    def one_step(one, left, got):
        one.receive(got)
        step = left.pop(0)
        sent = one.send(step)
        return sent, move(sent, step)

    def both_step():
        step = down_left.pop(0)
        sent = jnp.concatenate([down.send(step), out.send(step)], axis=-2)
        return sent, move(sent, step)

    def both_receive(got):
        rows = down.terms[0].shape[-2]
        down.receive(got[..., :rows, :])
        out.receive(got[..., rows:, :])

    for call in range(calls):
        dk_new, dv_new, dqt = attention_backward(
            q, k, v, do_t, lse, delta, starts, ends, ranges, dqt, scale, bq, bk, call * per_call, per_call
        )
        dkt.append(dk_new)
        dvt.append(dv_new)
        if call == 2:
            dqt, down_got, up_got, out_got, vectors = tie(dqt, down_got, up_got, out_got, vectors)
            up_sent, up_got = one_step(up, up_left, up_got)
            down_sent, down_got = one_step(down, down_left, down_got)
            out_sent, out_got = one_step(out, out_left, out_got)
            while len(down_left) >= len(ctx_steps):
                down_sent, down_got = one_step(down, down_left, down_got)
                out_sent, out_got = one_step(out, out_left, out_got)
            dqt, down_sent, up_sent, out_sent = tie(dqt, down_sent, up_sent, out_sent)

    dkt, dvt = jnp.concatenate(dkt, axis=1), jnp.concatenate(dvt, axis=1)
    dqt = (dqt * scale).astype(BF)
    if parts == 1:
        dqkv_t = jnp.concatenate([dqt, dkt, dvt], axis=0)
        outgoing = dqkv_t.reshape(3 * d, ctx, block).transpose(1, 0, 2)
        incoming = lax.all_to_all(outgoing, "ctx", 0, 0, tiled=True)
        outgoing, dqkv_t, up_got = tie(outgoing, dqkv_t, up_got)
        up_sent, up_got = one_step(up, up_left, up_got)
        down_got, out_got, up_sent = tie(down_got, out_got, up_sent)
        down.receive(down_got)
        out.receive(out_got)
        down_sent, down_got = both_step()
        dqkv_t, down_sent = tie(dqkv_t, down_sent)
        grad_head = dot(dqkv_t, everyone, 1, 0)
        sums = jnp.sum(dqkv_t.astype(F32), axis=1)
    else:
        dqt, up_got = tie(dqt, up_got)
        up_sent, up_got = one_step(up, up_left, up_got)
        down_got, out_got, up_sent = tie(down_got, out_got, up_sent)
        down.receive(down_got)
        out.receive(out_got)
        down_sent, down_got = both_step()
        dqt, down_sent = tie(dqt, down_sent)
        back = lambda a: lax.all_to_all(
            a.reshape(d, ctx, -1).transpose(1, 0, 2), "ctx", 0, 0, tiled=True
        ).reshape(heads, parts, d, -1)
        summed = lambda a: jnp.sum(back(a).astype(F32), axis=1).astype(BF)
        incoming = jnp.stack([back(dqt).transpose(0, 2, 1, 3).reshape(heads, d, block), summed(dkt), summed(dvt)], axis=1)
        grad_head = jnp.concatenate([dot(dqt, own_part(everyone), 1, 0), dot(dkt, everyone, 1, 0), dot(dvt, everyone, 1, 0)])
        sums = jnp.concatenate([jnp.sum(a.astype(F32), axis=1) for a in (dqt, dkt, dvt)])
    grad_head = grad_head.reshape(3 * d, fsdp, shard).transpose(1, 0, 2)
    extra = jnp.pad(sums[None, None], ((0, 0), (0, 15), (0, shard - 3 * d))) if shard >= 3 * d else jnp.pad(
        sums.reshape(1, -1, shard // 2), ((0, 0), (0, 16 - 6 * d // shard), (0, shard // 2))
    )
    grad_head = jnp.concatenate([grad_head, jnp.broadcast_to(extra, (fsdp, 16, shard))], axis=1)
    for step in fsdp_steps:
        pair = grad_head.reshape(2, -1, 3 * d + 16, shard)
        sent = lax.dynamic_index_in_dim(pair, 1 - own_bit(step), 0, keepdims=False).astype(BF)
        kept = lax.dynamic_index_in_dim(pair, own_bit(step), 0, keepdims=False)
        if step == fsdp_steps[0]:
            up_got, sent = tie(up_got, sent)
        grad_head = kept + move(sent, step).astype(F32)
    grad_head = grad_head[0].astype(BF)

    up_sent, up_got = one_step(up, up_left, up_got)
    down_got, up_sent = tie(down_got, up_sent)
    both_receive(down_got)
    while down_left:
        down_sent, down_got = both_step()
        down_got, grad_head = tie(down_got, grad_head)
        both_receive(down_got)
    while up_left:
        up_sent, up_got = one_step(up, up_left, up_got)
    up_got, incoming = tie(up_got, incoming)
    up.receive(up_got)
    vectors = jnp.sum(lax.dynamic_index_in_dim(vectors, row, 1, keepdims=False), axis=0)
    six = vectors[: 6 * shard].reshape(6, shard)
    grad_b_up = vectors[6 * shard :]

    up_block = up.total(up.terms)
    rows_up, rows_down = up_block.shape[0], down.terms[0].shape[0]
    wide = hidden // width
    per_row = width // shard
    rows_head = (3 * d + 16) // per_row
    at_head = rows_down + (wide + 1) * rows_up
    pieces = [down.total(down.terms)] + [up_block[:, i * width : (i + 1) * width] for i in range(wide)] + [out.total(out.terms)]
    split = grad_head.reshape(per_row, -1, shard)
    pieces.append(jnp.concatenate([split[i] for i in range(per_row)], axis=1))
    pieces = jnp.concatenate(pieces, axis=0)
    every = lax.all_gather(pieces, "ctx", axis=0, tiled=False)
    wqkv, pieces = tie(wqkv, pieces)
    wqkv_near = near_half(wqkv)
    wqkv_all = assemble(wqkv, wqkv_near, far_half(wqkv_near))
    token_grad = d_branch + dot(incoming.reshape(3 * width, block), wqkv_all, 0, 1)
    if parts == 1 and per_row == 2 and shard >= 3 * d:
        grad_w_down, grad_w_up, grad_w_out, grad_qkv = in_order(every, rows_down, rows_up, wide, d, shard)
        at = (3 * d) % rows_head
        sums = every[:, at_head + at, shard : shard + 3 * d].astype(F32)
    else:
        grad_w_down = sorted_rows(every[:, :rows_down]).astype(F32)
        take = lambda i: sorted_rows(every[:, rows_down + i * rows_up :][:, :rows_up]).astype(F32)
        grad_w_up = jnp.concatenate([take(i) for i in range(wide)], axis=1)
        grad_w_out = take(wide)
        every_head = every[:, at_head:]
        every_head = jnp.concatenate([every_head[:, :, i * shard : (i + 1) * shard] for i in range(per_row)], axis=1)
        every_head = every_head.astype(F32).reshape(heads, parts, 3 * d + 16, shard).sum(axis=1)
        grad_qkv = every_head[:, : 3 * d].reshape(heads, 3, d, shard).transpose(1, 3, 0, 2).reshape(3, shard, width)
        sums = every_head[:, 3 * d :]
        if shard >= 3 * d:
            sums = sums[:, 0, : 3 * d]
        else:
            sums = sums[:, : 6 * d // shard, : shard // 2]
    sums = sums.reshape(heads, 3, d).transpose(1, 0, 2).reshape(3, width)
    bias_q = cut(sums[0], row * shard, shard, 0)
    bias_v = cut(sums[2], row * shard, shard, 0)

    return (
        output[None].astype(BF),
        token_grad[None].astype(BF),
        grad_qkv[0],
        grad_qkv[1],
        grad_qkv[2],
        grad_w_out,
        bias_q,
        bias_v,
        six[0],
        six[1],
        six[2],
        grad_w_up,
        grad_b_up,
        grad_w_down,
        six[3],
        six[4],
        six[5],
    )


def solution(mesh):
    line, matrix, rows = P("fsdp"), P("fsdp", None), P("fsdp", "ctx", None)
    placed = (
        (rows, matrix) + (matrix,) * 4 + (line,) * 5 + (matrix, line, matrix) + (line,) * 3 + (rows,)
    )
    outs = (rows, rows) + (matrix,) * 4 + (line,) * 5 + (matrix, line, matrix) + (line,) * 3
    return jax.shard_map(
        functools.partial(body, mesh.shape["ctx"], mesh.shape["fsdp"]),
        mesh=mesh,
        in_specs=placed,
        out_specs=outs,
        check_vma=False,
    )
```

```python
import functools
import math

import jax
import jax.numpy as jnp
from jax import lax
from jax.experimental import pallas as pl
from jax.experimental.pallas import tpu as pltpu
from jax.sharding import PartitionSpec as P

HEADS = 16
LOG2E = 1.4426950408889634
NEG = -1e30
BF = jnp.bfloat16
F32 = jnp.float32


def layer_norm(hidden, gain, shift):
    mean = jnp.mean(hidden, axis=-1, keepdims=True)
    centred = hidden - mean
    variance = jnp.mean(centred * centred, axis=-1, keepdims=True)
    return centred * lax.rsqrt(variance + 1e-05) * gain + shift


def gelu_exact(value):
    return jax.nn.gelu(value, approximate=False)


def dot(left, right, on_left, on_right):
    return lax.dot_general(
        left, right, (((on_left,), (on_right,)), ((), ())), preferred_element_type=F32
    )


def flip(value, axis, bit, size):
    return lax.ppermute(value, axis, [(i, i ^ bit) for i in range(size)])


def forward_kernel(
    lo_ref, hi_ref, in_lo_ref, in_hi_ref, q_ref, k_ref, v_ref, start_ref, end_ref,
    out_ref, low_ref, lse_ref, total_ref, vt_ref, *, bk, scale
):
    i = pl.program_id(0)
    bq = q_ref.shape[0]

    @pl.when(i == 0)
    def _():
        @pl.loop(0, v_ref.shape[0] // bk)
        def _(j):
            at = pl.multiple_of(j * bk, bk)
            vt_ref[:, pl.ds(at, bk)] = v_ref[pl.ds(at, bk), :].T

    q = q_ref[...]
    start, end = start_ref[...], end_ref[...]
    total_ref[...] = jnp.zeros_like(total_ref)

    def step(j, carry, masked):
        peak, norm = carry
        at = pl.multiple_of(j * bk, bk)
        s = dot(k_ref[pl.ds(at, bk), :], q, 1, 1) * (scale * LOG2E)
        if masked:
            at_key = lax.broadcasted_iota(jnp.int32, (bk, bq), 0) + at
            s = jnp.where((at_key >= start) & (at_key < end), s, NEG)
        new_peak = jnp.maximum(peak, jnp.max(s, axis=0, keepdims=True))
        p = jnp.exp2(s - new_peak)
        shrink = jnp.exp2(peak - new_peak)
        norm = norm * shrink + jnp.sum(p, axis=0, keepdims=True)
        total_ref[...] = total_ref[...] * shrink + dot(vt_ref[:, pl.ds(at, bk)], p.astype(BF), 1, 0)
        return new_peak, norm

    lo, hi, in_lo, in_hi = lo_ref[i], hi_ref[i], in_lo_ref[i], in_hi_ref[i]
    carry = (jnp.full((1, bq), NEG, F32), jnp.zeros((1, bq), F32))
    carry = lax.fori_loop(in_lo, in_hi, lambda j, c: step(j, c, False), carry)
    carry = lax.fori_loop(lo, in_lo, lambda j, c: step(j, c, True), carry)
    peak, norm = lax.fori_loop(in_hi, hi, lambda j, c: step(j, c, True), carry)
    out = total_ref[...] / norm
    out_ref[...] = out
    n = low_ref.shape[2]
    for piece in range(bq // n):
        low_ref[piece] = out[:, piece * n : (piece + 1) * n].astype(low_ref.dtype)
    lse_ref[...] = peak + jnp.log2(norm)


def block_ranges(starts, ends, rows, others):
    first, last = starts.reshape(-1, rows), ends.reshape(-1, rows)
    lo = first[:, 0] // others
    hi = (last[:, -1] + others - 1) // others
    in_lo = jnp.clip((first[:, -1] + others - 1) // others, lo, hi)
    in_hi = jnp.clip(last[:, 0] // others, in_lo, hi)
    return lo, hi, in_lo, in_hi


def attention_forward(q, k, v, starts, ends, scale, n, bq=1024, bk=512):
    count, d = q.shape
    length = k.shape[0]
    bq = min(bq, count)
    ranges = block_ranges(starts, ends, bq, bk)
    row = lambda: pl.BlockSpec((1, bq), lambda i, *_: (0, i))
    whole = lambda shape: pl.BlockSpec(shape, lambda i, *_: (0, 0))
    return pl.pallas_call(
        functools.partial(forward_kernel, bk=bk, scale=scale),
        out_shape=(
            jax.ShapeDtypeStruct((d, count), F32),
            jax.ShapeDtypeStruct((count // n, d, n), BF),
            jax.ShapeDtypeStruct((1, count), F32),
        ),
        grid_spec=pltpu.PrefetchScalarGridSpec(
            num_scalar_prefetch=4,
            grid=(count // bq,),
            in_specs=[
                pl.BlockSpec((bq, d), lambda i, *_: (i, 0)),
                whole((length, d)),
                whole((length, d)),
                row(),
                row(),
            ],
            out_specs=[
                pl.BlockSpec((d, bq), lambda i, *_: (0, i)),
                pl.BlockSpec((bq // n, d, n), lambda i, *_: (i, 0, 0)),
                row(),
            ],
            scratch_shapes=[pltpu.VMEM((d, bq), F32), pltpu.VMEM((d, length), BF)],
        ),
        compiler_params=pltpu.CompilerParams(vmem_limit_bytes=40 << 20),
        cost_estimate=pl.CostEstimate(
            flops=16 * count * length * d, bytes_accessed=length * d * 16, transcendentals=count * length
        ),
        name="attention_forward",
    )(*ranges, q, k, v, starts[None], ends[None])


def backward_kernel(
    lo_ref, hi_ref, in_lo_ref, in_hi_ref, k_ref, v_ref, q_ref, do_ref, lse_ref, delta_ref, start_ref,
    end_ref, dqt_in_ref, dkt_ref, dvt_ref, dqt_ref, dk_sum, dv_sum, *, bq, scale, base
):
    j = pl.program_id(0) + base
    bk = k_ref.shape[0]
    pieces = bq // do_ref.shape[2]

    @pl.when(pl.program_id(0) == 0)
    def _():
        dqt_ref[...] = dqt_in_ref[...]

    k, v = k_ref[...], v_ref[...]
    kt = k.T
    dk_sum[...] = jnp.zeros_like(dk_sum)
    dv_sum[...] = jnp.zeros_like(dv_sum)

    def step(i, masked):
        at = pl.multiple_of(i * bq, bq)
        row = pl.ds(at, bq)
        q = q_ref[row, :]
        do_t = jnp.concatenate([do_ref[i * pieces + n] for n in range(pieces)], axis=1)
        s = dot(k, q, 1, 1) * (scale * LOG2E) - lse_ref[:, row]
        if masked:
            at_key = lax.broadcasted_iota(jnp.int32, (bk, bq), 0) + j * bk
            s = jnp.where((at_key >= start_ref[:, row]) & (at_key < end_ref[:, row]), s, NEG)
        p = jnp.exp2(s)
        dp = dot(v, do_t, 1, 0)
        dv_sum[...] += dot(p.astype(BF), do_t, 1, 1)
        ds = (p * (dp - delta_ref[:, row])).astype(BF)
        dk_sum[...] += dot(ds, q, 1, 0)
        dqt_ref[:, row] += dot(kt, ds, 1, 0)

    lo, hi, in_lo, in_hi = lo_ref[j], hi_ref[j], in_lo_ref[j], in_hi_ref[j]
    pl.loop(in_lo, in_hi)(lambda i: step(i, False))
    pl.loop(lo, in_lo)(lambda i: step(i, True))
    pl.loop(in_hi, hi)(lambda i: step(i, True))
    dkt_ref[...] = (dk_sum[...] * scale).T.astype(dkt_ref.dtype)
    dvt_ref[...] = dv_sum[...].T.astype(dvt_ref.dtype)


def attention_backward(q, k, v, do_t, lse, delta, starts, ends, ranges, dqt, scale, bq, bk, base, blocks):
    count, d = q.shape
    whole = lambda shape: pl.BlockSpec(shape, lambda j, *_: (0,) * len(shape))
    keys = lambda: pl.BlockSpec((bk, d), lambda j, *_: (j + base, 0))
    columns = lambda: pl.BlockSpec((d, bk), lambda j, *_: (0, j))
    return pl.pallas_call(
        functools.partial(backward_kernel, bq=bq, scale=scale, base=base),
        out_shape=(
            jax.ShapeDtypeStruct((d, blocks * bk), BF),
            jax.ShapeDtypeStruct((d, blocks * bk), BF),
            jax.ShapeDtypeStruct((d, count), F32),
        ),
        grid_spec=pltpu.PrefetchScalarGridSpec(
            num_scalar_prefetch=4,
            grid=(blocks,),
            in_specs=[
                keys(),
                keys(),
                whole((count, d)),
                whole(do_t.shape),
                whole((1, count)),
                whole((1, count)),
                whole((1, count)),
                whole((1, count)),
                whole((d, count)),
            ],
            out_specs=[columns(), columns(), whole((d, count))],
            scratch_shapes=[pltpu.VMEM((bk, d), F32), pltpu.VMEM((bk, d), F32)],
        ),
        compiler_params=pltpu.CompilerParams(vmem_limit_bytes=32 << 20),
        cost_estimate=pl.CostEstimate(
            flops=count * d, bytes_accessed=count * d, transcendentals=0
        ),
        name="attention_backward",
    )(*ranges, k, v, q, do_t, lse, delta, starts[None], ends[None], dqt)


class Halving:
    def __init__(self, place, sizes):
        self.place, self.sizes, self.terms = list(place), sizes, []

    def own(self, step):
        return (lax.axis_index(step[0]) // step[1]) % 2

    def share(self, step, which):
        at = self.place.index(step)
        return [lax.dynamic_index_in_dim(t, which, at, keepdims=False) for t in self.terms]

    def total(self, terms):
        return sum((t.astype(F32) for t in terms[1:]), terms[0].astype(F32)).astype(BF)

    def send(self, step):
        sent = self.total(self.share(step, 1 - self.own(step)))
        self.terms = self.share(step, self.own(step))
        self.place.remove(step)
        return sent

    def receive(self, got):
        self.terms.append(got)


def reversed_bits(i, count):
    n = count.bit_length() - 1
    return sum(((i // (1 << b)) % 2) * (1 << (n - 1 - b)) for b in range(n))


def order_kernel(every_ref, down_ref, up_ref, out_ref, qkv_ref, *, rows, wide, d, shard):
    rows_down, width = down_ref.shape[2:]
    starts = [rows_down + i * rows for i in range(wide + 2)]
    halves = []
    for half in range(2):
        down_ref[half, 0] = every_ref[half, :rows_down, :].astype(F32)
        for i in range(wide):
            slab = every_ref[half, starts[i] : starts[i + 1], :]
            up_ref[half, 0, :, i * width : (i + 1) * width] = slab.astype(F32)
        out_ref[half, 0] = every_ref[half, starts[wide] : starts[wide + 1], :].astype(F32)
        both = every_ref[half, starts[wide + 1] :, :].astype(F32)
        halves.append(jnp.concatenate([both[:, :shard], both[:, shard:]], axis=0))
    for t in range(3):
        pair = jnp.concatenate([h[t * d : (t + 1) * d] for h in halves], axis=0)
        qkv_ref[t] = pair.T


def in_order(every, rows_down, rows, wide, d, shard):
    n, whole, width = every.shape
    place = lambda i: (0, reversed_bits(i, n // 2), 0, 0)
    down, up, out, qkv = pl.pallas_call(
        functools.partial(order_kernel, rows=rows, wide=wide, d=d, shard=shard),
        out_shape=(
            jax.ShapeDtypeStruct((2, n // 2, rows_down, width), F32),
            jax.ShapeDtypeStruct((2, n // 2, rows, wide * width), F32),
            jax.ShapeDtypeStruct((2, n // 2, rows, width), F32),
            jax.ShapeDtypeStruct((3, shard, n * d), F32),
        ),
        grid=(n // 2,),
        in_specs=[pl.BlockSpec((2, whole, width), lambda i: (i, 0, 0))],
        out_specs=[
            pl.BlockSpec((2, 1, rows_down, width), place),
            pl.BlockSpec((2, 1, rows, wide * width), place),
            pl.BlockSpec((2, 1, rows, width), place),
            pl.BlockSpec((3, shard, 2 * d), lambda i: (0, 0, i)),
        ],
        compiler_params=pltpu.CompilerParams(vmem_limit_bytes=32 << 20),
        cost_estimate=pl.CostEstimate(flops=0, bytes_accessed=6 * every.size, transcendentals=0),
        name="in_order",
    )(every)
    return down.reshape(n * rows_down, width), up.reshape(n * rows, wide * width), out.reshape(n * rows, width), qkv


def body(ctx, fsdp, tokens, segments, w_query, w_key, w_value, w_out, b_query, b_value, b_out, gain_one, shift_one,
         w_up, b_up, w_down, b_down, gain_two, shift_two, cotangent):
    _, block, width = tokens.shape
    heads = HEADS
    d = width // heads
    scale = 1.0 / math.sqrt(d)
    parts = ctx // heads
    mine = block // parts
    length = ctx * block
    count = length // parts
    hidden = w_up.shape[1]
    shard = w_query.shape[0]
    me = lax.axis_index("ctx")
    row = lax.axis_index("fsdp")
    head, part = me // parts, me % parts
    core = me % 2
    cut = lambda a, at, size, axis: lax.dynamic_slice_in_dim(a, at, size, axis)

    bits = lambda n: [1 << i for i in range(n.bit_length() - 1)]
    sizes = {"fsdp": fsdp, "ctx": ctx}
    tie = lambda *arrays: lax.optimization_barrier(arrays)

    def gather_small(a):
        if fsdp == 2:
            other = flip(a, "fsdp", 1, 2)
            return jnp.concatenate([jnp.where(row == 0, a, other), jnp.where(row == 0, other, a)], axis=0)
        return lax.all_gather(a, "fsdp", axis=0, tiled=True)

    def near_half(w):
        if fsdp != 2:
            return lax.all_gather(w, "fsdp", axis=0, tiled=True)
        return flip(cut(w, core * (w.shape[0] // 2), w.shape[0] // 2, 0), "fsdp", 1, 2)

    def far_half(near):
        return flip(near, "ctx", 1, ctx) if fsdp == 2 else near

    def assemble(w, near, far):
        if fsdp != 2:
            return near
        rows, half = w.shape[0], w.shape[0] // 2
        whole = jnp.zeros((2 * rows, w.shape[1]), w.dtype)
        whole = lax.dynamic_update_slice_in_dim(whole, w, row * rows, 0)
        whole = lax.dynamic_update_slice_in_dim(whole, near, (1 - row) * rows + core * half, 0)
        return lax.dynamic_update_slice_in_dim(whole, far, (1 - row) * rows + (1 - core) * half, 0)

    def move(send, step):
        return flip(send, step[0], step[1], sizes[step[0]])

    core_step = ("ctx", 1)
    every_place = [("fsdp", b) for b in reversed(bits(fsdp))] + [("ctx", b) for b in bits(ctx)]
    own_bit = lambda step: (lax.axis_index(step[0]) // step[1]) % 2

    def columns_of(left, chosen):
        depth = max(every_place.index(step) for step in chosen) + 1
        size = left.shape[1] >> depth
        offsets = [0]
        for level, step in enumerate(every_place[:depth]):
            stride = left.shape[1] >> (level + 1)
            options = [chosen[step]] if step in chosen else [0, 1]
            offsets = [at + which * stride for at in offsets for which in options]
        return jnp.concatenate([cut(left, at, size, 1) for at in offsets], axis=1)

    def blocks(rows_data, place):
        return rows_data.reshape([2] * len(place) + [-1, rows_data.shape[1]])

    def first_share(left, right):
        return dot(columns_of(left, {core_step: 1 - own_bit(core_step)}), right, 0, 0).astype(BF)

    def second_share(left, right, got, step):
        place = [p for p in every_place if p != core_step]
        got = blocks(got, place)
        inner = [p for p in place if p != step]
        parts_of = []
        for which in (1 - own_bit(step), own_bit(step)):
            rows_data = dot(columns_of(left, {core_step: own_bit(core_step), step: which}), right, 0, 0)
            added = lax.dynamic_index_in_dim(got, which, place.index(step), keepdims=False)
            parts_of.append((blocks(rows_data, inner) + added.astype(F32)).astype(BF))
        rest = Halving(inner, sizes)
        rest.terms = [parts_of[1]]
        return parts_of[0], rest

    def sorted_rows(every):
        n = len(bits(ctx))
        shape = every.shape
        every = every.reshape((2,) * n + shape[1:]).transpose(list(reversed(range(n))) + [n, n + 1])
        return every.reshape(-1, shape[2])

    inputs = tokens[0]
    everyone = lax.all_gather(inputs, "ctx", axis=0, tiled=True)
    by_head = lambda w: w.reshape(shard, heads, 1, d)
    wqkv = jnp.concatenate([by_head(w) for w in (w_query, w_key, w_value)], axis=2).reshape(shard, 3 * width)
    small = jnp.stack([b_query, b_value, b_out, gain_one, shift_one, b_down, gain_two, shift_two])
    small = jnp.concatenate([small.reshape(-1), b_up])[None]
    w_head = gather_small(jnp.concatenate([cut(w, head * d, d, 1) for w in (w_query, w_key, w_value)], axis=1))
    small = gather_small(small)
    wo_near = near_half(w_out)
    wu_near = near_half(w_up)
    wo_near, w_head, small = tie(wo_near, w_head, small)
    wo = assemble(w_out, wo_near, far_half(wo_near))
    wu_near, w_down, wo = tie(wu_near, w_down, wo)
    wd_near = near_half(w_down)
    wu_far = far_half(wu_near)
    everyone, wu_near = tie(everyone, wu_near)

    eight = small[:, : 8 * shard].reshape(-1, 8, shard).transpose(1, 0, 2).reshape(8, width).astype(F32)
    bq_, bv_, bo, gain1, shift1, bd, gain2, shift2 = (eight[i] for i in range(8))
    bu = small[:, 8 * shard :].reshape(hidden).astype(F32)
    projected = dot(everyone, w_head, 1, 0)
    my_bias = jnp.concatenate([cut(bq_, head * d, d, 0), jnp.zeros((d,), F32), cut(bv_, head * d, d, 0)])
    projected = (projected + my_bias).astype(BF)
    own_part = lambda a: cut(a.reshape((ctx, block) + a.shape[1:]), part * mine, mine, 1).reshape(
        (count,) + a.shape[1:]
    )
    q = own_part(projected[:, :d])
    k, v = projected[:, d : 2 * d], projected[:, 2 * d :]
    seg = segments[0]
    starts_all = jnp.sum(seg[None, :] < seg[:, None], axis=1, dtype=jnp.int32)
    ends_all = jnp.sum(seg[None, :] <= seg[:, None], axis=1, dtype=jnp.int32)
    starts, ends = own_part(starts_all), own_part(ends_all)

    attended_t, outgoing, lse = attention_forward(q, k, v, starts, ends, scale, mine)
    incoming = lax.all_to_all(outgoing, "ctx", 0, 0, tiled=True)
    wu_far, outgoing, wu_near = tie(wu_far, outgoing, wu_near)
    wu = assemble(w_up, wu_near, wu_far)
    incoming, wu = tie(incoming, wu)
    attended = incoming.reshape(heads, parts, d, mine).transpose(1, 3, 0, 2).reshape(block, width)
    branch = dot(attended, wo, 1, 0) + bo
    first, first_pull = jax.vjp(layer_norm, inputs.astype(F32) + branch, gain1, shift1)
    first_low, wd_near = tie(first.astype(BF), wd_near)
    wd = assemble(w_down, wd_near, far_half(wd_near))
    hidden_pre = dot(first_low, wu, 1, 0) + bu
    active, active_pull = jax.vjp(gelu_exact, hidden_pre)
    (slope,) = active_pull(jnp.ones_like(active))
    active_low, slope = tie(active.astype(BF), slope)
    second = dot(active_low, wd, 1, 0) + bd
    output, out_pull = jax.vjp(layer_norm, first + second, gain2, shift2)

    fsdp_steps = [("fsdp", b) for b in reversed(bits(fsdp))]
    ctx_steps = [("ctx", b) for b in bits(ctx) if b > 1]
    down_order = fsdp_steps + ctx_steps
    up_order = ctx_steps[1:2] + fsdp_steps + ctx_steps[:1] + ctx_steps[2:]
    out_order = ctx_steps[:1] + fsdp_steps + ctx_steps[1:]
    d_second, grad_gain_two, grad_shift_two = out_pull(cotangent[0].astype(F32))
    d_second_low = d_second.astype(BF)
    down_sent = first_share(active_low, d_second_low)
    down_sent, d_second_low = tie(down_sent, d_second_low)
    down_got = move(down_sent, core_step)
    d_hidden = dot(d_second_low, wd, 1, 1) * slope
    d_hidden_low = d_hidden.astype(BF)
    up_sent = first_share(first_low, d_hidden_low)
    up_sent, d_hidden_low, down_got = tie(up_sent, d_hidden_low, down_got)
    up_got = move(up_sent, core_step)
    down_sent, down = second_share(active_low, d_second_low, down_got, down_order[0])
    down_sent, d_hidden_low = tie(down_sent, d_hidden_low)
    down_got = move(down_sent, down_order[0])
    d_first = d_second + dot(d_hidden_low, wu, 1, 1)
    d_branch, grad_gain_one, grad_shift_one = first_pull(d_first)
    d_branch_low = d_branch.astype(BF)
    d_attended_t = dot(wo, d_branch_low, 1, 1).astype(BF)
    outgoing = d_attended_t.reshape(heads, d, parts, mine).transpose(0, 2, 1, 3).reshape(ctx, d, mine)
    do_t = lax.all_to_all(outgoing, "ctx", 0, 0, tiled=True)
    outgoing, d_branch_low, up_got = tie(outgoing, d_branch_low, up_got)
    out_sent = first_share(attended, d_branch_low)
    out_sent, d_hidden_low = tie(out_sent, d_hidden_low)
    out_got = move(out_sent, core_step)
    up_sent, up = second_share(first_low, d_hidden_low, up_got, up_order[0])
    up_sent, out_got = tie(up_sent, out_got)
    out_sent, out = second_share(attended, d_branch_low, out_got, out_order[0])
    vectors = [
        jnp.sum(d_branch, axis=0), grad_gain_one, grad_shift_one, jnp.sum(d_second, axis=0), grad_gain_two,
        grad_shift_two,
    ]
    vectors = jnp.concatenate(
        [jnp.stack(vectors).reshape(6, fsdp, shard).transpose(1, 0, 2).reshape(fsdp, -1),
         jnp.sum(d_hidden, axis=0).reshape(fsdp, -1)], axis=1,
    )
    vectors = lax.all_gather(vectors, ("ctx", "fsdp"), axis=0, tiled=False)
    do_t, up_sent, out_sent, down.terms[0], up.terms[0], out.terms[0] = tie(
        do_t, up_sent, out_sent, down.terms[0], up.terms[0], out.terms[0]
    )
    up_got, out_got = move(up_sent, up_order[0]), move(out_sent, out_order[0])

    delta = jnp.sum(
        attended_t.reshape(d, ctx, mine) * do_t.transpose(1, 0, 2).astype(F32), axis=0
    ).reshape(1, count)
    bq, bk = min(512, count), 512
    ranges = block_ranges(starts_all, ends_all, bk, bq * parts)
    calls = 4
    per_call = length // bk // calls
    dqt = jnp.zeros((d, count), F32)
    dkt, dvt = [], []
    down_left, up_left, out_left = down_order[1:], up_order[1:], out_order[1:]

    def one_step(one, left, got):
        one.receive(got)
        step = left.pop(0)
        sent = one.send(step)
        return sent, move(sent, step)

    def both_step():
        step = down_left.pop(0)
        sent = jnp.concatenate([down.send(step), out.send(step)], axis=-2)
        return sent, move(sent, step)

    def both_receive(got):
        rows = down.terms[0].shape[-2]
        down.receive(got[..., :rows, :])
        out.receive(got[..., rows:, :])

    for call in range(calls):
        dk_new, dv_new, dqt = attention_backward(
            q, k, v, do_t, lse, delta, starts, ends, ranges, dqt, scale, bq, bk, call * per_call, per_call
        )
        dkt.append(dk_new)
        dvt.append(dv_new)
        if call == 1:
            dqt, down_got, out_got = tie(dqt, down_got, out_got)
            down_sent, down_got = one_step(down, down_left, down_got)
            out_sent, out_got = one_step(out, out_left, out_got)
            while len(down_left) >= len(ctx_steps):
                down_sent, down_got = one_step(down, down_left, down_got)
                out_sent, out_got = one_step(out, out_left, out_got)
            dqt, down_sent, out_sent = tie(dqt, down_sent, out_sent)

    dkt, dvt = jnp.concatenate(dkt, axis=1), jnp.concatenate(dvt, axis=1)
    dqt = (dqt * scale).astype(BF)
    if parts == 1:
        dqkv_t = jnp.concatenate([dqt, dkt, dvt], axis=0)
        outgoing = dqkv_t.reshape(3 * d, ctx, block).transpose(1, 0, 2)
        dqkv_t, up_got, vectors = tie(dqkv_t, up_got, vectors)
        up_sent, up_got = one_step(up, up_left, up_got)
        down_got, out_got, up_sent = tie(down_got, out_got, up_sent)
        down.receive(down_got)
        out.receive(out_got)
        down_sent, down_got = both_step()
        dqkv_t, down_sent = tie(dqkv_t, down_sent)
        grad_head = dot(dqkv_t, everyone, 1, 0)
        sums = jnp.sum(dqkv_t.astype(F32), axis=1)
    else:
        dqt, up_got, vectors = tie(dqt, up_got, vectors)
        up_sent, up_got = one_step(up, up_left, up_got)
        down_got, out_got, up_sent = tie(down_got, out_got, up_sent)
        down.receive(down_got)
        out.receive(out_got)
        down_sent, down_got = both_step()
        dqt, down_sent = tie(dqt, down_sent)
        back = lambda a: lax.all_to_all(
            a.reshape(d, ctx, -1).transpose(1, 0, 2), "ctx", 0, 0, tiled=True
        ).reshape(heads, parts, d, -1)
        summed = lambda a: jnp.sum(back(a).astype(F32), axis=1).astype(BF)
        incoming = jnp.stack([back(dqt).transpose(0, 2, 1, 3).reshape(heads, d, block), summed(dkt), summed(dvt)], axis=1)
        grad_head = jnp.concatenate([dot(dqt, own_part(everyone), 1, 0), dot(dkt, everyone, 1, 0), dot(dvt, everyone, 1, 0)])
        sums = jnp.concatenate([jnp.sum(a.astype(F32), axis=1) for a in (dqt, dkt, dvt)])
    grad_head = grad_head.reshape(3 * d, fsdp, shard).transpose(1, 0, 2)
    extra = jnp.pad(sums[None, None], ((0, 0), (0, 15), (0, shard - 3 * d))) if shard >= 3 * d else jnp.pad(
        sums.reshape(1, -1, shard // 2), ((0, 0), (0, 16 - 6 * d // shard), (0, shard // 2))
    )
    grad_head = jnp.concatenate([grad_head, jnp.broadcast_to(extra, (fsdp, 16, shard))], axis=1)
    for step in fsdp_steps:
        pair = grad_head.reshape(2, -1, 3 * d + 16, shard)
        sent = lax.dynamic_index_in_dim(pair, 1 - own_bit(step), 0, keepdims=False).astype(BF)
        kept = lax.dynamic_index_in_dim(pair, own_bit(step), 0, keepdims=False)
        if step == fsdp_steps[0]:
            down_got, sent = tie(down_got, sent)
        grad_head = kept + move(sent, step).astype(F32)
    grad_head = grad_head[0].astype(BF)

    both_receive(down_got)
    while down_left:
        down_sent, down_got = both_step()
        if len(up_left) > 1:
            up_got, down_sent = tie(up_got, down_sent)
            up_sent, up_got = one_step(up, up_left, up_got)
            down_got, up_sent = tie(down_got, up_sent)
        if down_left:
            both_receive(down_got)
    up_got, grad_head = tie(up_got, grad_head)
    while up_left:
        up_sent, up_got = one_step(up, up_left, up_got)
    down_got, up_sent = tie(down_got, up_sent)
    both_receive(down_got)
    up.receive(up_got)
    vectors = jnp.sum(lax.dynamic_index_in_dim(vectors, row, 1, keepdims=False), axis=0)
    six = vectors[: 6 * shard].reshape(6, shard)
    grad_b_up = vectors[6 * shard :]

    up_block = up.total(up.terms)
    rows_up, rows_down = up_block.shape[0], down.terms[0].shape[0]
    wide = hidden // width
    per_row = width // shard
    rows_head = (3 * d + 16) // per_row
    at_head = rows_down + (wide + 1) * rows_up
    pieces = [down.total(down.terms)] + [up_block[:, i * width : (i + 1) * width] for i in range(wide)] + [out.total(out.terms)]
    split = grad_head.reshape(per_row, -1, shard)
    pieces.append(jnp.concatenate([split[i] for i in range(per_row)], axis=1))
    pieces = jnp.concatenate(pieces, axis=0)
    every = lax.all_gather(pieces, "ctx", axis=0, tiled=False)
    wqkv, pieces, outgoing = tie(wqkv, pieces, outgoing)
    if parts == 1:
        incoming = lax.all_to_all(outgoing, "ctx", 0, 0, tiled=True)
    wqkv_near = near_half(wqkv)
    wqkv_all = assemble(wqkv, wqkv_near, far_half(wqkv_near))
    token_grad = d_branch + dot(incoming.reshape(3 * width, block), wqkv_all, 0, 1)
    if parts == 1 and per_row == 2 and shard >= 3 * d:
        grad_w_down, grad_w_up, grad_w_out, grad_qkv = in_order(every, rows_down, rows_up, wide, d, shard)
        at = (3 * d) % rows_head
        sums = every[:, at_head + at, shard : shard + 3 * d].astype(F32)
    else:
        grad_w_down = sorted_rows(every[:, :rows_down]).astype(F32)
        take = lambda i: sorted_rows(every[:, rows_down + i * rows_up :][:, :rows_up]).astype(F32)
        grad_w_up = jnp.concatenate([take(i) for i in range(wide)], axis=1)
        grad_w_out = take(wide)
        every_head = every[:, at_head:]
        every_head = jnp.concatenate([every_head[:, :, i * shard : (i + 1) * shard] for i in range(per_row)], axis=1)
        every_head = every_head.astype(F32).reshape(heads, parts, 3 * d + 16, shard).sum(axis=1)
        grad_qkv = every_head[:, : 3 * d].reshape(heads, 3, d, shard).transpose(1, 3, 0, 2).reshape(3, shard, width)
        sums = every_head[:, 3 * d :]
        if shard >= 3 * d:
            sums = sums[:, 0, : 3 * d]
        else:
            sums = sums[:, : 6 * d // shard, : shard // 2]
    sums = sums.reshape(heads, 3, d).transpose(1, 0, 2).reshape(3, width)
    bias_q = cut(sums[0], row * shard, shard, 0)
    bias_v = cut(sums[2], row * shard, shard, 0)

    return (
        output[None].astype(BF),
        token_grad[None].astype(BF),
        grad_qkv[0],
        grad_qkv[1],
        grad_qkv[2],
        grad_w_out,
        bias_q,
        bias_v,
        six[0],
        six[1],
        six[2],
        grad_w_up,
        grad_b_up,
        grad_w_down,
        six[3],
        six[4],
        six[5],
    )


def solution(mesh):
    line, matrix, rows = P("fsdp"), P("fsdp", None), P("fsdp", "ctx", None)
    placed = (
        (rows, matrix) + (matrix,) * 4 + (line,) * 5 + (matrix, line, matrix) + (line,) * 3 + (rows,)
    )
    outs = (rows, rows) + (matrix,) * 4 + (line,) * 5 + (matrix, line, matrix) + (line,) * 3
    return jax.shard_map(
        functools.partial(body, mesh.shape["ctx"], mesh.shape["fsdp"]),
        mesh=mesh,
        in_specs=placed,
        out_specs=outs,
        check_vma=False,
    )
```

```python
import functools
import math

import jax
import jax.numpy as jnp
from jax import lax
from jax.experimental import pallas as pl
from jax.experimental.pallas import tpu as pltpu
from jax.sharding import PartitionSpec as P

HEADS = 16
LOG2E = 1.4426950408889634
NEG = -1e30
BF = jnp.bfloat16
F32 = jnp.float32


def layer_norm(hidden, gain, shift):
    mean = jnp.mean(hidden, axis=-1, keepdims=True)
    centred = hidden - mean
    variance = jnp.mean(centred * centred, axis=-1, keepdims=True)
    return centred * lax.rsqrt(variance + 1e-05) * gain + shift


def gelu_exact(value):
    return jax.nn.gelu(value, approximate=False)


def dot(left, right, on_left, on_right):
    return lax.dot_general(
        left, right, (((on_left,), (on_right,)), ((), ())), preferred_element_type=F32
    )


def flip(value, axis, bit, size):
    return lax.ppermute(value, axis, [(i, i ^ bit) for i in range(size)])


def forward_kernel(
    lo_ref, hi_ref, in_lo_ref, in_hi_ref, q_ref, k_ref, v_ref, start_ref, end_ref,
    out_ref, low_ref, lse_ref, total_ref, vt_ref, *, bk, scale
):
    i = pl.program_id(0)
    bq = q_ref.shape[0]

    @pl.when(i == 0)
    def _():
        @pl.loop(0, v_ref.shape[0] // bk)
        def _(j):
            at = pl.multiple_of(j * bk, bk)
            vt_ref[:, pl.ds(at, bk)] = v_ref[pl.ds(at, bk), :].T

    q = q_ref[...]
    start, end = start_ref[...], end_ref[...]
    total_ref[...] = jnp.zeros_like(total_ref)

    def step(j, carry, masked):
        peak, norm = carry
        at = pl.multiple_of(j * bk, bk)
        s = dot(k_ref[pl.ds(at, bk), :], q, 1, 1) * (scale * LOG2E)
        if masked:
            at_key = lax.broadcasted_iota(jnp.int32, (bk, bq), 0) + at
            s = jnp.where((at_key >= start) & (at_key < end), s, NEG)
        new_peak = jnp.maximum(peak, jnp.max(s, axis=0, keepdims=True))
        p = jnp.exp2(s - new_peak)
        shrink = jnp.exp2(peak - new_peak)
        norm = norm * shrink + jnp.sum(p, axis=0, keepdims=True)
        total_ref[...] = total_ref[...] * shrink + dot(vt_ref[:, pl.ds(at, bk)], p.astype(BF), 1, 0)
        return new_peak, norm

    lo, hi, in_lo, in_hi = lo_ref[i], hi_ref[i], in_lo_ref[i], in_hi_ref[i]
    carry = (jnp.full((1, bq), NEG, F32), jnp.zeros((1, bq), F32))
    carry = lax.fori_loop(in_lo, in_hi, lambda j, c: step(j, c, False), carry)
    carry = lax.fori_loop(lo, in_lo, lambda j, c: step(j, c, True), carry)
    peak, norm = lax.fori_loop(in_hi, hi, lambda j, c: step(j, c, True), carry)
    out = total_ref[...] / norm
    out_ref[...] = out
    n = low_ref.shape[2]
    for piece in range(bq // n):
        low_ref[piece] = out[:, piece * n : (piece + 1) * n].astype(low_ref.dtype)
    lse_ref[...] = peak + jnp.log2(norm)


def block_ranges(starts, ends, rows, others):
    first, last = starts.reshape(-1, rows), ends.reshape(-1, rows)
    lo = first[:, 0] // others
    hi = (last[:, -1] + others - 1) // others
    in_lo = jnp.clip((first[:, -1] + others - 1) // others, lo, hi)
    in_hi = jnp.clip(last[:, 0] // others, in_lo, hi)
    return lo, hi, in_lo, in_hi


def attention_forward(q, k, v, starts, ends, scale, n, bq=1024, bk=512):
    count, d = q.shape
    length = k.shape[0]
    bq = min(bq, count)
    ranges = block_ranges(starts, ends, bq, bk)
    row = lambda: pl.BlockSpec((1, bq), lambda i, *_: (0, i))
    whole = lambda shape: pl.BlockSpec(shape, lambda i, *_: (0, 0))
    return pl.pallas_call(
        functools.partial(forward_kernel, bk=bk, scale=scale),
        out_shape=(
            jax.ShapeDtypeStruct((d, count), F32),
            jax.ShapeDtypeStruct((count // n, d, n), BF),
            jax.ShapeDtypeStruct((1, count), F32),
        ),
        grid_spec=pltpu.PrefetchScalarGridSpec(
            num_scalar_prefetch=4,
            grid=(count // bq,),
            in_specs=[
                pl.BlockSpec((bq, d), lambda i, *_: (i, 0)),
                whole((length, d)),
                whole((length, d)),
                row(),
                row(),
            ],
            out_specs=[
                pl.BlockSpec((d, bq), lambda i, *_: (0, i)),
                pl.BlockSpec((bq // n, d, n), lambda i, *_: (i, 0, 0)),
                row(),
            ],
            scratch_shapes=[pltpu.VMEM((d, bq), F32), pltpu.VMEM((d, length), BF)],
        ),
        compiler_params=pltpu.CompilerParams(vmem_limit_bytes=40 << 20),
        cost_estimate=pl.CostEstimate(
            flops=16 * count * length * d, bytes_accessed=length * d * 16, transcendentals=count * length
        ),
        name="attention_forward",
    )(*ranges, q, k, v, starts[None], ends[None])


def backward_kernel(
    lo_ref, hi_ref, in_lo_ref, in_hi_ref, k_ref, v_ref, q_ref, do_ref, lse_ref, delta_ref, start_ref,
    end_ref, dqt_in_ref, dkt_ref, dvt_ref, dqt_ref, dk_sum, dv_sum, *, bq, scale, base
):
    j = pl.program_id(0) + base
    bk = k_ref.shape[0]
    pieces = bq // do_ref.shape[2]

    @pl.when(pl.program_id(0) == 0)
    def _():
        dqt_ref[...] = dqt_in_ref[...]

    k, v = k_ref[...], v_ref[...]
    kt = k.T
    dk_sum[...] = jnp.zeros_like(dk_sum)
    dv_sum[...] = jnp.zeros_like(dv_sum)

    def step(i, masked):
        at = pl.multiple_of(i * bq, bq)
        row = pl.ds(at, bq)
        q = q_ref[row, :]
        do_t = jnp.concatenate([do_ref[i * pieces + n] for n in range(pieces)], axis=1)
        s = dot(k, q, 1, 1) * (scale * LOG2E) - lse_ref[:, row]
        if masked:
            at_key = lax.broadcasted_iota(jnp.int32, (bk, bq), 0) + j * bk
            s = jnp.where((at_key >= start_ref[:, row]) & (at_key < end_ref[:, row]), s, NEG)
        p = jnp.exp2(s)
        dp = dot(v, do_t, 1, 0)
        dv_sum[...] += dot(p.astype(BF), do_t, 1, 1)
        ds = (p * (dp - delta_ref[:, row])).astype(BF)
        dk_sum[...] += dot(ds, q, 1, 0)
        dqt_ref[:, row] += dot(kt, ds, 1, 0)

    lo, hi, in_lo, in_hi = lo_ref[j], hi_ref[j], in_lo_ref[j], in_hi_ref[j]
    pl.loop(in_lo, in_hi)(lambda i: step(i, False))
    pl.loop(lo, in_lo)(lambda i: step(i, True))
    pl.loop(in_hi, hi)(lambda i: step(i, True))
    dkt_ref[...] = (dk_sum[...] * scale).T.astype(dkt_ref.dtype)
    dvt_ref[...] = dv_sum[...].T.astype(dvt_ref.dtype)


def attention_backward(q, k, v, do_t, lse, delta, starts, ends, ranges, dqt, scale, bq, bk, base, blocks):
    count, d = q.shape
    whole = lambda shape: pl.BlockSpec(shape, lambda j, *_: (0,) * len(shape))
    keys = lambda: pl.BlockSpec((bk, d), lambda j, *_: (j + base, 0))
    columns = lambda: pl.BlockSpec((d, bk), lambda j, *_: (0, j))
    return pl.pallas_call(
        functools.partial(backward_kernel, bq=bq, scale=scale, base=base),
        out_shape=(
            jax.ShapeDtypeStruct((d, blocks * bk), BF),
            jax.ShapeDtypeStruct((d, blocks * bk), BF),
            jax.ShapeDtypeStruct((d, count), F32),
        ),
        grid_spec=pltpu.PrefetchScalarGridSpec(
            num_scalar_prefetch=4,
            grid=(blocks,),
            in_specs=[
                keys(),
                keys(),
                whole((count, d)),
                whole(do_t.shape),
                whole((1, count)),
                whole((1, count)),
                whole((1, count)),
                whole((1, count)),
                whole((d, count)),
            ],
            out_specs=[columns(), columns(), whole((d, count))],
            scratch_shapes=[pltpu.VMEM((bk, d), F32), pltpu.VMEM((bk, d), F32)],
        ),
        compiler_params=pltpu.CompilerParams(vmem_limit_bytes=32 << 20),
        cost_estimate=pl.CostEstimate(
            flops=count * d, bytes_accessed=count * d, transcendentals=0
        ),
        name="attention_backward",
    )(*ranges, k, v, q, do_t, lse, delta, starts[None], ends[None], dqt)


class Halving:
    def __init__(self, place, sizes):
        self.place, self.sizes, self.terms = list(place), sizes, []

    def own(self, step):
        return (lax.axis_index(step[0]) // step[1]) % 2

    def share(self, step, which):
        at = self.place.index(step)
        return [lax.dynamic_index_in_dim(t, which, at, keepdims=False) for t in self.terms]

    def total(self, terms):
        return sum((t.astype(F32) for t in terms[1:]), terms[0].astype(F32)).astype(BF)

    def send(self, step):
        sent = self.total(self.share(step, 1 - self.own(step)))
        self.terms = self.share(step, self.own(step))
        self.place.remove(step)
        return sent

    def receive(self, got):
        self.terms.append(got)


def reversed_bits(i, count):
    n = count.bit_length() - 1
    return sum(((i // (1 << b)) % 2) * (1 << (n - 1 - b)) for b in range(n))


def order_kernel(every_ref, down_ref, up_ref, out_ref, query_ref, key_ref, value_ref, *, rows, wide, d, shard):
    rows_down, width = down_ref.shape[2:]
    starts = [rows_down + i * rows for i in range(wide + 2)]
    halves = []
    for half in range(2):
        down_ref[half, 0] = every_ref[half, :rows_down, :].astype(F32)
        for i in range(wide):
            slab = every_ref[half, starts[i] : starts[i + 1], :]
            up_ref[half, 0, :, i * width : (i + 1) * width] = slab.astype(F32)
        out_ref[half, 0] = every_ref[half, starts[wide] : starts[wide + 1], :].astype(F32)
        both = every_ref[half, starts[wide + 1] :, :].astype(F32)
        halves.append(jnp.concatenate([both[:, :shard], both[:, shard:]], axis=0))
    for t, ref in enumerate((query_ref, key_ref, value_ref)):
        pair = jnp.concatenate([h[t * d : (t + 1) * d] for h in halves], axis=0)
        ref[...] = pair.T


def in_order(every, rows_down, rows, wide, d, shard):
    n, whole, width = every.shape
    place = lambda i: (0, reversed_bits(i, n // 2), 0, 0)
    down, up, out, *qkv = pl.pallas_call(
        functools.partial(order_kernel, rows=rows, wide=wide, d=d, shard=shard),
        out_shape=(
            jax.ShapeDtypeStruct((2, n // 2, rows_down, width), F32),
            jax.ShapeDtypeStruct((2, n // 2, rows, wide * width), F32),
            jax.ShapeDtypeStruct((2, n // 2, rows, width), F32),
        )
        + (jax.ShapeDtypeStruct((shard, n * d), F32),) * 3,
        grid=(n // 2,),
        in_specs=[pl.BlockSpec((2, whole, width), lambda i: (i, 0, 0))],
        out_specs=[
            pl.BlockSpec((2, 1, rows_down, width), place),
            pl.BlockSpec((2, 1, rows, wide * width), place),
            pl.BlockSpec((2, 1, rows, width), place),
        ]
        + [pl.BlockSpec((shard, 2 * d), lambda i: (0, i))] * 3,
        compiler_params=pltpu.CompilerParams(vmem_limit_bytes=32 << 20),
        cost_estimate=pl.CostEstimate(flops=0, bytes_accessed=6 * every.size, transcendentals=0),
        name="in_order",
    )(every)
    return down.reshape(n * rows_down, width), up.reshape(n * rows, wide * width), out.reshape(n * rows, width), qkv


def body(ctx, fsdp, tokens, segments, w_query, w_key, w_value, w_out, b_query, b_value, b_out, gain_one, shift_one,
         w_up, b_up, w_down, b_down, gain_two, shift_two, cotangent):
    _, block, width = tokens.shape
    heads = HEADS
    d = width // heads
    scale = 1.0 / math.sqrt(d)
    parts = ctx // heads
    mine = block // parts
    length = ctx * block
    count = length // parts
    hidden = w_up.shape[1]
    shard = w_query.shape[0]
    me = lax.axis_index("ctx")
    row = lax.axis_index("fsdp")
    head, part = me // parts, me % parts
    core = me % 2
    cut = lambda a, at, size, axis: lax.dynamic_slice_in_dim(a, at, size, axis)

    bits = lambda n: [1 << i for i in range(n.bit_length() - 1)]
    sizes = {"fsdp": fsdp, "ctx": ctx}
    tie = lambda *arrays: lax.optimization_barrier(arrays)

    def gather_small(a):
        if fsdp == 2:
            other = flip(a, "fsdp", 1, 2)
            return jnp.concatenate([jnp.where(row == 0, a, other), jnp.where(row == 0, other, a)], axis=0)
        return lax.all_gather(a, "fsdp", axis=0, tiled=True)

    def near_half(w):
        if fsdp != 2:
            return lax.all_gather(w, "fsdp", axis=0, tiled=True)
        return flip(cut(w, core * (w.shape[0] // 2), w.shape[0] // 2, 0), "fsdp", 1, 2)

    def far_half(near):
        return flip(near, "ctx", 1, ctx) if fsdp == 2 else near

    def assemble(w, near, far):
        if fsdp != 2:
            return near
        rows, half = w.shape[0], w.shape[0] // 2
        whole = jnp.zeros((2 * rows, w.shape[1]), w.dtype)
        whole = lax.dynamic_update_slice_in_dim(whole, w, row * rows, 0)
        whole = lax.dynamic_update_slice_in_dim(whole, near, (1 - row) * rows + core * half, 0)
        return lax.dynamic_update_slice_in_dim(whole, far, (1 - row) * rows + (1 - core) * half, 0)

    def move(send, step):
        return flip(send, step[0], step[1], sizes[step[0]])

    core_step = ("ctx", 1)
    every_place = [("fsdp", b) for b in reversed(bits(fsdp))] + [("ctx", b) for b in bits(ctx)]
    own_bit = lambda step: (lax.axis_index(step[0]) // step[1]) % 2

    def columns_of(left, chosen):
        depth = max(every_place.index(step) for step in chosen) + 1
        size = left.shape[1] >> depth
        offsets = [0]
        for level, step in enumerate(every_place[:depth]):
            stride = left.shape[1] >> (level + 1)
            options = [chosen[step]] if step in chosen else [0, 1]
            offsets = [at + which * stride for at in offsets for which in options]
        return jnp.concatenate([cut(left, at, size, 1) for at in offsets], axis=1)

    def blocks(rows_data, place):
        return rows_data.reshape([2] * len(place) + [-1, rows_data.shape[1]])

    def first_share(left, right):
        return dot(columns_of(left, {core_step: 1 - own_bit(core_step)}), right, 0, 0).astype(BF)

    def second_share(left, right, got, step):
        place = [p for p in every_place if p != core_step]
        got = blocks(got, place)
        inner = [p for p in place if p != step]
        parts_of = []
        for which in (1 - own_bit(step), own_bit(step)):
            rows_data = dot(columns_of(left, {core_step: own_bit(core_step), step: which}), right, 0, 0)
            added = lax.dynamic_index_in_dim(got, which, place.index(step), keepdims=False)
            parts_of.append((blocks(rows_data, inner) + added.astype(F32)).astype(BF))
        rest = Halving(inner, sizes)
        rest.terms = [parts_of[1]]
        return parts_of[0], rest

    def sorted_rows(every):
        n = len(bits(ctx))
        shape = every.shape
        every = every.reshape((2,) * n + shape[1:]).transpose(list(reversed(range(n))) + [n, n + 1])
        return every.reshape(-1, shape[2])

    inputs = tokens[0]
    everyone = lax.all_gather(inputs, "ctx", axis=0, tiled=True)
    by_head = lambda w: w.reshape(shard, heads, 1, d)
    wqkv = jnp.concatenate([by_head(w) for w in (w_query, w_key, w_value)], axis=2).reshape(shard, 3 * width)
    small = jnp.stack([b_query, b_value, b_out, gain_one, shift_one, b_down, gain_two, shift_two])
    small = jnp.concatenate([small.reshape(-1), b_up])[None]
    w_head = gather_small(jnp.concatenate([cut(w, head * d, d, 1) for w in (w_query, w_key, w_value)], axis=1))
    small = gather_small(small)
    wo_near = near_half(w_out)
    wu_near = near_half(w_up)
    wo_near, w_head, small = tie(wo_near, w_head, small)
    wo = assemble(w_out, wo_near, far_half(wo_near))
    wu_near, w_down, wo = tie(wu_near, w_down, wo)
    wd_near = near_half(w_down)
    wu_far = far_half(wu_near)
    everyone, wu_near = tie(everyone, wu_near)

    eight = small[:, : 8 * shard].reshape(-1, 8, shard).transpose(1, 0, 2).reshape(8, width).astype(F32)
    bq_, bv_, bo, gain1, shift1, bd, gain2, shift2 = (eight[i] for i in range(8))
    bu = small[:, 8 * shard :].reshape(hidden).astype(F32)
    projected = dot(everyone, w_head, 1, 0)
    my_bias = jnp.concatenate([cut(bq_, head * d, d, 0), jnp.zeros((d,), F32), cut(bv_, head * d, d, 0)])
    projected = (projected + my_bias).astype(BF)
    own_part = lambda a: cut(a.reshape((ctx, block) + a.shape[1:]), part * mine, mine, 1).reshape(
        (count,) + a.shape[1:]
    )
    q = own_part(projected[:, :d])
    k, v = projected[:, d : 2 * d], projected[:, 2 * d :]
    seg = segments[0]
    starts_all = jnp.sum(seg[None, :] < seg[:, None], axis=1, dtype=jnp.int32)
    ends_all = jnp.sum(seg[None, :] <= seg[:, None], axis=1, dtype=jnp.int32)
    starts, ends = own_part(starts_all), own_part(ends_all)

    attended_t, outgoing, lse = attention_forward(q, k, v, starts, ends, scale, mine)
    incoming = lax.all_to_all(outgoing, "ctx", 0, 0, tiled=True)
    wu_far, outgoing, wu_near = tie(wu_far, outgoing, wu_near)
    wu = assemble(w_up, wu_near, wu_far)
    incoming, wu = tie(incoming, wu)
    attended = incoming.reshape(heads, parts, d, mine).transpose(1, 3, 0, 2).reshape(block, width)
    branch = dot(attended, wo, 1, 0) + bo
    first, first_pull = jax.vjp(layer_norm, inputs.astype(F32) + branch, gain1, shift1)
    first_low, wd_near = tie(first.astype(BF), wd_near)
    wd = assemble(w_down, wd_near, far_half(wd_near))
    hidden_pre = dot(first_low, wu, 1, 0) + bu
    active, active_pull = jax.vjp(gelu_exact, hidden_pre)
    (slope,) = active_pull(jnp.ones_like(active))
    active_low, slope = tie(active.astype(BF), slope)
    second = dot(active_low, wd, 1, 0) + bd
    output, out_pull = jax.vjp(layer_norm, first + second, gain2, shift2)

    fsdp_steps = [("fsdp", b) for b in reversed(bits(fsdp))]
    ctx_steps = [("ctx", b) for b in bits(ctx) if b > 1]
    down_order = fsdp_steps + ctx_steps
    up_order = ctx_steps[1:2] + fsdp_steps + ctx_steps[:1] + ctx_steps[2:]
    out_order = ctx_steps[:1] + fsdp_steps + ctx_steps[1:]
    d_second, grad_gain_two, grad_shift_two = out_pull(cotangent[0].astype(F32))
    d_second_low = d_second.astype(BF)
    down_sent = first_share(active_low, d_second_low)
    down_sent, d_second_low = tie(down_sent, d_second_low)
    down_got = move(down_sent, core_step)
    d_hidden = dot(d_second_low, wd, 1, 1) * slope
    d_hidden_low = d_hidden.astype(BF)
    up_sent = first_share(first_low, d_hidden_low)
    up_sent, d_hidden_low, down_got = tie(up_sent, d_hidden_low, down_got)
    up_got = move(up_sent, core_step)
    down_sent, down = second_share(active_low, d_second_low, down_got, down_order[0])
    down_sent, d_hidden_low = tie(down_sent, d_hidden_low)
    down_got = move(down_sent, down_order[0])
    d_first = d_second + dot(d_hidden_low, wu, 1, 1)
    d_branch, grad_gain_one, grad_shift_one = first_pull(d_first)
    d_branch_low = d_branch.astype(BF)
    d_attended_t = dot(wo, d_branch_low, 1, 1).astype(BF)
    outgoing = d_attended_t.reshape(heads, d, parts, mine).transpose(0, 2, 1, 3).reshape(ctx, d, mine)
    do_t = lax.all_to_all(outgoing, "ctx", 0, 0, tiled=True)
    outgoing, d_branch_low, up_got = tie(outgoing, d_branch_low, up_got)
    out_sent = first_share(attended, d_branch_low)
    out_sent, d_hidden_low = tie(out_sent, d_hidden_low)
    out_got = move(out_sent, core_step)
    up_sent, up = second_share(first_low, d_hidden_low, up_got, up_order[0])
    up_sent, out_got = tie(up_sent, out_got)
    out_sent, out = second_share(attended, d_branch_low, out_got, out_order[0])
    vectors = [
        jnp.sum(d_branch, axis=0), grad_gain_one, grad_shift_one, jnp.sum(d_second, axis=0), grad_gain_two,
        grad_shift_two,
    ]
    vectors = jnp.concatenate(
        [jnp.stack(vectors).reshape(6, fsdp, shard).transpose(1, 0, 2).reshape(fsdp, -1),
         jnp.sum(d_hidden, axis=0).reshape(fsdp, -1)], axis=1,
    )
    vectors = lax.all_gather(vectors, ("ctx", "fsdp"), axis=0, tiled=False)
    do_t, up_sent, out_sent, down.terms[0], up.terms[0], out.terms[0] = tie(
        do_t, up_sent, out_sent, down.terms[0], up.terms[0], out.terms[0]
    )
    up_got, out_got = move(up_sent, up_order[0]), move(out_sent, out_order[0])

    delta = jnp.sum(
        attended_t.reshape(d, ctx, mine) * do_t.transpose(1, 0, 2).astype(F32), axis=0
    ).reshape(1, count)
    bq, bk = min(512, count), 512
    ranges = block_ranges(starts_all, ends_all, bk, bq * parts)
    calls = 4
    per_call = length // bk // calls
    dqt = jnp.zeros((d, count), F32)
    dkt, dvt = [], []
    down_left, up_left, out_left = down_order[1:], up_order[1:], out_order[1:]

    def one_step(one, left, got):
        one.receive(got)
        step = left.pop(0)
        sent = one.send(step)
        return sent, move(sent, step)

    def both_step():
        step = down_left.pop(0)
        sent = jnp.concatenate([down.send(step), out.send(step)], axis=-2)
        return sent, move(sent, step)

    def both_receive(got):
        rows = down.terms[0].shape[-2]
        down.receive(got[..., :rows, :])
        out.receive(got[..., rows:, :])

    for call in range(calls):
        dk_new, dv_new, dqt = attention_backward(
            q, k, v, do_t, lse, delta, starts, ends, ranges, dqt, scale, bq, bk, call * per_call, per_call
        )
        dkt.append(dk_new)
        dvt.append(dv_new)
        if call == 0:
            dqt, out_got = tie(dqt, out_got)
            while len(out_left) >= len(ctx_steps):
                out_sent, out_got = one_step(out, out_left, out_got)
            dqt, out_sent = tie(dqt, out_sent)
        if call == 1:
            dqt, down_got = tie(dqt, down_got)
            while len(down_left) >= len(ctx_steps):
                down_sent, down_got = one_step(down, down_left, down_got)
            dqt, down_sent = tie(dqt, down_sent)
        if call == 2:
            dqt, up_got, vectors = tie(dqt, up_got, vectors)
            up_sent, up_got = one_step(up, up_left, up_got)
            dqt, up_sent = tie(dqt, up_sent)

    dkt, dvt = jnp.concatenate(dkt, axis=1), jnp.concatenate(dvt, axis=1)
    dqt = (dqt * scale).astype(BF)
    if parts == 1:
        dqkv_t = jnp.concatenate([dqt, dkt, dvt], axis=0)
        outgoing = dqkv_t.reshape(3 * d, ctx, block).transpose(1, 0, 2)
        incoming = lax.all_to_all(outgoing, "ctx", 0, 0, tiled=True)
        outgoing, dqkv_t, down_got, out_got = tie(outgoing, dqkv_t, down_got, out_got)
        down.receive(down_got)
        out.receive(out_got)
        down_sent, down_got = both_step()
        dqkv_t, down_sent = tie(dqkv_t, down_sent)
        grad_head = dot(dqkv_t, everyone, 1, 0)
        sums = jnp.sum(dqkv_t.astype(F32), axis=1)
    else:
        dqt, down_got, out_got = tie(dqt, down_got, out_got)
        down.receive(down_got)
        out.receive(out_got)
        down_sent, down_got = both_step()
        dqt, down_sent = tie(dqt, down_sent)
        back = lambda a: lax.all_to_all(
            a.reshape(d, ctx, -1).transpose(1, 0, 2), "ctx", 0, 0, tiled=True
        ).reshape(heads, parts, d, -1)
        summed = lambda a: jnp.sum(back(a).astype(F32), axis=1).astype(BF)
        incoming = jnp.stack([back(dqt).transpose(0, 2, 1, 3).reshape(heads, d, block), summed(dkt), summed(dvt)], axis=1)
        grad_head = jnp.concatenate([dot(dqt, own_part(everyone), 1, 0), dot(dkt, everyone, 1, 0), dot(dvt, everyone, 1, 0)])
        sums = jnp.concatenate([jnp.sum(a.astype(F32), axis=1) for a in (dqt, dkt, dvt)])
    grad_head = grad_head.reshape(3 * d, fsdp, shard).transpose(1, 0, 2)
    extra = jnp.pad(sums[None, None], ((0, 0), (0, 15), (0, shard - 3 * d))) if shard >= 3 * d else jnp.pad(
        sums.reshape(1, -1, shard // 2), ((0, 0), (0, 16 - 6 * d // shard), (0, shard // 2))
    )
    grad_head = jnp.concatenate([grad_head, jnp.broadcast_to(extra, (fsdp, 16, shard))], axis=1)
    for step in fsdp_steps:
        pair = grad_head.reshape(2, -1, 3 * d + 16, shard)
        sent = lax.dynamic_index_in_dim(pair, 1 - own_bit(step), 0, keepdims=False).astype(BF)
        kept = lax.dynamic_index_in_dim(pair, own_bit(step), 0, keepdims=False)
        if step == fsdp_steps[0]:
            down_got, sent = tie(down_got, sent)
        grad_head = kept + move(sent, step).astype(F32)
    grad_head = grad_head[0].astype(BF)

    both_receive(down_got)
    while down_left:
        down_sent, down_got = both_step()
        if len(up_left) > 1:
            up_got, down_sent = tie(up_got, down_sent)
            up_sent, up_got = one_step(up, up_left, up_got)
            down_got, up_sent = tie(down_got, up_sent)
        if down_left:
            both_receive(down_got)
    up_got, grad_head = tie(up_got, grad_head)
    while up_left:
        up_sent, up_got = one_step(up, up_left, up_got)
    down_got, up_sent = tie(down_got, up_sent)
    both_receive(down_got)
    up_got, incoming = tie(up_got, incoming)
    up.receive(up_got)
    vectors = jnp.sum(lax.dynamic_index_in_dim(vectors, row, 1, keepdims=False), axis=0)
    six = vectors[: 6 * shard].reshape(6, shard)
    grad_b_up = vectors[6 * shard :]

    up_block = up.total(up.terms)
    rows_up, rows_down = up_block.shape[0], down.terms[0].shape[0]
    wide = hidden // width
    per_row = width // shard
    rows_head = (3 * d + 16) // per_row
    at_head = rows_down + (wide + 1) * rows_up
    pieces = [down.total(down.terms)] + [up_block[:, i * width : (i + 1) * width] for i in range(wide)] + [out.total(out.terms)]
    split = grad_head.reshape(per_row, -1, shard)
    pieces.append(jnp.concatenate([split[i] for i in range(per_row)], axis=1))
    pieces = jnp.concatenate(pieces, axis=0)
    every = lax.all_gather(pieces, "ctx", axis=0, tiled=False)
    wqkv, pieces = tie(wqkv, pieces)
    wqkv_near = near_half(wqkv)
    wqkv_all = assemble(wqkv, wqkv_near, far_half(wqkv_near))
    token_grad = d_branch + dot(incoming.reshape(3 * width, block), wqkv_all, 0, 1)
    if parts == 1 and per_row == 2 and shard >= 3 * d:
        grad_w_down, grad_w_up, grad_w_out, grad_qkv = in_order(every, rows_down, rows_up, wide, d, shard)
        at = (3 * d) % rows_head
        sums = every[:, at_head + at, shard : shard + 3 * d].astype(F32)
    else:
        grad_w_down = sorted_rows(every[:, :rows_down]).astype(F32)
        take = lambda i: sorted_rows(every[:, rows_down + i * rows_up :][:, :rows_up]).astype(F32)
        grad_w_up = jnp.concatenate([take(i) for i in range(wide)], axis=1)
        grad_w_out = take(wide)
        every_head = every[:, at_head:]
        every_head = jnp.concatenate([every_head[:, :, i * shard : (i + 1) * shard] for i in range(per_row)], axis=1)
        every_head = every_head.astype(F32).reshape(heads, parts, 3 * d + 16, shard).sum(axis=1)
        grad_qkv = every_head[:, : 3 * d].reshape(heads, 3, d, shard).transpose(1, 3, 0, 2).reshape(3, shard, width)
        sums = every_head[:, 3 * d :]
        if shard >= 3 * d:
            sums = sums[:, 0, : 3 * d]
        else:
            sums = sums[:, : 6 * d // shard, : shard // 2]
    sums = sums.reshape(heads, 3, d).transpose(1, 0, 2).reshape(3, width)
    bias_q = cut(sums[0], row * shard, shard, 0)
    bias_v = cut(sums[2], row * shard, shard, 0)

    return (
        output[None].astype(BF),
        token_grad[None].astype(BF),
        grad_qkv[0],
        grad_qkv[1],
        grad_qkv[2],
        grad_w_out,
        bias_q,
        bias_v,
        six[0],
        six[1],
        six[2],
        grad_w_up,
        grad_b_up,
        grad_w_down,
        six[3],
        six[4],
        six[5],
    )


def solution(mesh):
    line, matrix, rows = P("fsdp"), P("fsdp", None), P("fsdp", "ctx", None)
    placed = (
        (rows, matrix) + (matrix,) * 4 + (line,) * 5 + (matrix, line, matrix) + (line,) * 3 + (rows,)
    )
    outs = (rows, rows) + (matrix,) * 4 + (line,) * 5 + (matrix, line, matrix) + (line,) * 3
    return jax.shard_map(
        functools.partial(body, mesh.shape["ctx"], mesh.shape["fsdp"]),
        mesh=mesh,
        in_specs=placed,
        out_specs=outs,
        check_vma=False,
    )
```

```python
import functools
import math

import jax
import jax.numpy as jnp
from jax import lax
from jax.experimental import pallas as pl
from jax.experimental.pallas import tpu as pltpu
from jax.sharding import PartitionSpec as P

HEADS = 16
LOG2E = 1.4426950408889634
NEG = -1e30
BF = jnp.bfloat16
F32 = jnp.float32


def layer_norm(hidden, gain, shift):
    mean = jnp.mean(hidden, axis=-1, keepdims=True)
    centred = hidden - mean
    variance = jnp.mean(centred * centred, axis=-1, keepdims=True)
    return centred * lax.rsqrt(variance + 1e-05) * gain + shift


def gelu_exact(value):
    return jax.nn.gelu(value, approximate=False)


def dot(left, right, on_left, on_right):
    return lax.dot_general(
        left, right, (((on_left,), (on_right,)), ((), ())), preferred_element_type=F32
    )


def flip(value, axis, bit, size):
    return lax.ppermute(value, axis, [(i, i ^ bit) for i in range(size)])


def forward_kernel(
    lo_ref, hi_ref, in_lo_ref, in_hi_ref, q_ref, k_ref, v_ref, start_ref, end_ref,
    out_ref, low_ref, lse_ref, total_ref, vt_ref, *, bk, scale
):
    i = pl.program_id(0)
    bq = q_ref.shape[0]

    @pl.when(i == 0)
    def _():
        @pl.loop(0, v_ref.shape[0] // bk)
        def _(j):
            at = pl.multiple_of(j * bk, bk)
            vt_ref[:, pl.ds(at, bk)] = v_ref[pl.ds(at, bk), :].T

    q = q_ref[...]
    start, end = start_ref[...], end_ref[...]
    total_ref[...] = jnp.zeros_like(total_ref)

    def step(j, carry, masked):
        peak, norm = carry
        at = pl.multiple_of(j * bk, bk)
        s = dot(k_ref[pl.ds(at, bk), :], q, 1, 1) * (scale * LOG2E)
        if masked:
            at_key = lax.broadcasted_iota(jnp.int32, (bk, bq), 0) + at
            s = jnp.where((at_key >= start) & (at_key < end), s, NEG)
        new_peak = jnp.maximum(peak, jnp.max(s, axis=0, keepdims=True))
        p = jnp.exp2(s - new_peak)
        shrink = jnp.exp2(peak - new_peak)
        norm = norm * shrink + jnp.sum(p, axis=0, keepdims=True)
        total_ref[...] = total_ref[...] * shrink + dot(vt_ref[:, pl.ds(at, bk)], p.astype(BF), 1, 0)
        return new_peak, norm

    lo, hi, in_lo, in_hi = lo_ref[i], hi_ref[i], in_lo_ref[i], in_hi_ref[i]
    carry = (jnp.full((1, bq), NEG, F32), jnp.zeros((1, bq), F32))
    carry = lax.fori_loop(in_lo, in_hi, lambda j, c: step(j, c, False), carry)
    carry = lax.fori_loop(lo, in_lo, lambda j, c: step(j, c, True), carry)
    peak, norm = lax.fori_loop(in_hi, hi, lambda j, c: step(j, c, True), carry)
    out = total_ref[...] / norm
    out_ref[...] = out
    n = low_ref.shape[2]
    for piece in range(bq // n):
        low_ref[piece] = out[:, piece * n : (piece + 1) * n].astype(low_ref.dtype)
    lse_ref[...] = peak + jnp.log2(norm)


def block_ranges(starts, ends, rows, others):
    first, last = starts.reshape(-1, rows), ends.reshape(-1, rows)
    lo = first[:, 0] // others
    hi = (last[:, -1] + others - 1) // others
    in_lo = jnp.clip((first[:, -1] + others - 1) // others, lo, hi)
    in_hi = jnp.clip(last[:, 0] // others, in_lo, hi)
    return lo, hi, in_lo, in_hi


def attention_forward(q, k, v, starts, ends, scale, n, bq=1024, bk=512):
    count, d = q.shape
    length = k.shape[0]
    bq = min(bq, count)
    ranges = block_ranges(starts, ends, bq, bk)
    row = lambda: pl.BlockSpec((1, bq), lambda i, *_: (0, i))
    whole = lambda shape: pl.BlockSpec(shape, lambda i, *_: (0, 0))
    return pl.pallas_call(
        functools.partial(forward_kernel, bk=bk, scale=scale),
        out_shape=(
            jax.ShapeDtypeStruct((d, count), F32),
            jax.ShapeDtypeStruct((count // n, d, n), BF),
            jax.ShapeDtypeStruct((1, count), F32),
        ),
        grid_spec=pltpu.PrefetchScalarGridSpec(
            num_scalar_prefetch=4,
            grid=(count // bq,),
            in_specs=[
                pl.BlockSpec((bq, d), lambda i, *_: (i, 0)),
                whole((length, d)),
                whole((length, d)),
                row(),
                row(),
            ],
            out_specs=[
                pl.BlockSpec((d, bq), lambda i, *_: (0, i)),
                pl.BlockSpec((bq // n, d, n), lambda i, *_: (i, 0, 0)),
                row(),
            ],
            scratch_shapes=[pltpu.VMEM((d, bq), F32), pltpu.VMEM((d, length), BF)],
        ),
        compiler_params=pltpu.CompilerParams(vmem_limit_bytes=40 << 20),
        cost_estimate=pl.CostEstimate(
            flops=16 * count * length * d, bytes_accessed=length * d * 16, transcendentals=count * length
        ),
        name="attention_forward",
    )(*ranges, q, k, v, starts[None], ends[None])


def backward_kernel(
    lo_ref, hi_ref, in_lo_ref, in_hi_ref, k_ref, v_ref, q_ref, do_ref, lse_ref, delta_ref, start_ref,
    end_ref, dqt_in_ref, dkt_ref, dvt_ref, dqt_ref, dk_sum, dv_sum, *, bq, scale, base
):
    j = pl.program_id(0) + base
    bk = k_ref.shape[0]
    pieces = bq // do_ref.shape[2]

    @pl.when(pl.program_id(0) == 0)
    def _():
        dqt_ref[...] = dqt_in_ref[...]

    k, v = k_ref[...], v_ref[...]
    kt = k.T
    dk_sum[...] = jnp.zeros_like(dk_sum)
    dv_sum[...] = jnp.zeros_like(dv_sum)

    def step(i, masked):
        at = pl.multiple_of(i * bq, bq)
        row = pl.ds(at, bq)
        q = q_ref[row, :]
        do_t = jnp.concatenate([do_ref[i * pieces + n] for n in range(pieces)], axis=1)
        s = dot(k, q, 1, 1) * (scale * LOG2E) - lse_ref[:, row]
        if masked:
            at_key = lax.broadcasted_iota(jnp.int32, (bk, bq), 0) + j * bk
            s = jnp.where((at_key >= start_ref[:, row]) & (at_key < end_ref[:, row]), s, NEG)
        p = jnp.exp2(s)
        dp = dot(v, do_t, 1, 0)
        dv_sum[...] += dot(p.astype(BF), do_t, 1, 1)
        ds = (p * (dp - delta_ref[:, row])).astype(BF)
        dk_sum[...] += dot(ds, q, 1, 0)
        dqt_ref[:, row] += dot(kt, ds, 1, 0)

    lo, hi, in_lo, in_hi = lo_ref[j], hi_ref[j], in_lo_ref[j], in_hi_ref[j]
    pl.loop(in_lo, in_hi)(lambda i: step(i, False))
    pl.loop(lo, in_lo)(lambda i: step(i, True))
    pl.loop(in_hi, hi)(lambda i: step(i, True))
    dkt_ref[...] = (dk_sum[...] * scale).T.astype(dkt_ref.dtype)
    dvt_ref[...] = dv_sum[...].T.astype(dvt_ref.dtype)


def attention_backward(q, k, v, do_t, lse, delta, starts, ends, ranges, dqt, scale, bq, bk, base, blocks):
    count, d = q.shape
    whole = lambda shape: pl.BlockSpec(shape, lambda j, *_: (0,) * len(shape))
    keys = lambda: pl.BlockSpec((bk, d), lambda j, *_: (j + base, 0))
    columns = lambda: pl.BlockSpec((d, bk), lambda j, *_: (0, j))
    return pl.pallas_call(
        functools.partial(backward_kernel, bq=bq, scale=scale, base=base),
        out_shape=(
            jax.ShapeDtypeStruct((d, blocks * bk), BF),
            jax.ShapeDtypeStruct((d, blocks * bk), BF),
            jax.ShapeDtypeStruct((d, count), F32),
        ),
        grid_spec=pltpu.PrefetchScalarGridSpec(
            num_scalar_prefetch=4,
            grid=(blocks,),
            in_specs=[
                keys(),
                keys(),
                whole((count, d)),
                whole(do_t.shape),
                whole((1, count)),
                whole((1, count)),
                whole((1, count)),
                whole((1, count)),
                whole((d, count)),
            ],
            out_specs=[columns(), columns(), whole((d, count))],
            scratch_shapes=[pltpu.VMEM((bk, d), F32), pltpu.VMEM((bk, d), F32)],
        ),
        compiler_params=pltpu.CompilerParams(vmem_limit_bytes=32 << 20),
        cost_estimate=pl.CostEstimate(
            flops=count * d, bytes_accessed=count * d, transcendentals=0
        ),
        name="attention_backward",
    )(*ranges, k, v, q, do_t, lse, delta, starts[None], ends[None], dqt)


class Halving:
    def __init__(self, place, sizes):
        self.place, self.sizes, self.terms = list(place), sizes, []

    def own(self, step):
        return (lax.axis_index(step[0]) // step[1]) % 2

    def share(self, step, which):
        at = self.place.index(step)
        return [lax.dynamic_index_in_dim(t, which, at, keepdims=False) for t in self.terms]

    def total(self, terms):
        return sum((t.astype(F32) for t in terms[1:]), terms[0].astype(F32)).astype(BF)

    def send(self, step):
        sent = self.total(self.share(step, 1 - self.own(step)))
        self.terms = self.share(step, self.own(step))
        self.place.remove(step)
        return sent

    def receive(self, got):
        self.terms.append(got)


def reversed_bits(i, count):
    n = count.bit_length() - 1
    return sum(((i // (1 << b)) % 2) * (1 << (n - 1 - b)) for b in range(n))


def order_kernel(every_ref, down_ref, up_ref, out_ref, query_ref, key_ref, value_ref, *, rows, wide, d, shard):
    rows_down, width = down_ref.shape[2:]
    starts = [rows_down + i * rows for i in range(wide + 2)]
    halves = []
    for half in range(2):
        down_ref[half, 0] = every_ref[half, :rows_down, :].astype(F32)
        for i in range(wide):
            slab = every_ref[half, starts[i] : starts[i + 1], :]
            up_ref[half, 0, :, i * width : (i + 1) * width] = slab.astype(F32)
        out_ref[half, 0] = every_ref[half, starts[wide] : starts[wide + 1], :].astype(F32)
        both = every_ref[half, starts[wide + 1] :, :].astype(F32)
        halves.append(jnp.concatenate([both[:, :shard], both[:, shard:]], axis=0))
    for t, ref in enumerate((query_ref, key_ref, value_ref)):
        pair = jnp.concatenate([h[t * d : (t + 1) * d] for h in halves], axis=0)
        ref[...] = pair.T


def in_order(every, rows_down, rows, wide, d, shard):
    n, whole, width = every.shape
    place = lambda i: (0, reversed_bits(i, n // 2), 0, 0)
    down, up, out, *qkv = pl.pallas_call(
        functools.partial(order_kernel, rows=rows, wide=wide, d=d, shard=shard),
        out_shape=(
            jax.ShapeDtypeStruct((2, n // 2, rows_down, width), F32),
            jax.ShapeDtypeStruct((2, n // 2, rows, wide * width), F32),
            jax.ShapeDtypeStruct((2, n // 2, rows, width), F32),
        )
        + (jax.ShapeDtypeStruct((shard, n * d), F32),) * 3,
        grid=(n // 2,),
        in_specs=[pl.BlockSpec((2, whole, width), lambda i: (i, 0, 0))],
        out_specs=[
            pl.BlockSpec((2, 1, rows_down, width), place),
            pl.BlockSpec((2, 1, rows, wide * width), place),
            pl.BlockSpec((2, 1, rows, width), place),
        ]
        + [pl.BlockSpec((shard, 2 * d), lambda i: (0, i))] * 3,
        compiler_params=pltpu.CompilerParams(vmem_limit_bytes=32 << 20),
        cost_estimate=pl.CostEstimate(flops=0, bytes_accessed=6 * every.size, transcendentals=0),
        name="in_order",
    )(every)
    return down.reshape(n * rows_down, width), up.reshape(n * rows, wide * width), out.reshape(n * rows, width), qkv


def body(ctx, fsdp, tokens, segments, w_query, w_key, w_value, w_out, b_query, b_value, b_out, gain_one, shift_one,
         w_up, b_up, w_down, b_down, gain_two, shift_two, cotangent):
    _, block, width = tokens.shape
    heads = HEADS
    d = width // heads
    scale = 1.0 / math.sqrt(d)
    parts = ctx // heads
    mine = block // parts
    length = ctx * block
    count = length // parts
    hidden = w_up.shape[1]
    shard = w_query.shape[0]
    me = lax.axis_index("ctx")
    row = lax.axis_index("fsdp")
    head, part = me // parts, me % parts
    core = me % 2
    cut = lambda a, at, size, axis: lax.dynamic_slice_in_dim(a, at, size, axis)

    bits = lambda n: [1 << i for i in range(n.bit_length() - 1)]
    sizes = {"fsdp": fsdp, "ctx": ctx}
    tie = lambda *arrays: lax.optimization_barrier(arrays)

    def gather_small(a):
        if fsdp == 2:
            other = flip(a, "fsdp", 1, 2)
            return jnp.concatenate([jnp.where(row == 0, a, other), jnp.where(row == 0, other, a)], axis=0)
        return lax.all_gather(a, "fsdp", axis=0, tiled=True)

    def near_half(w):
        if fsdp != 2:
            return lax.all_gather(w, "fsdp", axis=0, tiled=True)
        return flip(cut(w, core * (w.shape[0] // 2), w.shape[0] // 2, 0), "fsdp", 1, 2)

    def far_half(near):
        return flip(near, "ctx", 1, ctx) if fsdp == 2 else near

    def assemble(w, near, far):
        if fsdp != 2:
            return near
        rows, half = w.shape[0], w.shape[0] // 2
        whole = jnp.zeros((2 * rows, w.shape[1]), w.dtype)
        whole = lax.dynamic_update_slice_in_dim(whole, w, row * rows, 0)
        whole = lax.dynamic_update_slice_in_dim(whole, near, (1 - row) * rows + core * half, 0)
        return lax.dynamic_update_slice_in_dim(whole, far, (1 - row) * rows + (1 - core) * half, 0)

    def move(send, step):
        return flip(send, step[0], step[1], sizes[step[0]])

    core_step = ("ctx", 1)
    every_place = [("fsdp", b) for b in reversed(bits(fsdp))] + [("ctx", b) for b in bits(ctx)]
    own_bit = lambda step: (lax.axis_index(step[0]) // step[1]) % 2

    def columns_of(left, chosen):
        depth = max(every_place.index(step) for step in chosen) + 1
        size = left.shape[1] >> depth
        offsets = [0]
        for level, step in enumerate(every_place[:depth]):
            stride = left.shape[1] >> (level + 1)
            options = [chosen[step]] if step in chosen else [0, 1]
            offsets = [at + which * stride for at in offsets for which in options]
        return jnp.concatenate([cut(left, at, size, 1) for at in offsets], axis=1)

    def blocks(rows_data, place):
        return rows_data.reshape([2] * len(place) + [-1, rows_data.shape[1]])

    def first_share(left, right):
        return dot(columns_of(left, {core_step: 1 - own_bit(core_step)}), right, 0, 0).astype(BF)

    def second_share(left, right, got, step):
        place = [p for p in every_place if p != core_step]
        got = blocks(got, place)
        inner = [p for p in place if p != step]
        parts_of = []
        for which in (1 - own_bit(step), own_bit(step)):
            rows_data = dot(columns_of(left, {core_step: own_bit(core_step), step: which}), right, 0, 0)
            added = lax.dynamic_index_in_dim(got, which, place.index(step), keepdims=False)
            parts_of.append((blocks(rows_data, inner) + added.astype(F32)).astype(BF))
        rest = Halving(inner, sizes)
        rest.terms = [parts_of[1]]
        return parts_of[0], rest

    def sorted_rows(every):
        n = len(bits(ctx))
        shape = every.shape
        every = every.reshape((2,) * n + shape[1:]).transpose(list(reversed(range(n))) + [n, n + 1])
        return every.reshape(-1, shape[2])

    inputs = tokens[0]
    everyone = lax.all_gather(inputs, "ctx", axis=0, tiled=True)
    by_head = lambda w: w.reshape(shard, heads, 1, d)
    wqkv = jnp.concatenate([by_head(w) for w in (w_query, w_key, w_value)], axis=2).reshape(shard, 3 * width)
    small = jnp.stack([b_query, b_value, b_out, gain_one, shift_one, b_down, gain_two, shift_two])
    small = jnp.concatenate([small.reshape(-1), b_up])[None]
    w_head = gather_small(jnp.concatenate([cut(w, head * d, d, 1) for w in (w_query, w_key, w_value)], axis=1))
    small = gather_small(small)
    wo_near = near_half(w_out)
    wu_near = near_half(w_up)
    wo_near, w_head, small = tie(wo_near, w_head, small)
    wo = assemble(w_out, wo_near, far_half(wo_near))
    wu_near, w_down, wo = tie(wu_near, w_down, wo)
    wd_near = near_half(w_down)
    wu_far = far_half(wu_near)
    everyone, wu_near = tie(everyone, wu_near)

    eight = small[:, : 8 * shard].reshape(-1, 8, shard).transpose(1, 0, 2).reshape(8, width).astype(F32)
    bq_, bv_, bo, gain1, shift1, bd, gain2, shift2 = (eight[i] for i in range(8))
    bu = small[:, 8 * shard :].reshape(hidden).astype(F32)
    projected = dot(everyone, w_head, 1, 0)
    my_bias = jnp.concatenate([cut(bq_, head * d, d, 0), jnp.zeros((d,), F32), cut(bv_, head * d, d, 0)])
    projected = (projected + my_bias).astype(BF)
    own_part = lambda a: cut(a.reshape((ctx, block) + a.shape[1:]), part * mine, mine, 1).reshape(
        (count,) + a.shape[1:]
    )
    q = own_part(projected[:, :d])
    k, v = projected[:, d : 2 * d], projected[:, 2 * d :]
    seg = segments[0]
    starts_all = jnp.sum(seg[None, :] < seg[:, None], axis=1, dtype=jnp.int32)
    ends_all = jnp.sum(seg[None, :] <= seg[:, None], axis=1, dtype=jnp.int32)
    starts, ends = own_part(starts_all), own_part(ends_all)

    attended_t, outgoing, lse = attention_forward(q, k, v, starts, ends, scale, mine)
    incoming = lax.all_to_all(outgoing, "ctx", 0, 0, tiled=True)
    wu_far, outgoing, wu_near = tie(wu_far, outgoing, wu_near)
    wu = assemble(w_up, wu_near, wu_far)
    incoming, wu = tie(incoming, wu)
    attended = incoming.reshape(heads, parts, d, mine).transpose(1, 3, 0, 2).reshape(block, width)
    branch = dot(attended, wo, 1, 0) + bo
    first, first_pull = jax.vjp(layer_norm, inputs.astype(F32) + branch, gain1, shift1)
    first_low, wd_near = tie(first.astype(BF), wd_near)
    wd = assemble(w_down, wd_near, far_half(wd_near))
    hidden_pre = dot(first_low, wu, 1, 0) + bu
    active, active_pull = jax.vjp(gelu_exact, hidden_pre)
    (slope,) = active_pull(jnp.ones_like(active))
    active_low, slope = tie(active.astype(BF), slope)
    second = dot(active_low, wd, 1, 0) + bd
    output, out_pull = jax.vjp(layer_norm, first + second, gain2, shift2)

    fsdp_steps = [("fsdp", b) for b in reversed(bits(fsdp))]
    ctx_steps = [("ctx", b) for b in bits(ctx) if b > 1]
    down_order = fsdp_steps + ctx_steps
    up_order = ctx_steps[1:2] + fsdp_steps + ctx_steps[:1] + ctx_steps[2:]
    out_order = ctx_steps[:1] + fsdp_steps + ctx_steps[1:]
    d_second, grad_gain_two, grad_shift_two = out_pull(cotangent[0].astype(F32))
    d_second_low = d_second.astype(BF)
    down_sent = first_share(active_low, d_second_low)
    down_sent, d_second_low = tie(down_sent, d_second_low)
    down_got = move(down_sent, core_step)
    d_hidden = dot(d_second_low, wd, 1, 1) * slope
    d_hidden_low = d_hidden.astype(BF)
    up_sent = first_share(first_low, d_hidden_low)
    up_sent, d_hidden_low, down_got = tie(up_sent, d_hidden_low, down_got)
    up_got = move(up_sent, core_step)
    down_sent, down = second_share(active_low, d_second_low, down_got, down_order[0])
    down_sent, d_hidden_low = tie(down_sent, d_hidden_low)
    down_got = move(down_sent, down_order[0])
    d_first = d_second + dot(d_hidden_low, wu, 1, 1)
    d_branch, grad_gain_one, grad_shift_one = first_pull(d_first)
    d_branch_low = d_branch.astype(BF)
    d_attended_t = dot(wo, d_branch_low, 1, 1).astype(BF)
    outgoing = d_attended_t.reshape(heads, d, parts, mine).transpose(0, 2, 1, 3).reshape(ctx, d, mine)
    do_t = lax.all_to_all(outgoing, "ctx", 0, 0, tiled=True)
    outgoing, d_branch_low, up_got = tie(outgoing, d_branch_low, up_got)
    out_sent = first_share(attended, d_branch_low)
    out_sent, d_hidden_low = tie(out_sent, d_hidden_low)
    out_got = move(out_sent, core_step)
    up_sent, up = second_share(first_low, d_hidden_low, up_got, up_order[0])
    up_sent, out_got = tie(up_sent, out_got)
    out_sent, out = second_share(attended, d_branch_low, out_got, out_order[0])
    vectors = [
        jnp.sum(d_branch, axis=0), grad_gain_one, grad_shift_one, jnp.sum(d_second, axis=0), grad_gain_two,
        grad_shift_two,
    ]
    vectors = jnp.concatenate(
        [jnp.stack(vectors).reshape(6, fsdp, shard).transpose(1, 0, 2).reshape(fsdp, -1),
         jnp.sum(d_hidden, axis=0).reshape(fsdp, -1)], axis=1,
    )
    vectors = lax.all_gather(vectors, ("ctx", "fsdp"), axis=0, tiled=False)
    do_t, up_sent, out_sent, down.terms[0], up.terms[0], out.terms[0] = tie(
        do_t, up_sent, out_sent, down.terms[0], up.terms[0], out.terms[0]
    )
    up_got, out_got = move(up_sent, up_order[0]), move(out_sent, out_order[0])

    delta = jnp.sum(
        attended_t.reshape(d, ctx, mine) * do_t.transpose(1, 0, 2).astype(F32), axis=0
    ).reshape(1, count)
    bq, bk = min(512, count), 512
    ranges = block_ranges(starts_all, ends_all, bk, bq * parts)
    calls = 4
    per_call = length // bk // calls
    dqt = jnp.zeros((d, count), F32)
    dkt, dvt = [], []
    down_left, up_left, out_left = down_order[1:], up_order[1:], out_order[1:]

    def one_step(one, left, got):
        one.receive(got)
        step = left.pop(0)
        sent = one.send(step)
        return sent, move(sent, step)

    def both_step():
        step = down_left.pop(0)
        sent = jnp.concatenate([down.send(step), out.send(step)], axis=-2)
        return sent, move(sent, step)

    def both_receive(got):
        rows = down.terms[0].shape[-2]
        down.receive(got[..., :rows, :])
        out.receive(got[..., rows:, :])

    for call in range(calls):
        dk_new, dv_new, dqt = attention_backward(
            q, k, v, do_t, lse, delta, starts, ends, ranges, dqt, scale, bq, bk, call * per_call, per_call
        )
        dkt.append(dk_new)
        dvt.append(dv_new)
        if call == 0:
            dqt, out_got = tie(dqt, out_got)
            while len(out_left) >= len(ctx_steps):
                out_sent, out_got = one_step(out, out_left, out_got)
            dqt, out_sent = tie(dqt, out_sent)
        if call == 1:
            dqt, down_got = tie(dqt, down_got)
            while len(down_left) >= len(ctx_steps):
                down_sent, down_got = one_step(down, down_left, down_got)
            dqt, down_sent = tie(dqt, down_sent)
        if call == 2:
            dqt, up_got, vectors = tie(dqt, up_got, vectors)
            up_sent, up_got = one_step(up, up_left, up_got)
            dqt, up_sent = tie(dqt, up_sent)

    dqt, down_got, out_got = tie(dqt, down_got, out_got)
    down.receive(down_got)
    out.receive(out_got)
    down_sent, down_got = both_step()
    dqt, down_sent = tie(dqt, down_sent)
    dkt, dvt = jnp.concatenate(dkt, axis=1), jnp.concatenate(dvt, axis=1)
    dqt = (dqt * scale).astype(BF)
    if parts == 1:
        dqkv_t = jnp.concatenate([dqt, dkt, dvt], axis=0)
        outgoing = dqkv_t.reshape(3 * d, ctx, block).transpose(1, 0, 2)
        outgoing, dqkv_t = tie(outgoing, dqkv_t)
        grad_head = dot(dqkv_t, everyone, 1, 0)
        sums = jnp.sum(dqkv_t.astype(F32), axis=1)
    else:
        back = lambda a: lax.all_to_all(
            a.reshape(d, ctx, -1).transpose(1, 0, 2), "ctx", 0, 0, tiled=True
        ).reshape(heads, parts, d, -1)
        summed = lambda a: jnp.sum(back(a).astype(F32), axis=1).astype(BF)
        incoming = jnp.stack([back(dqt).transpose(0, 2, 1, 3).reshape(heads, d, block), summed(dkt), summed(dvt)], axis=1)
        grad_head = jnp.concatenate([dot(dqt, own_part(everyone), 1, 0), dot(dkt, everyone, 1, 0), dot(dvt, everyone, 1, 0)])
        sums = jnp.concatenate([jnp.sum(a.astype(F32), axis=1) for a in (dqt, dkt, dvt)])
    grad_head = grad_head.reshape(3 * d, fsdp, shard).transpose(1, 0, 2)
    extra = jnp.pad(sums[None, None], ((0, 0), (0, 15), (0, shard - 3 * d))) if shard >= 3 * d else jnp.pad(
        sums.reshape(1, -1, shard // 2), ((0, 0), (0, 16 - 6 * d // shard), (0, shard // 2))
    )
    grad_head = jnp.concatenate([grad_head, jnp.broadcast_to(extra, (fsdp, 16, shard))], axis=1)
    for step in fsdp_steps:
        pair = grad_head.reshape(2, -1, 3 * d + 16, shard)
        sent = lax.dynamic_index_in_dim(pair, 1 - own_bit(step), 0, keepdims=False).astype(BF)
        kept = lax.dynamic_index_in_dim(pair, own_bit(step), 0, keepdims=False)
        if step == fsdp_steps[0]:
            up_got, sent = tie(up_got, sent)
        grad_head = kept + move(sent, step).astype(F32)
    grad_head = grad_head[0].astype(BF)

    if len(up_left) > 1:
        up_sent, up_got = one_step(up, up_left, up_got)
        down_got, up_sent = tie(down_got, up_sent)
    both_receive(down_got)
    while down_left:
        down_sent, down_got = both_step()
        if down_left:
            both_receive(down_got)
    up_got, grad_head = tie(up_got, grad_head)
    while up_left:
        up_sent, up_got = one_step(up, up_left, up_got)
    if parts == 1:
        outgoing, up_sent = tie(outgoing, up_sent)
        incoming = lax.all_to_all(outgoing, "ctx", 0, 0, tiled=True)
    down_got, up_sent = tie(down_got, up_sent)
    both_receive(down_got)
    up.receive(up_got)
    vectors = jnp.sum(lax.dynamic_index_in_dim(vectors, row, 1, keepdims=False), axis=0)
    six = vectors[: 6 * shard].reshape(6, shard)
    grad_b_up = vectors[6 * shard :]

    up_block = up.total(up.terms)
    rows_up, rows_down = up_block.shape[0], down.terms[0].shape[0]
    wide = hidden // width
    per_row = width // shard
    rows_head = (3 * d + 16) // per_row
    at_head = rows_down + (wide + 1) * rows_up
    pieces = [down.total(down.terms)] + [up_block[:, i * width : (i + 1) * width] for i in range(wide)] + [out.total(out.terms)]
    split = grad_head.reshape(per_row, -1, shard)
    pieces.append(jnp.concatenate([split[i] for i in range(per_row)], axis=1))
    pieces = jnp.concatenate(pieces, axis=0)
    every = lax.all_gather(pieces, "ctx", axis=0, tiled=False)
    wqkv, pieces = tie(wqkv, pieces)
    wqkv_near = near_half(wqkv)
    wqkv_all = assemble(wqkv, wqkv_near, far_half(wqkv_near))
    token_grad = d_branch + dot(incoming.reshape(3 * width, block), wqkv_all, 0, 1)
    if parts == 1 and per_row == 2 and shard >= 3 * d:
        grad_w_down, grad_w_up, grad_w_out, grad_qkv = in_order(every, rows_down, rows_up, wide, d, shard)
        at = (3 * d) % rows_head
        sums = every[:, at_head + at, shard : shard + 3 * d].astype(F32)
    else:
        grad_w_down = sorted_rows(every[:, :rows_down]).astype(F32)
        take = lambda i: sorted_rows(every[:, rows_down + i * rows_up :][:, :rows_up]).astype(F32)
        grad_w_up = jnp.concatenate([take(i) for i in range(wide)], axis=1)
        grad_w_out = take(wide)
        every_head = every[:, at_head:]
        every_head = jnp.concatenate([every_head[:, :, i * shard : (i + 1) * shard] for i in range(per_row)], axis=1)
        every_head = every_head.astype(F32).reshape(heads, parts, 3 * d + 16, shard).sum(axis=1)
        grad_qkv = every_head[:, : 3 * d].reshape(heads, 3, d, shard).transpose(1, 3, 0, 2).reshape(3, shard, width)
        sums = every_head[:, 3 * d :]
        if shard >= 3 * d:
            sums = sums[:, 0, : 3 * d]
        else:
            sums = sums[:, : 6 * d // shard, : shard // 2]
    sums = sums.reshape(heads, 3, d).transpose(1, 0, 2).reshape(3, width)
    bias_q = cut(sums[0], row * shard, shard, 0)
    bias_v = cut(sums[2], row * shard, shard, 0)

    return (
        output[None].astype(BF),
        token_grad[None].astype(BF),
        grad_qkv[0],
        grad_qkv[1],
        grad_qkv[2],
        grad_w_out,
        bias_q,
        bias_v,
        six[0],
        six[1],
        six[2],
        grad_w_up,
        grad_b_up,
        grad_w_down,
        six[3],
        six[4],
        six[5],
    )


def solution(mesh):
    line, matrix, rows = P("fsdp"), P("fsdp", None), P("fsdp", "ctx", None)
    placed = (
        (rows, matrix) + (matrix,) * 4 + (line,) * 5 + (matrix, line, matrix) + (line,) * 3 + (rows,)
    )
    outs = (rows, rows) + (matrix,) * 4 + (line,) * 5 + (matrix, line, matrix) + (line,) * 3
    return jax.shard_map(
        functools.partial(body, mesh.shape["ctx"], mesh.shape["fsdp"]),
        mesh=mesh,
        in_specs=placed,
        out_specs=outs,
        check_vma=False,
    )
```

```python
import functools
import math

import jax
import jax.numpy as jnp
from jax import lax
from jax.experimental import pallas as pl
from jax.experimental.pallas import tpu as pltpu
from jax.sharding import PartitionSpec as P

HEADS = 16
LOG2E = 1.4426950408889634
NEG = -1e30
BF = jnp.bfloat16
F32 = jnp.float32


def layer_norm(hidden, gain, shift):
    mean = jnp.mean(hidden, axis=-1, keepdims=True)
    centred = hidden - mean
    variance = jnp.mean(centred * centred, axis=-1, keepdims=True)
    return centred * lax.rsqrt(variance + 1e-05) * gain + shift


def gelu_exact(value):
    return jax.nn.gelu(value, approximate=False)


def dot(left, right, on_left, on_right):
    return lax.dot_general(
        left, right, (((on_left,), (on_right,)), ((), ())), preferred_element_type=F32
    )


def flip(value, axis, bit, size):
    return lax.ppermute(value, axis, [(i, i ^ bit) for i in range(size)])


def forward_kernel(
    lo_ref, hi_ref, in_lo_ref, in_hi_ref, q_ref, k_ref, v_ref, start_ref, end_ref,
    out_ref, low_ref, lse_ref, total_ref, vt_ref, *, bk, scale
):
    i = pl.program_id(0)
    bq = q_ref.shape[0]

    @pl.when(i == 0)
    def _():
        @pl.loop(0, v_ref.shape[0] // bk)
        def _(j):
            at = pl.multiple_of(j * bk, bk)
            vt_ref[:, pl.ds(at, bk)] = v_ref[pl.ds(at, bk), :].T

    q = q_ref[...]
    start, end = start_ref[...], end_ref[...]
    total_ref[...] = jnp.zeros_like(total_ref)

    def step(j, carry, masked):
        peak, norm = carry
        at = pl.multiple_of(j * bk, bk)
        s = dot(k_ref[pl.ds(at, bk), :], q, 1, 1) * (scale * LOG2E)
        if masked:
            at_key = lax.broadcasted_iota(jnp.int32, (bk, bq), 0) + at
            s = jnp.where((at_key >= start) & (at_key < end), s, NEG)
        new_peak = jnp.maximum(peak, jnp.max(s, axis=0, keepdims=True))
        p = jnp.exp2(s - new_peak)
        shrink = jnp.exp2(peak - new_peak)
        norm = norm * shrink + jnp.sum(p, axis=0, keepdims=True)
        total_ref[...] = total_ref[...] * shrink + dot(vt_ref[:, pl.ds(at, bk)], p.astype(BF), 1, 0)
        return new_peak, norm

    lo, hi, in_lo, in_hi = lo_ref[i], hi_ref[i], in_lo_ref[i], in_hi_ref[i]
    carry = (jnp.full((1, bq), NEG, F32), jnp.zeros((1, bq), F32))
    carry = lax.fori_loop(in_lo, in_hi, lambda j, c: step(j, c, False), carry)
    carry = lax.fori_loop(lo, in_lo, lambda j, c: step(j, c, True), carry)
    peak, norm = lax.fori_loop(in_hi, hi, lambda j, c: step(j, c, True), carry)
    out = total_ref[...] / norm
    out_ref[...] = out
    n = low_ref.shape[2]
    for piece in range(bq // n):
        low_ref[piece] = out[:, piece * n : (piece + 1) * n].astype(low_ref.dtype)
    lse_ref[...] = peak + jnp.log2(norm)


def block_ranges(starts, ends, rows, others):
    first, last = starts.reshape(-1, rows), ends.reshape(-1, rows)
    lo = first[:, 0] // others
    hi = (last[:, -1] + others - 1) // others
    in_lo = jnp.clip((first[:, -1] + others - 1) // others, lo, hi)
    in_hi = jnp.clip(last[:, 0] // others, in_lo, hi)
    return lo, hi, in_lo, in_hi


def attention_forward(q, k, v, starts, ends, scale, n, bq=1024, bk=512):
    count, d = q.shape
    length = k.shape[0]
    bq = min(bq, count)
    ranges = block_ranges(starts, ends, bq, bk)
    row = lambda: pl.BlockSpec((1, bq), lambda i, *_: (0, i))
    whole = lambda shape: pl.BlockSpec(shape, lambda i, *_: (0, 0))
    return pl.pallas_call(
        functools.partial(forward_kernel, bk=bk, scale=scale),
        out_shape=(
            jax.ShapeDtypeStruct((d, count), F32),
            jax.ShapeDtypeStruct((count // n, d, n), BF),
            jax.ShapeDtypeStruct((1, count), F32),
        ),
        grid_spec=pltpu.PrefetchScalarGridSpec(
            num_scalar_prefetch=4,
            grid=(count // bq,),
            in_specs=[
                pl.BlockSpec((bq, d), lambda i, *_: (i, 0)),
                whole((length, d)),
                whole((length, d)),
                row(),
                row(),
            ],
            out_specs=[
                pl.BlockSpec((d, bq), lambda i, *_: (0, i)),
                pl.BlockSpec((bq // n, d, n), lambda i, *_: (i, 0, 0)),
                row(),
            ],
            scratch_shapes=[pltpu.VMEM((d, bq), F32), pltpu.VMEM((d, length), BF)],
        ),
        compiler_params=pltpu.CompilerParams(vmem_limit_bytes=40 << 20),
        cost_estimate=pl.CostEstimate(
            flops=16 * count * length * d, bytes_accessed=length * d * 16, transcendentals=count * length
        ),
        name="attention_forward",
    )(*ranges, q, k, v, starts[None], ends[None])


def backward_kernel(
    lo_ref, hi_ref, in_lo_ref, in_hi_ref, k_ref, v_ref, q_ref, do_ref, lse_ref, delta_ref, start_ref,
    end_ref, dqt_in_ref, dkt_ref, dvt_ref, dqt_ref, dk_sum, dv_sum, *, bq, scale, base
):
    j = pl.program_id(0) + base
    bk = k_ref.shape[0]
    pieces = bq // do_ref.shape[2]

    @pl.when(pl.program_id(0) == 0)
    def _():
        dqt_ref[...] = dqt_in_ref[...]

    k, v = k_ref[...], v_ref[...]
    kt = k.T
    dk_sum[...] = jnp.zeros_like(dk_sum)
    dv_sum[...] = jnp.zeros_like(dv_sum)

    def step(i, masked):
        at = pl.multiple_of(i * bq, bq)
        row = pl.ds(at, bq)
        q = q_ref[row, :]
        do_t = jnp.concatenate([do_ref[i * pieces + n] for n in range(pieces)], axis=1)
        s = dot(k, q, 1, 1) * (scale * LOG2E) - lse_ref[:, row]
        if masked:
            at_key = lax.broadcasted_iota(jnp.int32, (bk, bq), 0) + j * bk
            s = jnp.where((at_key >= start_ref[:, row]) & (at_key < end_ref[:, row]), s, NEG)
        p = jnp.exp2(s)
        dp = dot(v, do_t, 1, 0)
        dv_sum[...] += dot(p.astype(BF), do_t, 1, 1)
        ds = (p * (dp - delta_ref[:, row])).astype(BF)
        dk_sum[...] += dot(ds, q, 1, 0)
        dqt_ref[:, row] += dot(kt, ds, 1, 0)

    lo, hi, in_lo, in_hi = lo_ref[j], hi_ref[j], in_lo_ref[j], in_hi_ref[j]
    pl.loop(in_lo, in_hi)(lambda i: step(i, False))
    pl.loop(lo, in_lo)(lambda i: step(i, True))
    pl.loop(in_hi, hi)(lambda i: step(i, True))
    dkt_ref[...] = (dk_sum[...] * scale).T.astype(dkt_ref.dtype)
    dvt_ref[...] = dv_sum[...].T.astype(dvt_ref.dtype)


def attention_backward(q, k, v, do_t, lse, delta, starts, ends, ranges, dqt, scale, bq, bk, base, blocks):
    count, d = q.shape
    whole = lambda shape: pl.BlockSpec(shape, lambda j, *_: (0,) * len(shape))
    keys = lambda: pl.BlockSpec((bk, d), lambda j, *_: (j + base, 0))
    columns = lambda: pl.BlockSpec((d, bk), lambda j, *_: (0, j))
    return pl.pallas_call(
        functools.partial(backward_kernel, bq=bq, scale=scale, base=base),
        out_shape=(
            jax.ShapeDtypeStruct((d, blocks * bk), BF),
            jax.ShapeDtypeStruct((d, blocks * bk), BF),
            jax.ShapeDtypeStruct((d, count), F32),
        ),
        grid_spec=pltpu.PrefetchScalarGridSpec(
            num_scalar_prefetch=4,
            grid=(blocks,),
            in_specs=[
                keys(),
                keys(),
                whole((count, d)),
                whole(do_t.shape),
                whole((1, count)),
                whole((1, count)),
                whole((1, count)),
                whole((1, count)),
                whole((d, count)),
            ],
            out_specs=[columns(), columns(), whole((d, count))],
            scratch_shapes=[pltpu.VMEM((bk, d), F32), pltpu.VMEM((bk, d), F32)],
        ),
        compiler_params=pltpu.CompilerParams(vmem_limit_bytes=32 << 20),
        cost_estimate=pl.CostEstimate(
            flops=count * d, bytes_accessed=count * d, transcendentals=0
        ),
        name="attention_backward",
    )(*ranges, k, v, q, do_t, lse, delta, starts[None], ends[None], dqt)


class Halving:
    def __init__(self, place, sizes):
        self.place, self.sizes, self.terms = list(place), sizes, []

    def own(self, step):
        return (lax.axis_index(step[0]) // step[1]) % 2

    def share(self, step, which):
        at = self.place.index(step)
        return [lax.dynamic_index_in_dim(t, which, at, keepdims=False) for t in self.terms]

    def total(self, terms):
        return sum((t.astype(F32) for t in terms[1:]), terms[0].astype(F32)).astype(BF)

    def send(self, step):
        sent = self.total(self.share(step, 1 - self.own(step)))
        self.terms = self.share(step, self.own(step))
        self.place.remove(step)
        return sent

    def receive(self, got):
        self.terms.append(got)


def reversed_bits(i, count):
    n = count.bit_length() - 1
    return sum(((i // (1 << b)) % 2) * (1 << (n - 1 - b)) for b in range(n))


def order_kernel(every_ref, down_ref, up_ref, out_ref, query_ref, key_ref, value_ref, *, rows, wide, d, shard):
    rows_down, width = down_ref.shape[2:]
    starts = [rows_down + i * rows for i in range(wide + 2)]
    halves = []
    for half in range(2):
        down_ref[half, 0] = every_ref[half, :rows_down, :].astype(F32)
        for i in range(wide):
            slab = every_ref[half, starts[i] : starts[i + 1], :]
            up_ref[half, 0, :, i * width : (i + 1) * width] = slab.astype(F32)
        out_ref[half, 0] = every_ref[half, starts[wide] : starts[wide + 1], :].astype(F32)
        both = every_ref[half, starts[wide + 1] :, :].astype(F32)
        halves.append(jnp.concatenate([both[:, :shard], both[:, shard:]], axis=0))
    for t, ref in enumerate((query_ref, key_ref, value_ref)):
        pair = jnp.concatenate([h[t * d : (t + 1) * d] for h in halves], axis=0)
        ref[...] = pair.T


def in_order(every, rows_down, rows, wide, d, shard):
    n, whole, width = every.shape
    place = lambda i: (0, reversed_bits(i, n // 2), 0, 0)
    down, up, out, *qkv = pl.pallas_call(
        functools.partial(order_kernel, rows=rows, wide=wide, d=d, shard=shard),
        out_shape=(
            jax.ShapeDtypeStruct((2, n // 2, rows_down, width), F32),
            jax.ShapeDtypeStruct((2, n // 2, rows, wide * width), F32),
            jax.ShapeDtypeStruct((2, n // 2, rows, width), F32),
        )
        + (jax.ShapeDtypeStruct((shard, n * d), F32),) * 3,
        grid=(n // 2,),
        in_specs=[pl.BlockSpec((2, whole, width), lambda i: (i, 0, 0))],
        out_specs=[
            pl.BlockSpec((2, 1, rows_down, width), place),
            pl.BlockSpec((2, 1, rows, wide * width), place),
            pl.BlockSpec((2, 1, rows, width), place),
        ]
        + [pl.BlockSpec((shard, 2 * d), lambda i: (0, i))] * 3,
        compiler_params=pltpu.CompilerParams(vmem_limit_bytes=32 << 20),
        cost_estimate=pl.CostEstimate(flops=0, bytes_accessed=6 * every.size, transcendentals=0),
        name="in_order",
    )(every)
    return down.reshape(n * rows_down, width), up.reshape(n * rows, wide * width), out.reshape(n * rows, width), qkv


def body(ctx, fsdp, tokens, segments, w_query, w_key, w_value, w_out, b_query, b_value, b_out, gain_one, shift_one,
         w_up, b_up, w_down, b_down, gain_two, shift_two, cotangent):
    _, block, width = tokens.shape
    heads = HEADS
    d = width // heads
    scale = 1.0 / math.sqrt(d)
    parts = ctx // heads
    mine = block // parts
    length = ctx * block
    count = length // parts
    hidden = w_up.shape[1]
    shard = w_query.shape[0]
    me = lax.axis_index("ctx")
    row = lax.axis_index("fsdp")
    head, part = me // parts, me % parts
    core = me % 2
    cut = lambda a, at, size, axis: lax.dynamic_slice_in_dim(a, at, size, axis)

    bits = lambda n: [1 << i for i in range(n.bit_length() - 1)]
    sizes = {"fsdp": fsdp, "ctx": ctx}
    tie = lambda *arrays: lax.optimization_barrier(arrays)

    def gather_small(a):
        if fsdp == 2:
            other = flip(a, "fsdp", 1, 2)
            return jnp.concatenate([jnp.where(row == 0, a, other), jnp.where(row == 0, other, a)], axis=0)
        return lax.all_gather(a, "fsdp", axis=0, tiled=True)

    def near_half(w):
        if fsdp != 2:
            return lax.all_gather(w, "fsdp", axis=0, tiled=True)
        return flip(cut(w, core * (w.shape[0] // 2), w.shape[0] // 2, 0), "fsdp", 1, 2)

    def far_half(near):
        return flip(near, "ctx", 1, ctx) if fsdp == 2 else near

    def assemble(w, near, far):
        if fsdp != 2:
            return near
        rows, half = w.shape[0], w.shape[0] // 2
        whole = jnp.zeros((2 * rows, w.shape[1]), w.dtype)
        whole = lax.dynamic_update_slice_in_dim(whole, w, row * rows, 0)
        whole = lax.dynamic_update_slice_in_dim(whole, near, (1 - row) * rows + core * half, 0)
        return lax.dynamic_update_slice_in_dim(whole, far, (1 - row) * rows + (1 - core) * half, 0)

    def move(send, step):
        return flip(send, step[0], step[1], sizes[step[0]])

    core_step = ("ctx", 1)
    every_place = [("fsdp", b) for b in reversed(bits(fsdp))] + [("ctx", b) for b in bits(ctx)]
    own_bit = lambda step: (lax.axis_index(step[0]) // step[1]) % 2

    def columns_of(left, chosen):
        depth = max(every_place.index(step) for step in chosen) + 1
        size = left.shape[1] >> depth
        offsets = [0]
        for level, step in enumerate(every_place[:depth]):
            stride = left.shape[1] >> (level + 1)
            options = [chosen[step]] if step in chosen else [0, 1]
            offsets = [at + which * stride for at in offsets for which in options]
        return jnp.concatenate([cut(left, at, size, 1) for at in offsets], axis=1)

    def blocks(rows_data, place):
        return rows_data.reshape([2] * len(place) + [-1, rows_data.shape[1]])

    def first_share(left, right):
        return dot(columns_of(left, {core_step: 1 - own_bit(core_step)}), right, 0, 0).astype(BF)

    def second_share(left, right, got, step):
        place = [p for p in every_place if p != core_step]
        got = blocks(got, place)
        inner = [p for p in place if p != step]
        parts_of = []
        for which in (1 - own_bit(step), own_bit(step)):
            rows_data = dot(columns_of(left, {core_step: own_bit(core_step), step: which}), right, 0, 0)
            added = lax.dynamic_index_in_dim(got, which, place.index(step), keepdims=False)
            parts_of.append((blocks(rows_data, inner) + added.astype(F32)).astype(BF))
        rest = Halving(inner, sizes)
        rest.terms = [parts_of[1]]
        return parts_of[0], rest

    def sorted_rows(every):
        n = len(bits(ctx))
        shape = every.shape
        every = every.reshape((2,) * n + shape[1:]).transpose(list(reversed(range(n))) + [n, n + 1])
        return every.reshape(-1, shape[2])

    inputs = tokens[0]
    everyone = lax.all_gather(inputs, "ctx", axis=0, tiled=True)
    by_head = lambda w: w.reshape(shard, heads, 1, d)
    wqkv = jnp.concatenate([by_head(w) for w in (w_query, w_key, w_value)], axis=2).reshape(shard, 3 * width)
    small = jnp.stack([b_query, b_value, b_out, gain_one, shift_one, b_down, gain_two, shift_two])
    small = jnp.concatenate([small.reshape(-1), b_up])[None]
    w_head = gather_small(jnp.concatenate([cut(w, head * d, d, 1) for w in (w_query, w_key, w_value)], axis=1))
    small = gather_small(small)
    wo_near = near_half(w_out)
    wu_near = near_half(w_up)
    wo_near, w_head, small = tie(wo_near, w_head, small)
    wo = assemble(w_out, wo_near, far_half(wo_near))
    wu_near, w_down, wo = tie(wu_near, w_down, wo)
    wd_near = near_half(w_down)
    wu_far = far_half(wu_near)
    everyone, wu_near = tie(everyone, wu_near)

    eight = small[:, : 8 * shard].reshape(-1, 8, shard).transpose(1, 0, 2).reshape(8, width).astype(F32)
    bq_, bv_, bo, gain1, shift1, bd, gain2, shift2 = (eight[i] for i in range(8))
    bu = small[:, 8 * shard :].reshape(hidden).astype(F32)
    projected = dot(everyone, w_head, 1, 0)
    my_bias = jnp.concatenate([cut(bq_, head * d, d, 0), jnp.zeros((d,), F32), cut(bv_, head * d, d, 0)])
    projected = (projected + my_bias).astype(BF)
    own_part = lambda a: cut(a.reshape((ctx, block) + a.shape[1:]), part * mine, mine, 1).reshape(
        (count,) + a.shape[1:]
    )
    q = own_part(projected[:, :d])
    k, v = projected[:, d : 2 * d], projected[:, 2 * d :]
    seg = segments[0]
    starts_all = jnp.sum(seg[None, :] < seg[:, None], axis=1, dtype=jnp.int32)
    ends_all = jnp.sum(seg[None, :] <= seg[:, None], axis=1, dtype=jnp.int32)
    starts, ends = own_part(starts_all), own_part(ends_all)

    attended_t, outgoing, lse = attention_forward(q, k, v, starts, ends, scale, mine)
    incoming = lax.all_to_all(outgoing, "ctx", 0, 0, tiled=True)
    wu_far, outgoing, wu_near = tie(wu_far, outgoing, wu_near)
    wu = assemble(w_up, wu_near, wu_far)
    incoming, wu = tie(incoming, wu)
    attended = incoming.reshape(heads, parts, d, mine).transpose(1, 3, 0, 2).reshape(block, width)
    branch = dot(attended, wo, 1, 0) + bo
    first, first_pull = jax.vjp(layer_norm, inputs.astype(F32) + branch, gain1, shift1)
    first_low, wd_near = tie(first.astype(BF), wd_near)
    wd = assemble(w_down, wd_near, far_half(wd_near))
    hidden_pre = dot(first_low, wu, 1, 0) + bu
    active, active_pull = jax.vjp(gelu_exact, hidden_pre)
    (slope,) = active_pull(jnp.ones_like(active))
    active_low, slope = tie(active.astype(BF), slope)
    second = dot(active_low, wd, 1, 0) + bd
    output, out_pull = jax.vjp(layer_norm, first + second, gain2, shift2)

    fsdp_steps = [("fsdp", b) for b in reversed(bits(fsdp))]
    ctx_steps = [("ctx", b) for b in bits(ctx) if b > 1]
    down_order = fsdp_steps + ctx_steps
    up_order = ctx_steps[1:2] + fsdp_steps + ctx_steps[:1] + ctx_steps[2:]
    out_order = ctx_steps[:1] + fsdp_steps + ctx_steps[1:]
    d_second, grad_gain_two, grad_shift_two = out_pull(cotangent[0].astype(F32))
    d_second_low = d_second.astype(BF)
    down_sent = first_share(active_low, d_second_low)
    down_sent, d_second_low = tie(down_sent, d_second_low)
    down_got = move(down_sent, core_step)
    d_hidden = dot(d_second_low, wd, 1, 1) * slope
    d_hidden_low = d_hidden.astype(BF)
    up_sent = first_share(first_low, d_hidden_low)
    up_sent, d_hidden_low, down_got = tie(up_sent, d_hidden_low, down_got)
    up_got = move(up_sent, core_step)
    down_sent, down = second_share(active_low, d_second_low, down_got, down_order[0])
    down_sent, d_hidden_low = tie(down_sent, d_hidden_low)
    down_got = move(down_sent, down_order[0])
    d_first = d_second + dot(d_hidden_low, wu, 1, 1)
    d_branch, grad_gain_one, grad_shift_one = first_pull(d_first)
    d_branch_low = d_branch.astype(BF)
    d_attended_t = dot(wo, d_branch_low, 1, 1).astype(BF)
    outgoing = d_attended_t.reshape(heads, d, parts, mine).transpose(0, 2, 1, 3).reshape(ctx, d, mine)
    do_t = lax.all_to_all(outgoing, "ctx", 0, 0, tiled=True)
    outgoing, d_branch_low, up_got = tie(outgoing, d_branch_low, up_got)
    out_sent = first_share(attended, d_branch_low)
    out_sent, d_hidden_low = tie(out_sent, d_hidden_low)
    out_got = move(out_sent, core_step)
    up_sent, up = second_share(first_low, d_hidden_low, up_got, up_order[0])
    up_sent, out_got = tie(up_sent, out_got)
    out_sent, out = second_share(attended, d_branch_low, out_got, out_order[0])
    vectors = [
        jnp.sum(d_branch, axis=0), grad_gain_one, grad_shift_one, jnp.sum(d_second, axis=0), grad_gain_two,
        grad_shift_two,
    ]
    vectors = jnp.concatenate(
        [jnp.stack(vectors).reshape(6, fsdp, shard).transpose(1, 0, 2).reshape(fsdp, -1),
         jnp.sum(d_hidden, axis=0).reshape(fsdp, -1)], axis=1,
    )
    vectors = lax.all_gather(vectors, ("ctx", "fsdp"), axis=0, tiled=False)
    do_t, up_sent, out_sent, down.terms[0], up.terms[0], out.terms[0] = tie(
        do_t, up_sent, out_sent, down.terms[0], up.terms[0], out.terms[0]
    )
    up_got, out_got = move(up_sent, up_order[0]), move(out_sent, out_order[0])

    delta = jnp.sum(
        attended_t.reshape(d, ctx, mine) * do_t.transpose(1, 0, 2).astype(F32), axis=0
    ).reshape(1, count)
    bq, bk = min(512, count), 512
    ranges = block_ranges(starts_all, ends_all, bk, bq * parts)
    calls = 4
    per_call = length // bk // calls
    dqt = jnp.zeros((d, count), F32)
    dkt, dvt = [], []
    down_left, up_left, out_left = down_order[1:], up_order[1:], out_order[1:]

    def one_step(one, left, got):
        one.receive(got)
        step = left.pop(0)
        sent = one.send(step)
        return sent, move(sent, step)

    def both_step():
        step = down_left.pop(0)
        sent = jnp.concatenate([down.send(step), out.send(step)], axis=-2)
        return sent, move(sent, step)

    def both_receive(got):
        rows = down.terms[0].shape[-2]
        down.receive(got[..., :rows, :])
        out.receive(got[..., rows:, :])

    for call in range(calls):
        dk_new, dv_new, dqt = attention_backward(
            q, k, v, do_t, lse, delta, starts, ends, ranges, dqt, scale, bq, bk, call * per_call, per_call
        )
        dkt.append(dk_new)
        dvt.append(dv_new)
        if call == 0:
            dqt, out_got = tie(dqt, out_got)
            while len(out_left) >= len(ctx_steps):
                out_sent, out_got = one_step(out, out_left, out_got)
            dqt, out_sent = tie(dqt, out_sent)
        if call == 1:
            dqt, down_got = tie(dqt, down_got)
            while len(down_left) >= len(ctx_steps):
                down_sent, down_got = one_step(down, down_left, down_got)
            dqt, down_sent = tie(dqt, down_sent)
        if call == 2:
            dqt, up_got, vectors = tie(dqt, up_got, vectors)
            up_sent, up_got = one_step(up, up_left, up_got)
            dqt, up_sent = tie(dqt, up_sent)

    dqt, down_got, out_got = tie(dqt, down_got, out_got)
    down.receive(down_got)
    out.receive(out_got)
    down_sent, down_got = both_step()
    dqt, down_sent = tie(dqt, down_sent)
    dkt, dvt = jnp.concatenate(dkt, axis=1), jnp.concatenate(dvt, axis=1)
    dqt = (dqt * scale).astype(BF)
    if parts == 1:
        dqkv_t = jnp.concatenate([dqt, dkt, dvt], axis=0)
        outgoing = dqkv_t.reshape(3 * d, ctx, block).transpose(1, 0, 2)
        outgoing, dqkv_t = tie(outgoing, dqkv_t)
        grad_head = dot(dqkv_t, everyone, 1, 0)
        sums = jnp.sum(dqkv_t.astype(F32), axis=1)
    else:
        back = lambda a: lax.all_to_all(
            a.reshape(d, ctx, -1).transpose(1, 0, 2), "ctx", 0, 0, tiled=True
        ).reshape(heads, parts, d, -1)
        summed = lambda a: jnp.sum(back(a).astype(F32), axis=1).astype(BF)
        incoming = jnp.stack([back(dqt).transpose(0, 2, 1, 3).reshape(heads, d, block), summed(dkt), summed(dvt)], axis=1)
        grad_head = jnp.concatenate([dot(dqt, own_part(everyone), 1, 0), dot(dkt, everyone, 1, 0), dot(dvt, everyone, 1, 0)])
        sums = jnp.concatenate([jnp.sum(a.astype(F32), axis=1) for a in (dqt, dkt, dvt)])
    grad_head = grad_head.reshape(3 * d, fsdp, shard).transpose(1, 0, 2)
    extra = jnp.pad(sums[None, None], ((0, 0), (0, 15), (0, shard - 3 * d))) if shard >= 3 * d else jnp.pad(
        sums.reshape(1, -1, shard // 2), ((0, 0), (0, 16 - 6 * d // shard), (0, shard // 2))
    )
    grad_head = jnp.concatenate([grad_head, jnp.broadcast_to(extra, (fsdp, 16, shard))], axis=1)
    for step in fsdp_steps:
        pair = grad_head.reshape(2, -1, 3 * d + 16, shard)
        sent = lax.dynamic_index_in_dim(pair, 1 - own_bit(step), 0, keepdims=False).astype(BF)
        kept = lax.dynamic_index_in_dim(pair, own_bit(step), 0, keepdims=False)
        if step == fsdp_steps[0]:
            up_got, sent = tie(up_got, sent)
        grad_head = kept + move(sent, step).astype(F32)
    grad_head = grad_head[0].astype(BF)

    if len(up_left) > 1:
        up_sent, up_got = one_step(up, up_left, up_got)
        down_got, up_sent = tie(down_got, up_sent)
    both_receive(down_got)
    while down_left:
        down_sent, down_got = both_step()
        if down_left:
            both_receive(down_got)
    if parts == 1:
        outgoing, down_sent = tie(outgoing, down_sent)
        incoming = lax.all_to_all(outgoing, "ctx", 0, 0, tiled=True)
    up_got, grad_head = tie(up_got, grad_head)
    while up_left:
        up_sent, up_got = one_step(up, up_left, up_got)
    down_got, up_sent = tie(down_got, up_sent)
    both_receive(down_got)
    up_got, incoming = tie(up_got, incoming)
    up.receive(up_got)
    vectors = jnp.sum(lax.dynamic_index_in_dim(vectors, row, 1, keepdims=False), axis=0)
    six = vectors[: 6 * shard].reshape(6, shard)
    grad_b_up = vectors[6 * shard :]

    up_block = up.total(up.terms)
    rows_up, rows_down = up_block.shape[0], down.terms[0].shape[0]
    wide = hidden // width
    per_row = width // shard
    rows_head = (3 * d + 16) // per_row
    at_head = rows_down + (wide + 1) * rows_up
    pieces = [down.total(down.terms)] + [up_block[:, i * width : (i + 1) * width] for i in range(wide)] + [out.total(out.terms)]
    split = grad_head.reshape(per_row, -1, shard)
    pieces.append(jnp.concatenate([split[i] for i in range(per_row)], axis=1))
    pieces = jnp.concatenate(pieces, axis=0)
    every = lax.all_gather(pieces, "ctx", axis=0, tiled=False)
    wqkv, pieces = tie(wqkv, pieces)
    wqkv_near = near_half(wqkv)
    wqkv_all = assemble(wqkv, wqkv_near, far_half(wqkv_near))
    token_grad = d_branch + dot(incoming.reshape(3 * width, block), wqkv_all, 0, 1)
    if parts == 1 and per_row == 2 and shard >= 3 * d:
        grad_w_down, grad_w_up, grad_w_out, grad_qkv = in_order(every, rows_down, rows_up, wide, d, shard)
        at = (3 * d) % rows_head
        sums = every[:, at_head + at, shard : shard + 3 * d].astype(F32)
    else:
        grad_w_down = sorted_rows(every[:, :rows_down]).astype(F32)
        take = lambda i: sorted_rows(every[:, rows_down + i * rows_up :][:, :rows_up]).astype(F32)
        grad_w_up = jnp.concatenate([take(i) for i in range(wide)], axis=1)
        grad_w_out = take(wide)
        every_head = every[:, at_head:]
        every_head = jnp.concatenate([every_head[:, :, i * shard : (i + 1) * shard] for i in range(per_row)], axis=1)
        every_head = every_head.astype(F32).reshape(heads, parts, 3 * d + 16, shard).sum(axis=1)
        grad_qkv = every_head[:, : 3 * d].reshape(heads, 3, d, shard).transpose(1, 3, 0, 2).reshape(3, shard, width)
        sums = every_head[:, 3 * d :]
        if shard >= 3 * d:
            sums = sums[:, 0, : 3 * d]
        else:
            sums = sums[:, : 6 * d // shard, : shard // 2]
    sums = sums.reshape(heads, 3, d).transpose(1, 0, 2).reshape(3, width)
    bias_q = cut(sums[0], row * shard, shard, 0)
    bias_v = cut(sums[2], row * shard, shard, 0)

    return (
        output[None].astype(BF),
        token_grad[None].astype(BF),
        grad_qkv[0],
        grad_qkv[1],
        grad_qkv[2],
        grad_w_out,
        bias_q,
        bias_v,
        six[0],
        six[1],
        six[2],
        grad_w_up,
        grad_b_up,
        grad_w_down,
        six[3],
        six[4],
        six[5],
    )


def solution(mesh):
    line, matrix, rows = P("fsdp"), P("fsdp", None), P("fsdp", "ctx", None)
    placed = (
        (rows, matrix) + (matrix,) * 4 + (line,) * 5 + (matrix, line, matrix) + (line,) * 3 + (rows,)
    )
    outs = (rows, rows) + (matrix,) * 4 + (line,) * 5 + (matrix, line, matrix) + (line,) * 3
    return jax.shard_map(
        functools.partial(body, mesh.shape["ctx"], mesh.shape["fsdp"]),
        mesh=mesh,
        in_specs=placed,
        out_specs=outs,
        check_vma=False,
    )
```
